32 devices in a mesh: seq: 8 (over y, x, core), fsdp: 4 (over z).
Axes of the slice: x: 2, y: 2, z: 4, core: 2. Of those that a mesh axis runs over, the one named last changes fastest.
Arguments:
- tokens: bfloat16 [8192, 2048], P(('seq', 'fsdp')), may hold values from -6 to 6
- cotangent: bfloat16 [8192, 2048], P(('seq', 'fsdp')), may hold values from -6 to 6
- lengths: int32 [4], replicated, may hold values from 1 to 8192, as said below
- offsets: int32 [4], replicated, may hold values from 0 to 63, as said below
- deal: int32 [64], replicated, may hold values from 0 to 63, as said below
- norm_gain1: float32 [2048], P(('seq', 'fsdp')), may hold values from 0.1 to 1.9
- w_branch: float32 [2048, 2560], P(('seq', 'fsdp')), may hold values from -0.125 to 0.125
- w_input: float32 [2048, 2560], P(('seq', 'fsdp')), may hold values from -0.125 to 0.125
- conv_kernel: float32 [4, 2560], P(None, ('seq', 'fsdp')), may hold values from -3 to 3
- conv_bias: float32 [2560], P(('seq', 'fsdp')), may hold values from -3 to 3
- gate_rec: float32 [2560, 160], P(('seq', 'fsdp')), may hold values from -0.5 to 0.5
- bias_rec: float32 [2560], P(('seq', 'fsdp')), may hold values from -4 to 4
- gate_in: float32 [2560, 160], P(('seq', 'fsdp')), may hold values from -0.5 to 0.5
- bias_in: float32 [2560], P(('seq', 'fsdp')), may hold values from -4 to 4
- decay_param: float32 [2560], P(('seq', 'fsdp')), may hold values from 5 to 16
- w_out: float32 [2560, 2048], P(('seq', 'fsdp')), may hold values from -0.25 to 0.25
- norm_gain2: float32 [2048], P(('seq', 'fsdp')), may hold values from 0.1 to 1.9
- w_gate: float32 [2048, 6144], P(('seq', 'fsdp')), may hold values from -0.125 to 0.125
- w_up: float32 [2048, 6144], P(('seq', 'fsdp')), may hold values from -0.125 to 0.125
- w_down: float32 [6144, 2048], P(('seq', 'fsdp')), may hold values from -0.109375 to 0.109375
Outputs:
- mixed: bfloat16 [8192, 2048], P(('seq', 'fsdp'))
- tokens_grad: bfloat16 [8192, 2048], P(('seq', 'fsdp'))
- grad_norm_gain1: float32 [2048], P(('seq', 'fsdp'))
- grad_w_branch: float32 [2048, 2560], P(('seq', 'fsdp'))
- grad_w_input: float32 [2048, 2560], P(('seq', 'fsdp'))
- grad_conv_kernel: float32 [4, 2560], P(None, ('seq', 'fsdp'))
- grad_conv_bias: float32 [2560], P(('seq', 'fsdp'))
- grad_gate_rec: float32 [2560, 160], P(('seq', 'fsdp'))
- grad_bias_rec: float32 [2560], P(('seq', 'fsdp'))
- grad_gate_in: float32 [2560, 160], P(('seq', 'fsdp'))
- grad_bias_in: float32 [2560], P(('seq', 'fsdp'))
- grad_decay_param: float32 [2560], P(('seq', 'fsdp'))
- grad_w_out: float32 [2560, 2048], P(('seq', 'fsdp'))
- grad_norm_gain2: float32 [2048], P(('seq', 'fsdp'))
- grad_w_gate: float32 [2048, 6144], P(('seq', 'fsdp'))
- grad_w_up: float32 [2048, 6144], P(('seq', 'fsdp'))
- grad_w_down: float32 [6144, 2048], P(('seq', 'fsdp'))
The draws below stay inside these ranges and needn't reach their ends.
Inputs may be any that keep to these rules, and one draw needn't show every extreme that they name: deal is a permutation that keeps each block in its row: deal[b] // 8 == b // 8. Sequence s fills logical tokens offsets[s] * 128 to offsets[s] * 128 + lengths[s] - 1 and ends in its last block; offsets rise with s and no two sequences share a block. One sequence, which one varies, begins in the first 8 logical blocks and ends in the last 8. `offsets`: see lengths; a block may belong to no sequence.
All inputs are finite; a program needn't handle non-finite values.
Results may differ from the reference program's by a relative error of at most 0.008.
The reference program's roundings to bfloat16 on the way count: a program that leaves them out, or rounds other values in their place, can miss the bound.
Values may be sent and summed in bfloat16 or wider, within the bound.
No kernel may reach another device: no remote copies, remote signals or barrier semaphores. Data moves between devices by JAX's collectives and lax.ppermute only.
A program may use at most 448 MiB of HBM per device.

```python
import jax
import jax.numpy as jnp
from jax import lax

D = 2048
R = 2560
F = 6144
GATES = 16
BLOCK = 128
NSEQ = 4
GW = 160
ROWBLK = 8
NBLK = 64
TOKENS = 8192


def sequence_layout(base):
    base_key = jax.random.fold_in(base, 11)
    key_list = jax.random.split(base_key, 4)
    short_most = ROWBLK // 4
    short_blocks = jax.random.randint(key_list[0], (NSEQ,), 1, short_most + 1).astype(jnp.int32)
    long_index = jax.random.randint(key_list[1], (), 0, 3).astype(jnp.int32)
    gap_bits = jax.random.randint(key_list[2], (NSEQ,), 0, 2).astype(jnp.int32)
    seq_slot = jnp.arange(NSEQ, dtype=jnp.int32)
    gap_blocks = jnp.where(seq_slot < long_index, gap_bits, 0)
    short_blocks = jnp.where(seq_slot == long_index, 0, short_blocks)
    long_blocks = NBLK - jnp.sum(short_blocks) - jnp.sum(gap_blocks)
    seq_blocks = jnp.where(seq_slot == long_index, long_blocks, short_blocks)
    block_ends = jnp.cumsum(seq_blocks + gap_blocks)
    starts = block_ends - seq_blocks - gap_blocks
    last_fill = jax.random.randint(key_list[3], (NSEQ,), 1, BLOCK + 1).astype(jnp.int32)
    seq_lengths = (seq_blocks - 1) * BLOCK + last_fill
    return (seq_lengths.astype(jnp.int32), starts.astype(jnp.int32))


def draw_lengths(key, part):
    return sequence_layout(key)[0]


def draw_offsets(key, part):
    return sequence_layout(key)[1]


def draw_deal(key, part):
    row_count = NBLK // ROWBLK
    key_list = jax.random.split(jax.random.fold_in(key, 5), row_count)
    row_perms = jax.vmap(lambda row_key: jax.random.permutation(row_key, ROWBLK))(key_list)
    shifted = row_perms + (jnp.arange(row_count, dtype=jnp.int32) * ROWBLK)[:, None]
    return shifted.reshape(NBLK).astype(jnp.int32)


def steps_of(own_key, extent, cuts, low, top_value):
    def one(position, parts):
        steps = jax.random.uniform(jax.random.fold_in(jax.random.fold_in(own_key, 6), position), (parts,), jnp.float32, low / len(cuts), top_value / len(cuts))
        return jnp.repeat(jnp.exp(steps), extent[position] // parts).reshape((-1,) + (1,) * (len(extent) - position - 1))

    loudness = one(*cuts[0])
    for cut in cuts[1:]:
        loudness = loudness * one(*cut)
    return loudness


def noise(stream_key, dims, scale, limit, pieces=(), held_as=jnp.bfloat16):
    values = scale * jax.random.normal(stream_key, dims, jnp.float32)
    if pieces:
        values = values * steps_of(stream_key, dims, pieces, -0.22, 0.18)
    return jnp.clip(values, -limit, limit).astype(held_as)


def setup_inputs(seed: int = 0) -> dict:
    keys = jax.random.split(jax.random.key(seed), 21)
    tokens = noise(keys[0], (TOKENS, D), 1.0, 6.0, ((0, 32),))
    cotangent = noise(keys[1], (TOKENS, D), 1.0, 6.0, ((0, 32),))
    lengths = draw_lengths(jax.random.fold_in(keys[20], 71), 0)
    offsets = draw_offsets(jax.random.fold_in(keys[20], 71), 0)
    deal = draw_deal(jax.random.fold_in(keys[20], 71), 0)
    norm_gain1 = jnp.clip(1.0 + 0.18 * jax.random.normal(keys[5], (D,), jnp.float32), 0.1, 1.9)
    w_branch = noise(keys[6], (D, R), D ** -0.5, 0.125, ((0, 32),), jnp.float32)
    w_input = noise(keys[7], (D, R), D ** -0.5, 0.125, ((0, 32),), jnp.float32)
    conv_kernel = noise(keys[8], (4, R), 0.5, 3.0, ((1, 32),), jnp.float32)
    conv_bias = noise(keys[9], (R,), 0.5, 3.0, ((0, 32),), jnp.float32)
    gate_rec = noise(keys[10], (R, GW), GW ** -0.5, 0.5, ((0, 32),), jnp.float32)
    bias_rec = noise(keys[11], (R,), 1.0, 4.0, ((0, 32),), jnp.float32)
    gate_in = noise(keys[12], (R, GW), GW ** -0.5, 0.5, ((0, 32),), jnp.float32)
    bias_in = noise(keys[13], (R,), 1.0, 4.0, ((0, 32),), jnp.float32)
    decay_param = jnp.clip(5.0 + 11.0 * jax.random.uniform(keys[14], (R,), jnp.float32) ** steps_of(keys[14], (R,), ((0, 32),), -0.2, 0.2), 5.0, 16.0)
    w_out = noise(keys[15], (R, D), (R // 4) ** -0.5, 0.25, ((0, 32),), jnp.float32)
    norm_gain2 = jnp.clip(1.0 + 0.18 * jax.random.normal(keys[16], (D,), jnp.float32), 0.1, 1.9)
    w_gate = noise(keys[17], (D, F), D ** -0.5, 0.125, ((0, 32),), jnp.float32)
    w_up = noise(keys[18], (D, F), D ** -0.5, 0.125, ((0, 32),), jnp.float32)
    w_down = noise(keys[19], (F, D), (F // 2) ** -0.5, 0.109375, ((0, 32),), jnp.float32)
    return {"tokens": tokens, "cotangent": cotangent, "lengths": lengths, "offsets": offsets, "deal": deal, "norm_gain1": norm_gain1, "w_branch": w_branch, "w_input": w_input, "conv_kernel": conv_kernel, "conv_bias": conv_bias, "gate_rec": gate_rec, "bias_rec": bias_rec, "gate_in": gate_in, "bias_in": bias_in, "decay_param": decay_param, "w_out": w_out, "norm_gain2": norm_gain2, "w_gate": w_gate, "w_up": w_up, "w_down": w_down}


NORM_EPSILON = 1e-06
GATE_SCALE = 8.0
PRECISE = lax.Precision.HIGHEST

@jax.custom_vjp
def low(v):
    return lax.optimization_barrier(v.astype(jnp.bfloat16)).astype(jnp.float32)

@jax.custom_vjp
def low_back(v):
    return v

def low_keep(v):
    return (low(v), None)

def low_pass(kept, grad):
    return (grad,)

def back_keep(v):
    return (v, None)

def back_low(kept, grad):
    return (low(grad),)
low.defvjp(low_keep, low_pass)
low_back.defvjp(back_keep, back_low)

def rms_norm(values, gain_vec):
    inv_scale = lax.rsqrt(lax.optimization_barrier(jnp.mean(values * values, axis=-1, keepdims=True)) + NORM_EPSILON)
    return values * inv_scale * gain_vec

def lru_terms(pre_rec, pre_in, xc_value, decay_value, reset_mask):
    rate_gate = jax.nn.sigmoid(pre_rec)
    entry_gate = jax.nn.sigmoid(pre_in)
    log_keep = -GATE_SCALE * rate_gate * jax.nn.softplus(-decay_value)
    keep_rate = jnp.exp(log_keep) * reset_mask
    drive_in = jnp.sqrt(-jnp.expm1(2.0 * log_keep)) * entry_gate * xc_value
    return (keep_rate, drive_in)

def token_places(logical, lengths, offsets):
    within = jnp.arange(BLOCK, dtype=jnp.int32)
    token_place = (logical[:, None] * BLOCK + within[None, :]).reshape(-1)
    starts = offsets * BLOCK
    inside = (token_place[:, None] >= starts[None, :]) & (token_place[:, None] < (starts + lengths)[None, :])
    live_rows = jnp.any(inside, axis=1).astype(jnp.float32)
    seq_depth = lax.optimization_barrier(jnp.sum(jnp.where(inside, token_place[:, None] - starts[None, :], 0), axis=1)).astype(jnp.int32)
    return (live_rows, seq_depth)

def matmul(left, right):
    return jnp.dot(left, right, precision=PRECISE, preferred_element_type=jnp.float32)

def run_block(state_in, block_pair):

    def advance(state_now, pair_now):
        state_now = pair_now[0] * state_now + pair_now[1]
        return (state_now, state_now)
    return lax.scan(advance, state_in, block_pair)

def layer(x_store, gain1, branch_w, input_w, kernel_w, kernel_b, rec_w, rec_b, in_w, in_b, decay_w, out_w, gain2, gate_w, up_w, down_w, live_rows, seq_depth, block_order, deal):
    gain1 = low(gain1)
    branch_w = low(branch_w)
    input_w = low(input_w)
    kernel_w = low(kernel_w)
    kernel_b = low(kernel_b)
    rec_w = low(rec_w)
    rec_b = low(rec_b)
    in_w = low(in_w)
    in_b = low(in_b)
    decay_w = low(decay_w)
    out_w = low(out_w)
    gain2 = low(gain2)
    gate_w = low(gate_w)
    up_w = low(up_w)
    down_w = low(down_w)
    resid_in = x_store.reshape(NBLK, BLOCK, D)[block_order].reshape(TOKENS, D)
    normed_one = low(rms_norm(resid_in, gain1))
    branch_pre = low_back(matmul(normed_one, branch_w))
    branch_act = jax.nn.gelu(branch_pre)
    u_value = low_back(matmul(normed_one, input_w))
    conv_pre = kernel_b + kernel_w[0] * u_value
    for tap_index in range(1, 4):
        shifted = jnp.concatenate([jnp.zeros((tap_index, R), jnp.float32), u_value[:TOKENS - tap_index]], axis=0)
        conv_pre = conv_pre + kernel_w[tap_index] * shifted * (seq_depth >= tap_index).astype(jnp.float32)[:, None]
    conv_out = low(conv_pre)
    conv_heads = conv_out.reshape(TOKENS, GATES, GW)
    pre_rec = low_back(jnp.einsum('thb,hbc->thc', conv_heads, rec_w.reshape(GATES, GW, GW), precision=PRECISE).reshape(TOKENS, R) + rec_b)
    pre_in = low_back(jnp.einsum('thb,hbc->thc', conv_heads, in_w.reshape(GATES, GW, GW), precision=PRECISE).reshape(TOKENS, R) + in_b)
    reset_mask = (seq_depth > 0).astype(jnp.float32)[:, None]
    keep_rate, drive_in = lru_terms(pre_rec, pre_in, conv_out, decay_w, reset_mask)
    final_state, states = lax.scan(jax.checkpoint(run_block), jnp.zeros((R,), jnp.float32), (keep_rate.reshape(NBLK, BLOCK, R), drive_in.reshape(NBLK, BLOCK, R)))
    hidden_state = states.reshape(TOKENS, R)
    gated_state = low(hidden_state * branch_act)
    resid_mid = resid_in + low_back(matmul(gated_state, out_w))
    normed_two = low(rms_norm(resid_mid, gain2))
    gate_pre = low_back(matmul(normed_two, gate_w))
    up_pre = low_back(matmul(normed_two, up_w))
    hidden = low(jax.nn.gelu(gate_pre) * up_pre)
    down_out = low_back(matmul(hidden, down_w))
    result_log = live_rows[:, None] * (resid_mid + down_out)
    return result_log.reshape(NBLK, BLOCK, D)[deal].reshape(TOKENS, D)

def reference(tokens, cotangent, lengths, offsets, deal, norm_gain1, w_branch, w_input, conv_kernel, conv_bias, gate_rec, bias_rec, gate_in, bias_in, decay_param, w_out, norm_gain2, w_gate, w_up, w_down):
    logical = jnp.arange(NBLK, dtype=jnp.int32)
    live_rows, seq_depth = token_places(logical, lengths, offsets)
    block_order = jnp.argsort(deal).astype(jnp.int32)

    def forward(x_store, gain1, branch_w, input_w, kernel_w, kernel_b, rec_w, rec_b, in_w, in_b, decay_w, out_w, gain2, gate_w, up_w, down_w):
        return layer(x_store, gain1, branch_w, input_w, kernel_w, kernel_b, rec_w, rec_b, in_w, in_b, decay_w, out_w, gain2, gate_w, up_w, down_w, live_rows, seq_depth, block_order, deal)
    result_out, pull_back = jax.vjp(forward, tokens.astype(jnp.float32), norm_gain1, w_branch, w_input, conv_kernel, conv_bias, gate_rec, bias_rec, gate_in, bias_in, decay_param, w_out, norm_gain2, w_gate, w_up, w_down)
    all_grads = pull_back(cotangent.astype(jnp.float32))
    return (result_out.astype(jnp.bfloat16), all_grads[0].astype(jnp.bfloat16), all_grads[1], all_grads[2], all_grads[3], all_grads[4], all_grads[5], all_grads[6], all_grads[7], all_grads[8], all_grads[9], all_grads[10], all_grads[11], all_grads[12], all_grads[13], all_grads[14], all_grads[15])
```

```python
import jax
import jax.numpy as jnp
from jax import lax
from jax.experimental import pallas as pl
from jax.experimental.pallas import tpu as pltpu
from jax.sharding import PartitionSpec as P

BLOCK = 128
LANES = 128
TAPS = 4
UNROLL = 8
NORM_EPSILON = 1e-06
GATE_SCALE = 8.0
VMEM_LIMIT = 48 * 1024 * 1024
GELU_C = 0.7978845608028654
GELU_A = 0.044715


def as_low(values):
    return values.astype(jnp.bfloat16)


def as_wide(values):
    return values.astype(jnp.float32)


def mm(left, right, out=jnp.float32):
    return jnp.dot(left, right, preferred_element_type=jnp.float32).astype(out)


def mm_tn(left, right, out=jnp.float32):
    return lax.dot_general(
        left, right, (((0,), (0,)), ((), ())), preferred_element_type=jnp.float32
    ).astype(out)


def mm_nt(left, right, out=jnp.float32):
    return lax.dot_general(
        left, right, (((1,), (1,)), ((), ())), preferred_element_type=jnp.float32
    ).astype(out)


def swap(values, axis, flip):
    count = lax.axis_size(axis)
    return lax.ppermute(values, axis, [(i, i ^ flip) for i in range(count)])


def gather_plane(own):
    count = lax.axis_size("seq")
    if count == 8:
        half = own.shape[0] // 2
        near, side = swap(own, "seq", 2), swap(own, "seq", 4)
        far = (swap(side[:half], "seq", 2), swap(near[half:], "seq", 4))
        even = [(own,), (near,), (side,), far]
    else:
        even = [(own,)] + [(swap(own, "seq", k),) for k in range(2, count, 2)]
    odd = [tuple(swap(part, "seq", 1) for part in slot) for slot in even]
    return even + odd


def scatter_plane(product, hold=lambda value: value):
    count = lax.axis_size("seq")
    other = swap(hold(as_low(product(True))), "seq", 1)
    pair = product(False) + as_wide(other)
    rows = pair.shape[0] // (count // 2)
    if count != 8:
        total = pair[:rows]
        for index, k in enumerate(range(2, count, 2), start=1):
            total = total + as_wide(swap(as_low(pair[index * rows : (index + 1) * rows]), "seq", k))
        return total
    half = rows // 2

    def part(slot, lower):
        start = slot * rows + (half if lower else 0)
        return pair[start : start + half]

    far_top = swap(as_low(part(3, False)), "seq", 2)
    far_low = swap(as_low(part(3, True)), "seq", 4)
    near_top = swap(as_low(part(1, False)), "seq", 2)
    side_low = swap(as_low(part(2, True)), "seq", 4)
    near_low = swap(as_low(part(1, True) + as_wide(far_low)), "seq", 2)
    side_top = swap(as_low(part(2, False) + as_wide(far_top)), "seq", 4)
    top = part(0, False) + as_wide(near_top) + as_wide(side_top)
    low = part(0, True) + as_wide(near_low) + as_wide(side_low)
    return jnp.concatenate([top, low], axis=0)


def spread_z(value):
    count = lax.axis_size("fsdp")
    return jnp.stack([value] + [swap(value, "fsdp", j) for j in range(1, count)], axis=0)


def gelu_parts(values):
    inner = GELU_C * (values + GELU_A * values * values * values)
    bend = jnp.tanh(inner)
    return (0.5 * values * (1.0 + bend), bend)


def gelu_slope(values, bend):
    return 0.5 * (1.0 + bend) + 0.5 * values * (1.0 - bend * bend) * GELU_C * (
        1.0 + 3.0 * GELU_A * values * values
    )


def expm1_small(values):
    series = values * (1.0 / 120.0) + 1.0 / 24.0
    for scale in (1.0 / 6.0, 0.5, 1.0):
        series = series * values + scale
    return series * values


def block_rows(index):
    return pl.ds(pl.multiple_of(index * BLOCK, BLOCK), BLOCK)


def lane_tiles(width):
    return [(low, min(LANES, width - low)) for low in range(0, width, LANES)]


def stack_step(refs, slots):
    step = pl.program_id(0)
    steps = pl.num_programs(0)
    rows, at = [], 0
    for parts in slots:
        if parts == 1:
            rows.append(refs[at][...])
        else:
            rows.append(jnp.where(step < steps // 2, refs[at][...], refs[at + 1][...]))
        at += parts
    return jnp.concatenate(rows, axis=0)


def slot_specs(pieces, steps):
    specs = []
    for slot in pieces:
        chunk = sum(part.shape[0] for part in slot) // steps
        model = slot[0].shape[1]
        if len(slot) == 1:
            specs.append(pl.BlockSpec((chunk, model), lambda i: (i, 0)))
        else:
            last = steps // 2 - 1
            specs.append(pl.BlockSpec((chunk, model), lambda i, last=last: (jnp.minimum(i, last), 0)))
            specs.append(pl.BlockSpec((chunk, model), lambda i, last=last: (jnp.maximum(i - last - 1, 0), 0)))
    return specs


def stack(pieces, name, gain=None, weights=(), steps=8):
    slots = tuple(len(slot) for slot in pieces)
    count = len(pieces)
    flat = [part for slot in pieces for part in slot]
    rows = sum(part.shape[0] for part in pieces[0])
    model = flat[0].shape[1]
    chunk = rows // steps
    extra = ([gain] if gain is not None else []) + list(weights)

    def kernel(*refs):
        pieces_in, refs = refs[: len(flat)], refs[len(flat) :]
        values = stack_step(pieces_in, slots)
        if gain is not None:
            gain_ref, refs = refs[0], refs[1:]
            wide = values.astype(jnp.float32)
            scale = lax.rsqrt(jnp.mean(wide * wide, axis=-1, keepdims=True) + NORM_EPSILON)
            values = (wide * scale * gain_ref[...]).astype(jnp.bfloat16)
        weight_refs, refs = refs[: len(weights)], refs[len(weights) :]
        refs[0][...] = values.reshape(count, chunk, model)
        for weight_ref, out_ref in zip(weight_refs, refs[1:]):
            out = jnp.dot(values, weight_ref[...], preferred_element_type=jnp.float32)
            out_ref[...] = out.reshape(count, chunk, out.shape[1])

    widths = [weight.shape[1] for weight in weights]
    outs = [shaped((count, rows, model), jnp.bfloat16)] + [shaped((count, rows, w)) for w in widths]
    done = pl.pallas_call(
        kernel,
        grid=(steps,),
        in_specs=slot_specs(pieces, steps) + [pl.BlockSpec(e.shape, lambda i: (0, 0)) for e in extra],
        out_specs=[pl.BlockSpec((count, chunk, w), lambda i: (0, i, 0)) for w in [model] + widths],
        out_shape=outs,
        compiler_params=pltpu.CompilerParams(vmem_limit_bytes=VMEM_LIMIT),
        name=name,
    )(*flat, *extra)
    return [out.reshape(count * rows, out.shape[2]) for out in done]


def dead_mask(rows, live_count):
    return (rows < live_count).astype(jnp.float32)


def lru_forward_kernel(
    live_ref,
    first_ref,
    pred_ref,
    u_ref,
    tail_ref,
    vec_ref,
    rec_ref,
    in_ref,
    xc_ref,
    keep_ref,
    drive_ref,
    rate_ref,
    entry_ref,
    sum_ref,
    ext_ref,
):
    blocks = u_ref.shape[0] // BLOCK
    tiles = lane_tiles(u_ref.shape[1])
    rows = lax.broadcasted_iota(jnp.int32, (BLOCK, LANES), 0)

    def block(index, carry):
        at = block_rows(index)
        first = first_ref[index]
        pred = pred_ref[index]
        live = dead_mask(rows, live_ref[index])
        before = jnp.maximum(pred, 0)
        joined = jnp.where((pred >= 0) & (first == 0), 1.0, 0.0)
        for low, size in tiles:
            lanes = slice(low, low + size)
            u_value = u_ref[at, lanes]
            ext_ref[0:8, :size] = tail_ref[before, :, lanes] * joined
            ext_ref[8 : 8 + BLOCK, :size] = u_value
            later = vec_ref[1:2, lanes] * ext_ref[7 : 7 + BLOCK, :size]
            for tap in range(2, TAPS):
                later = later + vec_ref[tap : tap + 1, lanes] * ext_ref[8 - tap : 8 - tap + BLOCK, :size]
            conv = vec_ref[4:5, lanes] + vec_ref[0:1, lanes] * u_value + later * live[:, :size]
            xc_ref[at, lanes] = conv.astype(jnp.bfloat16)
        low_rows = xc_ref[at, :]
        pre_rec = jnp.dot(low_rows, rec_ref[...], preferred_element_type=jnp.float32)
        pre_in = jnp.dot(low_rows, in_ref[...], preferred_element_type=jnp.float32)
        for tile, (low, size) in enumerate(tiles):
            lanes = slice(low, low + size)
            rate = jax.nn.sigmoid(pre_rec[:, lanes] + vec_ref[5:6, lanes])
            entry = jax.nn.sigmoid(pre_in[:, lanes] + vec_ref[6:7, lanes])
            minus = expm1_small(rate * vec_ref[7:8, lanes])
            rate_ref[tile, at, :size] = rate
            entry_ref[tile, at, :size] = entry
            keep_ref[tile, at, :size] = (1.0 + minus) * live[:, :size]
            drive_ref[tile, at, :size] = (
                jnp.sqrt(-minus * (2.0 + minus)) * entry * low_rows[:, lanes].astype(jnp.float32)
            )

        @pl.when(first > 0)
        def _():
            top = pl.ds(pl.multiple_of(index * BLOCK, BLOCK), 8)
            after = (rows[:8] > 0).astype(jnp.float32)
            for tile in range(len(tiles)):
                keep_ref[tile, top, :] = keep_ref[tile, top, :] * after

        return carry

    lax.fori_loop(0, blocks, block, 0)

    def step(place, carry):
        at = pl.ds(place, blocks, stride=BLOCK)
        after = []
        for tile, (total, state) in enumerate(carry):
            keep = keep_ref[tile, at, :]
            after.append((total * keep, keep * state + drive_ref[tile, at, :]))
        return tuple(after)

    ones = jnp.ones((blocks, LANES), jnp.float32)
    start = tuple((ones, jnp.zeros_like(ones)) for _ in tiles)
    ends = lax.fori_loop(0, BLOCK, step, start, unroll=UNROLL)
    for tile, (total, state) in enumerate(ends):
        sum_ref[0, tile] = total
        sum_ref[1, tile] = state


def lru_state_kernel(pos_ref, all_ref, keep_ref, drive_ref, ypre_ref, h_ref, hy_ref, enter_ref, line_ref):
    tiles = lane_tiles(ypre_ref.shape[1])
    turns, _, _, blocks, _ = all_ref.shape

    def chain(place, states):
        slot = pos_ref[place]
        turn, index = slot // blocks, slot % blocks
        after = []
        for tile, state in enumerate(states):
            line_ref[tile, pl.ds(slot, 1), :] = state
            keep = all_ref[turn, 0, tile, pl.ds(index, 1), :]
            after.append(keep * state + all_ref[turn, 1, tile, pl.ds(index, 1), :])
        return tuple(after)

    zero = jnp.zeros((1, LANES), jnp.float32)
    lax.fori_loop(0, turns * blocks, chain, tuple(zero for _ in tiles))
    for tile in range(len(tiles)):
        enter_ref[tile] = line_ref[tile, 0:blocks, :]

    def step(place, states):
        at = pl.ds(place, blocks, stride=BLOCK)
        after = []
        for tile, state in enumerate(states):
            state = keep_ref[tile, at, :] * state + drive_ref[tile, at, :]
            h_ref[tile, at, :] = state
            after.append(state)
        return tuple(after)

    start = tuple(line_ref[tile, 0:blocks, :] for tile in range(len(tiles)))
    lax.fori_loop(0, BLOCK, step, start, unroll=UNROLL)

    def block(index, carry):
        at = block_rows(index)
        for tile, (low, size) in enumerate(tiles):
            lanes = slice(low, low + size)
            act = gelu_parts(ypre_ref[at, lanes])[0]
            hy_ref[at, lanes] = (h_ref[tile, at, :size] * act).astype(jnp.bfloat16)
        return carry

    lax.fori_loop(0, blocks, block, 0)


def lru_back(pieces, out_w, state, branch_pre, keep, steps=8):
    slots = tuple(len(slot) for slot in pieces)
    count = len(pieces)
    flat = [part for slot in pieces for part in slot]
    rows = sum(part.shape[0] for part in pieces[0])
    model = flat[0].shape[1]
    width = out_w.shape[0]
    tiles = lane_tiles(width)
    chunk = rows // steps
    blocks = count * rows // BLOCK

    def kernel(*refs):
        values = stack_step(refs[: len(flat)], slots)
        w_ref, h_ref, ypre_ref, keep_ref, out_ref, dy_ref, dh_ref, send_ref = refs[len(flat) :]
        here = pl.program_id(0)
        out_ref[...] = values.reshape(count, chunk, model)
        grads = lax.dot_general(
            values, w_ref[...], (((1,), (1,)), ((), ())), preferred_element_type=jnp.float32
        )
        for slot in range(count):
            span = pl.ds(pl.multiple_of(slot * rows + here * chunk, chunk), chunk)
            for tile, (low, size) in enumerate(tiles):
                lanes = slice(low, low + size)
                value = ypre_ref[slot, :, lanes]
                act, bend = gelu_parts(value)
                grad = grads[slot * chunk : (slot + 1) * chunk, lanes]
                slope = gelu_slope(value, bend)
                dy_ref[slot, :, lanes] = (grad * h_ref[tile, slot, :, :size] * slope).astype(jnp.bfloat16)
                dh_ref[tile, span, :size] = grad * act

        @pl.when(here == steps - 1)
        def _():
            def step(turn, carry):
                at = pl.ds(BLOCK - 1 - turn, blocks, stride=BLOCK)
                return tuple(
                    keep_ref[tile, at, :] * (dh_ref[tile, at, :] + value)
                    for tile, value in enumerate(carry)
                )

            zero = jnp.zeros((blocks, LANES), jnp.float32)
            ends = lax.fori_loop(0, BLOCK, step, tuple(zero for _ in tiles), unroll=UNROLL)
            for tile, value in enumerate(ends):
                send_ref[tile] = value

    depth = len(tiles)
    total = count * rows
    out, dy, dh, send = pl.pallas_call(
        kernel,
        grid=(steps,),
        in_specs=slot_specs(pieces, steps)
        + [
            pl.BlockSpec((width, model), lambda i: (0, 0)),
            pl.BlockSpec((depth, count, chunk, LANES), lambda i: (0, 0, i, 0)),
            pl.BlockSpec((count, chunk, width), lambda i: (0, i, 0)),
            pl.BlockSpec((depth, total, LANES), lambda i: (0, 0, 0)),
        ],
        out_specs=[
            pl.BlockSpec((count, chunk, model), lambda i: (0, i, 0)),
            pl.BlockSpec((count, chunk, width), lambda i: (0, i, 0)),
            pl.BlockSpec((depth, total, LANES), lambda i: (0, 0, 0)),
            pl.BlockSpec((depth, blocks, LANES), lambda i: (0, 0, 0)),
        ],
        out_shape=[
            shaped((count, rows, model), jnp.bfloat16),
            shaped((count, rows, width), jnp.bfloat16),
            shaped((depth, total, LANES)),
            shaped((depth, blocks, LANES)),
        ],
        compiler_params=pltpu.CompilerParams(vmem_limit_bytes=VMEM_LIMIT),
        name="lru_back",
    )(
        *flat,
        out_w,
        state.reshape(depth, count, rows, LANES),
        branch_pre.reshape(count, rows, width),
        keep,
    )
    return out.reshape(total, model), dy.reshape(total, width), dh, send


def fold_rows(values):
    return values.reshape(BLOCK // 8, 8, values.shape[1]).sum(axis=0)


def lru_grad_kernel(
    live_ref,
    first_ref,
    pred_ref,
    pos_ref,
    all_ref,
    back_ref,
    dh_ref,
    keep_ref,
    drive_ref,
    rate_ref,
    entry_ref,
    h_ref,
    enter_ref,
    xc_ref,
    u_ref,
    tail_ref,
    vec_ref,
    rec_ref,
    in_ref,
    drec_ref,
    din_ref,
    du_ref,
    last_ref,
    head_ref,
    total_ref,
    line_ref,
    g_ref,
    ext_ref,
    acc_ref,
    direct_ref,
):
    blocks = u_ref.shape[0] // BLOCK
    width = u_ref.shape[1]
    tiles = lane_tiles(width)
    every = back_ref.shape[0] * blocks
    rows = lax.broadcasted_iota(jnp.int32, (BLOCK, LANES), 0)

    def chain(count, carry):
        slot = pos_ref[every - 1 - count]
        turn, index = slot // blocks, slot % blocks
        after = []
        for tile, value in enumerate(carry):
            line_ref[tile, pl.ds(slot, 1), :] = value
            keep = all_ref[turn, 0, tile, pl.ds(index, 1), :]
            after.append(keep * value + back_ref[turn, tile, pl.ds(index, 1), :])
        return tuple(after)

    zero = jnp.zeros((1, LANES), jnp.float32)
    lax.fori_loop(0, every, chain, tuple(zero for _ in tiles))

    def step(turn, carry):
        at = pl.ds(BLOCK - 1 - turn, blocks, stride=BLOCK)
        after = []
        for tile, value in enumerate(carry):
            grad = dh_ref[tile, at, :] + value
            g_ref[tile, at, :] = grad
            after.append(keep_ref[tile, at, :] * grad)
        return tuple(after)

    start = tuple(line_ref[tile, 0:blocks, :] for tile in range(len(tiles)))
    lax.fori_loop(0, BLOCK, step, start, unroll=UNROLL)
    acc_ref[...] = jnp.zeros_like(acc_ref)
    contract = (((1,), (1,)), ((), ()))

    def block(index, carry):
        at = block_rows(index)
        first = first_ref[index]
        pred = pred_ref[index]
        live = dead_mask(rows, live_ref[index])
        before = jnp.maximum(pred, 0)
        joined = jnp.where((pred >= 0) & (first == 0), 1.0, 0.0)
        for tile, (low, size) in enumerate(tiles):
            lanes = slice(low, low + size)
            grad = g_ref[tile, at, :size]
            rate = rate_ref[tile, at, :size]
            entry = entry_ref[tile, at, :size]
            decay = vec_ref[7:8, lanes]
            minus = expm1_small(rate * decay)
            twice = minus * (2.0 + minus)
            ext_ref[7:8, :size] = enter_ref[tile, pl.ds(index, 1), :size]
            ext_ref[8 : 8 + BLOCK, :size] = h_ref[tile, at, :size]
            d_log = grad * (
                keep_ref[tile, at, :size] * ext_ref[7 : 7 + BLOCK, :size]
                + drive_ref[tile, at, :size] * ((1.0 + twice) / twice)
            )
            slow = rate * d_log
            acc_ref[7, :, lanes] += fold_rows(slow)
            d_rec = (decay * slow * (1.0 - rate)).astype(jnp.bfloat16)
            scaled = grad * jnp.sqrt(-twice) * entry
            d_in = scaled * xc_ref[at, lanes].astype(jnp.float32) * (1.0 - entry)
            d_in = d_in.astype(jnp.bfloat16)
            drec_ref[at, lanes] = d_rec
            din_ref[at, lanes] = d_in
            acc_ref[5, :, lanes] += fold_rows(d_rec.astype(jnp.float32))
            acc_ref[6, :, lanes] += fold_rows(d_in.astype(jnp.float32))
            direct_ref[:, lanes] = scaled
        direct_ref[...] += lax.dot_general(
            drec_ref[at, :], rec_ref[...], contract, preferred_element_type=jnp.float32
        ) + lax.dot_general(
            din_ref[at, :], in_ref[...], contract, preferred_element_type=jnp.float32
        )
        for low, size in tiles:
            lanes = slice(low, low + size)
            dxc = direct_ref[:, lanes]
            u_value = u_ref[at, lanes]
            ext_ref[0:8, :size] = tail_ref[before, :, lanes] * joined
            ext_ref[8 : 8 + BLOCK, :size] = u_value
            acc_ref[4, :, lanes] += fold_rows(dxc)
            acc_ref[0, :, lanes] += fold_rows(dxc * u_value)
            part = dxc * live[:, :size]
            for tap in range(1, TAPS):
                acc_ref[tap, :, lanes] += fold_rows(part * ext_ref[8 - tap : 8 - tap + BLOCK, :size])
            zero_tile = jnp.zeros((8, size), jnp.float32)
            ext_ref[0:8, :size] = zero_tile
            ext_ref[8 : 8 + BLOCK, :size] = part
            ext_ref[8 + BLOCK : 16 + BLOCK, :size] = zero_tile
            du_value = dxc * vec_ref[0:1, lanes]
            head = zero_tile
            for tap in range(1, TAPS):
                weight = vec_ref[tap : tap + 1, lanes]
                du_value = du_value + weight * ext_ref[8 + tap : 8 + tap + BLOCK, :size]
                head = head + weight * ext_ref[tap : tap + 8, :size]
            du_ref[at, lanes] = du_value.astype(jnp.bfloat16)
            last_ref[index, :, lanes] = du_value[BLOCK - 8 :]
            head_ref[index, :, lanes] = head * joined
        return carry

    lax.fori_loop(0, blocks, block, 0)
    for index in range(8):
        total_ref[index : index + 1, :] = jnp.sum(acc_ref[index], axis=0, keepdims=True)


def head_kernel(succ_ref, prev_ref, last_ref, head_ref, out_ref):
    blocks = last_ref.shape[0]

    def block(index, carry):
        succ = succ_ref[index]
        head = head_ref[jnp.maximum(succ, 0)]
        tail = last_ref[index] + jnp.where(succ >= 0, head, jnp.zeros_like(head))
        out_ref[index, :8, :] = prev_ref[index, :8, :]
        out_ref[index, 8:, :] = tail.astype(jnp.bfloat16)
        return carry

    lax.fori_loop(0, blocks, block, 0)


def shaped(shape, dtype=jnp.float32):
    return jax.ShapeDtypeStruct(shape, dtype)


def whole(kernel, scalars, arrays, outs, scratch, name):
    specs = [pl.BlockSpec(memory_space=pltpu.SMEM)] * len(scalars)
    specs += [pl.BlockSpec(memory_space=pltpu.VMEM)] * len(arrays)
    return pl.pallas_call(
        kernel,
        out_shape=outs,
        in_specs=specs,
        out_specs=[pl.BlockSpec(memory_space=pltpu.VMEM)] * len(outs),
        scratch_shapes=scratch,
        compiler_params=pltpu.CompilerParams(vmem_limit_bytes=VMEM_LIMIT),
        name=name,
    )(*scalars, *arrays)


def shards(
    tokens,
    cotangent,
    lengths,
    offsets,
    deal,
    norm_gain1,
    w_branch,
    w_input,
    conv_kernel,
    conv_bias,
    gate_rec,
    bias_rec,
    gate_in,
    bias_in,
    decay_param,
    w_out,
    norm_gain2,
    w_gate,
    w_up,
    w_down,
):
    seq_size, z_size = lax.axis_size("seq"), lax.axis_size("fsdp")
    seq_at, z_at = lax.axis_index("seq"), lax.axis_index("fsdp")
    rows_here, model = tokens.shape
    blocks_here = rows_here // BLOCK
    blocks = seq_size * blocks_here
    every = blocks * z_size
    count = rows_here * seq_size
    width = w_branch.shape[1] // seq_size
    ffw = w_gate.shape[1] // seq_size
    chunk = w_branch.shape[0]
    gate_width = gate_rec.shape[1]
    groups = width // gate_width
    tiles = len(lane_tiles(width))
    tiled = shaped((tiles, count, LANES))

    order = jnp.array([k for k in range(seq_size) if k % 2 == 0] + [k for k in range(seq_size) if k % 2], jnp.int32)
    source = jnp.bitwise_xor(order, seq_at)
    flips = jnp.bitwise_xor(jnp.arange(z_size, dtype=jnp.int32), z_at)
    stored = (source[None, :, None] * z_size + flips[:, None, None]) * blocks_here
    stored = (stored + jnp.arange(blocks_here, dtype=jnp.int32)[None, None, :]).reshape(every)
    logical = deal[stored]
    places = jnp.arange(every, dtype=jnp.int32)
    at_place = logical[None, :] == places[:, None]
    position = jnp.sum(jnp.where(at_place, places[None, :], 0), axis=1)
    mine = logical[:blocks]

    def place_of(wanted):
        hit = logical[None, :] == wanted[:, None]
        return jnp.sum(jnp.where(hit, places[None, :] + 1, 0), axis=1) - 1

    pred = place_of(mine - 1)
    succ = place_of(mine + 1)
    left_over = lengths[None, :] - (mine[:, None] - offsets[None, :]) * BLOCK
    inside = (mine[:, None] >= offsets[None, :]) & (left_over > 0)
    live_count = jnp.max(jnp.where(inside, jnp.minimum(left_over, BLOCK), 0), axis=1)
    first = jnp.any(inside & (mine[:, None] == offsets[None, :]), axis=1).astype(jnp.int32)
    own_live = live_count[:blocks_here]
    live_col = (
        jnp.arange(BLOCK, dtype=jnp.int32)[None, :] < own_live[:, None]
    ).astype(jnp.float32).reshape(rows_here, 1)

    def columns(weight):
        return jnp.swapaxes(as_low(weight).reshape(chunk, seq_size, -1), 0, 1)

    def exchange(value):
        return lax.all_to_all(value, "seq", 0, 0, tiled=True)

    def gather_columns(value):
        got = lax.all_gather(value, "fsdp", axis=0, tiled=False)
        return jnp.swapaxes(got, 0, 1).reshape(-1, value.shape[-1])

    def gather_rows(value):
        return lax.all_gather(value, "fsdp", axis=0, tiled=True)

    barrier = lax.optimization_barrier
    out_w = gather_rows(as_low(w_out))
    mix = exchange(jnp.stack([columns(w_input), columns(w_branch)], axis=1))
    x_pieces = gather_plane(tokens)
    wide_small = jnp.concatenate(
        [
            as_low(conv_kernel),
            as_low(conv_bias)[None],
            as_low(bias_rec)[None],
            as_low(bias_in)[None],
            as_low(decay_param)[None],
            as_low(jnp.pad(jnp.stack([norm_gain1, norm_gain2]), ((0, 0), (0, width // z_size - chunk)))),
        ],
        axis=0,
    ).T
    small = jnp.concatenate([as_low(gate_rec), as_low(gate_in), wide_small], axis=1)
    small, x_pieces = barrier((small, x_pieces))
    small = lax.all_gather(small, "fsdp", axis=0, tiled=False)
    gains = lax.all_gather(small[:, :chunk, 2 * gate_width + 8 :], "seq", axis=0, tiled=False)
    gains = as_wide(gains.reshape(model, 2)).T
    gain_one, gain_two = gains[:1], gains[1:]
    small = small.reshape(width, -1)
    input_w = gather_columns(mix[:, 0])
    branch_w = gather_columns(mix[:, 1])
    ff = exchange(jnp.stack([columns(w_gate), columns(w_up)], axis=1))
    down_w = gather_rows(as_low(w_down))

    same = jnp.arange(width)[:, None] // gate_width == jnp.arange(width)[None, :] // gate_width

    def diagonal(part):
        return jnp.where(same, jnp.tile(part, (1, groups)), jnp.zeros((), jnp.bfloat16))

    rec_w = diagonal(small[:, :gate_width])
    in_w = diagonal(small[:, gate_width : 2 * gate_width])
    vectors = as_wide(small[:, 2 * gate_width : 2 * gate_width + 8]).T
    decay = vectors[7]
    vectors = jnp.concatenate([vectors[:7], -GATE_SCALE * jax.nn.softplus(-decay)[None]], axis=0)

    x_pieces, top_own = barrier((x_pieces, as_low(live_col * as_wide(cotangent))))
    normed_one, u_value = stack(x_pieces, "norm_one", gain_one, (input_w,))
    normed_one, ff = barrier((normed_one, ff))
    gate_w = gather_columns(ff[:, 0])
    up_w = gather_columns(ff[:, 1])
    top_pieces = gather_plane(top_own)

    def edges(rows):
        rows = spread_z(as_low(rows).reshape(blocks * (TAPS - 1), width))
        rows = as_wide(rows).reshape(every, TAPS - 1, width)
        return jnp.pad(rows, ((0, 0), (9 - TAPS, 0), (0, 0)))

    tails = edges(u_value.reshape(blocks, BLOCK, width)[:, BLOCK - TAPS + 1 :])
    branch_pre = mm(normed_one, branch_w)
    conv_low, keep, drive, rate, entry, summary = whole(
        lru_forward_kernel,
        (live_count, first, pred),
        (u_value, tails, vectors, rec_w, in_w),
        (
            shaped((count, width), jnp.bfloat16),
            tiled,
            tiled,
            tiled,
            tiled,
            shaped((2, tiles, blocks, LANES)),
        ),
        [pltpu.VMEM((BLOCK + 8, LANES), jnp.float32)],
        "lru_forward",
    )
    summaries = spread_z(summary)
    summaries, top_pieces, out_w, branch_pre = barrier(
        (summaries, top_pieces, out_w, branch_pre)
    )
    state, gated, enter = whole(
        lru_state_kernel,
        (position,),
        (summaries, keep, drive, branch_pre),
        (
            tiled,
            shaped((count, width), jnp.bfloat16),
            shaped((tiles, blocks, LANES)),
        ),
        [pltpu.VMEM((tiles, every, LANES), jnp.float32)],
        "lru_state",
    )
    gated, gate_w = barrier((gated, gate_w))
    half = count // 2

    def side(rows, odd):
        return rows[half:] if odd else rows[:half]

    resid_in = as_wide(tokens)
    resid_mid = resid_in + scatter_plane(lambda odd: mm(side(gated, odd), out_w))
    scale_two = lax.rsqrt(jnp.mean(resid_mid * resid_mid, axis=-1, keepdims=True) + NORM_EPSILON)
    own_two = as_low(resid_mid * scale_two * gain_two)
    own_two, up_w = barrier((own_two, up_w))
    two_pieces = gather_plane(own_two)
    (top_low,) = stack(top_pieces, "stack_top")
    two_pieces, top_low = barrier((two_pieces, top_low))
    (normed_two,) = stack(two_pieces, "stack_two")
    gate_pre = mm(normed_two, gate_w)
    up_pre = mm(normed_two, up_w)
    act, bend = gelu_parts(gate_pre)
    hidden = as_low(act * up_pre)
    grad_down = mm_tn(hidden, top_low, jnp.bfloat16)
    gate_pre, up_pre, hidden, grad_down, down_w = barrier(
        (gate_pre, up_pre, hidden, grad_down, down_w)
    )
    act, bend = gelu_parts(gate_pre)
    grad_hidden = mm_nt(top_low, down_w)
    d_gate = as_low(grad_hidden * up_pre * gelu_slope(gate_pre, bend))
    d_up = as_low(grad_hidden * act)
    grad_normed_two = scatter_plane(
        lambda odd: mm_nt(side(d_gate, odd), gate_w) + mm_nt(side(d_up, odd), up_w)
    )
    grad_gate = mm_tn(normed_two, d_gate, jnp.bfloat16)
    grad_up = mm_tn(normed_two, d_up, jnp.bfloat16)

    def home_rows(value):
        return lax.psum_scatter(value, "fsdp", scatter_dimension=0, tiled=True)

    def by_owner(values):
        parts = [value.reshape(seq_size, z_size, chunk, value.shape[-1]) for value in values]
        return jnp.transpose(jnp.stack(parts, axis=0), (2, 1, 0, 3, 4))

    def own_columns(got):
        return as_wide(jnp.swapaxes(got, 0, 1).reshape(chunk, -1))

    down_home = home_rows(grad_down)
    ff_pair = by_owner((grad_gate, grad_up)).reshape(z_size * seq_size * 2 * chunk, ffw)
    grad_normed_two, ff_pair, down_home = barrier((grad_normed_two, ff_pair, down_home))
    ff_home = home_rows(ff_pair)

    def gain_home(gain, pairs):
        total = sum(jnp.sum(grad * as_wide(as_low(weight)), axis=1) for grad, weight in pairs)
        return total / as_wide(as_low(gain))

    scaled_two = gain_two * grad_normed_two
    grad_mid = (
        live_col * as_wide(cotangent)
        + scale_two * scaled_two
        - resid_mid
        * scale_two
        * scale_two
        * scale_two
        * jnp.mean(scaled_two * resid_mid, axis=-1, keepdims=True)
    )
    out_pieces = gather_plane(as_low(grad_mid))

    def after_out(value):
        return barrier((value, out_pieces))[0]

    mlp_out = scatter_plane(lambda odd: mm(side(hidden, odd), down_w), after_out)
    mixed = as_low(live_col * (resid_mid + mlp_out))
    grad_out_low, d_branch, direct, send = lru_back(out_pieces, out_w, state, branch_pre, keep)
    backs = spread_z(send)
    grad_out = mm_tn(gated, grad_out_low, jnp.bfloat16)
    backs, grad_out = barrier((backs, grad_out))
    out_home = home_rows(grad_out)
    d_rec, d_in, du_part, du_last, heads, totals = whole(
        lru_grad_kernel,
        (live_count, first, pred, position),
        (
            summaries,
            backs,
            direct,
            keep,
            drive,
            rate,
            entry,
            state,
            enter,
            conv_low,
            u_value,
            tails,
            vectors,
            rec_w,
            in_w,
        ),
        (
            shaped((count, width), jnp.bfloat16),
            shaped((count, width), jnp.bfloat16),
            shaped((count, width), jnp.bfloat16),
            shaped((blocks, 8, width)),
            shaped((blocks, 8, width)),
            shaped((8, width)),
        ),
        [
            pltpu.VMEM((tiles, every, LANES), jnp.float32),
            pltpu.VMEM((tiles, count, LANES), jnp.float32),
            pltpu.VMEM((BLOCK + 16, LANES), jnp.float32),
            pltpu.VMEM((8, 8, width), jnp.float32),
            pltpu.VMEM((BLOCK, width), jnp.float32),
        ],
        "lru_grad",
    )
    du_part, heads, totals, d_rec, d_in, d_branch, ff_home = barrier(
        (du_part, heads, totals, d_rec, d_in, d_branch, ff_home)
    )
    heads = edges(heads[:, 9 - TAPS :])
    grad_branch = mm_tn(normed_one, d_branch, jnp.bfloat16)
    full_rec, full_in = mm_tn(conv_low, d_rec), mm_tn(conv_low, d_in)
    du_part = du_part.reshape(blocks, BLOCK, width)
    (patch,) = whole(
        head_kernel,
        (succ,),
        (du_part[:, BLOCK - 16 :], du_last, heads),
        (shaped((blocks, 16, width), jnp.bfloat16),),
        [],
        "lru_heads",
    )
    d_input = lax.dynamic_update_slice(du_part, patch, (0, BLOCK - 16, 0)).reshape(count, width)
    d_input, mixed, grad_branch, full_rec, full_in, out_home = barrier(
        (d_input, mixed, grad_branch, full_rec, full_in, out_home)
    )
    grad_input = mm_tn(normed_one, d_input, jnp.bfloat16)
    got = exchange(ff_home.reshape(seq_size, 2, chunk, ffw))
    grad_gate_home, grad_up_home = own_columns(got[:, 0]), own_columns(got[:, 1])
    grad_gain_two = gain_home(norm_gain2, ((grad_gate_home, w_gate), (grad_up_home, w_up)))
    grad_normed_one = scatter_plane(
        lambda odd: mm_nt(side(d_branch, odd), branch_w) + mm_nt(side(d_input, odd), input_w)
    )
    scaled_one = gain_one * grad_normed_one
    scale_one = lax.rsqrt(jnp.mean(resid_in * resid_in, axis=-1, keepdims=True) + NORM_EPSILON)
    tokens_grad = as_low(
        grad_mid
        + scale_one * scaled_one
        - resid_in
        * scale_one
        * scale_one
        * scale_one
        * jnp.mean(scaled_one * resid_in, axis=-1, keepdims=True)
    )

    def blocks_of(full, start):
        place = start + jnp.arange(width)[:, None] % gate_width
        fold = (place == jnp.arange(2 * gate_width)[None, :]).astype(jnp.float32)
        full = jnp.where(same, full, 0.0)
        return jnp.dot(full, fold, precision=lax.Precision.HIGHEST)

    totals = jnp.concatenate(
        [totals[:7], totals[7:] * (GATE_SCALE * jax.nn.sigmoid(-decay))[None]], axis=0
    )
    owned = width // z_size
    gates = blocks_of(full_rec, 0) + blocks_of(full_in, gate_width)
    gates = as_low(gates).reshape(z_size, owned, 2 * gate_width)
    totals = jnp.swapaxes(jnp.pad(totals, ((0, 8), (0, 0))).reshape(16, z_size, owned), 0, 1)
    totals = as_low(totals)
    lanes = max(width, 2 * gate_width)
    edge = seq_size * chunk
    pack = jnp.concatenate(
        [
            jnp.pad(part, ((0, 0), (0, 0), (0, lanes - part.shape[-1])))
            for part in (by_owner((grad_branch,)).reshape(z_size, edge, width), gates, totals)
        ],
        axis=1,
    )
    pack = home_rows(pack.reshape(z_size * pack.shape[1], lanes))
    input_home = home_rows(by_owner((grad_input,)).reshape(z_size * edge, width))
    grad_branch_home = own_columns(exchange(pack[:edge, :width].reshape(seq_size, chunk, width)))
    grad_input_home = own_columns(exchange(input_home.reshape(seq_size, chunk, width)))
    grad_gain_one = gain_home(
        norm_gain1, ((grad_branch_home, w_branch), (grad_input_home, w_input))
    )
    gates = as_wide(pack[edge : edge + owned])
    totals = as_wide(pack[edge + owned :, :owned])
    return (
        mixed,
        tokens_grad,
        grad_gain_one,
        grad_branch_home,
        grad_input_home,
        totals[:TAPS],
        totals[4],
        gates[:, :gate_width],
        totals[5],
        gates[:, gate_width : 2 * gate_width],
        totals[6],
        totals[7],
        as_wide(out_home),
        grad_gain_two,
        grad_gate_home,
        grad_up_home,
        as_wide(down_home),
    )


def solution(mesh):
    row = P(("seq", "fsdp"))
    rows = P(("seq", "fsdp"), None)
    columns = P(None, ("seq", "fsdp"))
    return jax.shard_map(
        shards,
        mesh=mesh,
        in_specs=(
            rows,
            rows,
            P(),
            P(),
            P(),
            row,
            rows,
            rows,
            columns,
            row,
            rows,
            row,
            rows,
            row,
            row,
            rows,
            row,
            rows,
            rows,
            rows,
        ),
        out_specs=(
            rows,
            rows,
            row,
            rows,
            rows,
            columns,
            row,
            rows,
            row,
            rows,
            row,
            row,
            rows,
            row,
            rows,
            rows,
            rows,
        ),
        check_vma=False,
    )
```

```python
import jax
import jax.numpy as jnp
from jax import lax
from jax.experimental import pallas as pl
from jax.experimental.pallas import tpu as pltpu
from jax.sharding import PartitionSpec as P

BLOCK = 128
LANES = 128
TAPS = 4
UNROLL = 8
NORM_EPSILON = 1e-06
GATE_SCALE = 8.0
VMEM_LIMIT = 48 * 1024 * 1024
GELU_C = 0.7978845608028654
GELU_A = 0.044715
LIGHT = pl.CostEstimate(flops=1, transcendentals=0, bytes_accessed=1)


def as_low(values):
    return values.astype(jnp.bfloat16)


def as_wide(values):
    return values.astype(jnp.float32)


def mm(left, right, out=jnp.float32):
    return jnp.dot(left, right, preferred_element_type=jnp.float32).astype(out)


def mm_tn(left, right, out=jnp.float32):
    return lax.dot_general(
        left, right, (((0,), (0,)), ((), ())), preferred_element_type=jnp.float32
    ).astype(out)


def mm_nt(left, right, out=jnp.float32):
    return lax.dot_general(
        left, right, (((1,), (1,)), ((), ())), preferred_element_type=jnp.float32
    ).astype(out)


def swap(values, axis, flip):
    count = lax.axis_size(axis)
    return lax.ppermute(values, axis, [(i, i ^ flip) for i in range(count)])


barrier = lax.optimization_barrier


def plane_even(own):
    return [own] + [swap(own, "seq", k) for k in range(2, lax.axis_size("seq"), 2)]


def plane_first(own):
    count = lax.axis_size("seq")
    flips = (2, 4) if count == 8 else range(2, count, 2)
    return [swap(own, "seq", k) for k in flips]


def plane_second(own, first):
    even = [own, *first]
    if lax.axis_size("seq") == 8:
        half = own.shape[0] // 2
        near, side = first
        even.append((swap(side[:half], "seq", 2), swap(near[half:], "seq", 4)))
    return even


def plane_all(even):
    return list(even) + [jax.tree.map(lambda part: swap(part, "seq", 1), piece) for piece in even]


def slot_order():
    evens = lax.axis_size("seq") // 2
    return sorted(range(1, evens), key=lambda slot: -bin(slot).count("1")) + [0]


def scatter_plane(product):
    evens = lax.axis_size("seq") // 2
    order = slot_order()
    ready, pairs, after = {}, {}, None

    def odd(slot):
        value = as_low(product(evens + slot, after))
        ready[slot] = swap(value, "seq", 1)
        return value

    after = odd(order[0])
    for index, slot in enumerate(order):
        if index + 1 < evens:
            after = odd(order[index + 1])
        after = product(slot, after) + as_wide(ready[slot])
        pairs[slot] = after
    if evens != 4:
        return [swap(as_low(pairs[slot]), "seq", 2 * slot) if slot else after for slot in order], after
    own, near, side, far = (pairs[slot] for slot in range(4))
    half = far.shape[0] // 2
    far_top = swap(as_low(far[:half]), "seq", 2)
    far_low = swap(as_low(far[half:]), "seq", 4)
    near_top = swap(as_low(near[:half]), "seq", 2)
    side_low = swap(as_low(side[half:]), "seq", 4)
    near_low = swap(as_low(near[half:] + as_wide(far_low)), "seq", 2)
    side_top = swap(as_low(side[:half] + as_wide(far_top)), "seq", 4)
    return [own, (near_top, near_low), (side_top, side_low)], own


def split_pairs(pair):
    rows = pair.shape[0] // (lax.axis_size("seq") // 2)
    parts = [pair[slot * rows : (slot + 1) * rows] for slot in slot_order()]
    return [as_low(part) for part in parts[:-1]] + parts[-1:]


def scatter_pairs(parts):
    return [
        swap(part, "seq", 2 * slot) if slot else part for slot, part in zip(slot_order(), parts)
    ]


def slot_product(operands, multiply):
    rows = operands[0].shape[0] // lax.axis_size("seq")

    def product(slot, after):
        parts = tuple(operand[slot * rows : (slot + 1) * rows] for operand in operands)
        if after is not None:
            parts = barrier((*parts, after))[:-1]
        return multiply(*parts)

    return product


def summed(parts):
    total = None
    for part in parts:
        if isinstance(part, (tuple, list)):
            part = jnp.concatenate(part, axis=0)
        total = as_wide(part) if total is None else total + as_wide(part)
    return total


def gather_small(value, axis):
    value = value[None]
    bit = 1
    while bit < lax.axis_size(axis):
        other = swap(value, axis, bit)
        upper = (lax.axis_index(axis) // bit) % 2 == 1
        value = jnp.where(
            upper, jnp.concatenate([other, value]), jnp.concatenate([value, other])
        )
        bit *= 2
    return value


def spread_z(value):
    count = lax.axis_size("fsdp")
    return jnp.stack([value] + [swap(value, "fsdp", j) for j in range(1, count)], axis=0)


def gelu_parts(values):
    inner = GELU_C * (values + GELU_A * values * values * values)
    bend = jnp.tanh(inner)
    return (0.5 * values * (1.0 + bend), bend)


def gelu_slope(values, bend):
    return 0.5 * (1.0 + bend) + 0.5 * values * (1.0 - bend * bend) * GELU_C * (
        1.0 + 3.0 * GELU_A * values * values
    )


def expm1_small(values):
    series = values * (1.0 / 120.0) + 1.0 / 24.0
    for scale in (1.0 / 6.0, 0.5, 1.0):
        series = series * values + scale
    return series * values


def block_rows(index):
    return pl.ds(pl.multiple_of(index * BLOCK, BLOCK), BLOCK)


def lane_tiles(width):
    return [(low, min(LANES, width - low)) for low in range(0, width, LANES)]


def piece_specs(pieces, steps):
    specs = []
    chunk = pieces[0].shape[0] // steps
    block = (chunk, pieces[0].shape[1])
    last = steps // 2 - 1
    for piece in pieces:
        if isinstance(piece, (tuple, list)):
            specs.append(pl.BlockSpec(block, lambda i: (jnp.minimum(i, last), 0)))
            specs.append(pl.BlockSpec(block, lambda i: (jnp.maximum(i - last - 1, 0), 0)))
        else:
            specs.append(pl.BlockSpec(block, lambda i: (i, 0)))
    return specs


def piece_halves(pieces):
    return [len(piece) if isinstance(piece, (tuple, list)) else 1 for piece in pieces]


def joined_rows(refs, halves):
    upper = pl.program_id(0) < pl.num_programs(0) // 2
    rows, at = [], 0
    for parts in halves:
        value = refs[at][...]
        rows.append(value if parts == 1 else jnp.where(upper, value, refs[at + 1][...]))
        at += parts
    return jnp.concatenate(rows, axis=0)


def stack(pieces, name, gain=None, weights=(), gated=False, steps=8):
    count = len(pieces)
    halves, flat = piece_halves(pieces), jax.tree.leaves(pieces)
    rows, model = pieces[0].shape
    chunk = rows // steps
    extra = ([gain] if gain is not None else []) + list(weights)

    def kernel(*refs):
        values = joined_rows(refs[: len(flat)], halves)
        refs = refs[len(flat) :]
        if gain is not None:
            gain_ref, refs = refs[0], refs[1:]
            wide = values.astype(jnp.float32)
            scale = lax.rsqrt(jnp.mean(wide * wide, axis=-1, keepdims=True) + NORM_EPSILON)
            values = (wide * scale * gain_ref[...]).astype(jnp.bfloat16)
        weight_refs, refs = refs[: len(weights)], refs[len(weights) :]
        refs[0][...] = values.reshape(count, chunk, model)
        products = []
        for weight_ref, out_ref in zip(weight_refs, refs[1:]):
            out = jnp.dot(values, weight_ref[...], preferred_element_type=jnp.float32)
            out_ref[...] = out.reshape(count, chunk, out.shape[1])
            products.append(out)
        if gated:
            out = (gelu_parts(products[0])[0] * products[1]).astype(jnp.bfloat16)
            refs[-1][...] = out.reshape(count, chunk, out.shape[1])

    widths = [weight.shape[1] for weight in weights]
    outs = [shaped((count, rows, model), jnp.bfloat16)] + [shaped((count, rows, w)) for w in widths]
    if gated:
        outs.append(shaped((count, rows, widths[0]), jnp.bfloat16))
    done = pl.pallas_call(
        kernel,
        grid=(steps,),
        in_specs=piece_specs(pieces, steps) + [pl.BlockSpec(e.shape, lambda i: (0, 0)) for e in extra],
        out_specs=[pl.BlockSpec((count, chunk, o.shape[2]), lambda i: (0, i, 0)) for o in outs],
        out_shape=outs,
        compiler_params=pltpu.CompilerParams(vmem_limit_bytes=VMEM_LIMIT),
        cost_estimate=LIGHT,
        name=name,
    )(*flat, *extra)
    return [out.reshape(count * rows, out.shape[2]) for out in done]


def ff_backward(top, down_w, gate_pre, up_pre, steps=8):
    chunk = top.shape[0] // steps
    ffw, model = down_w.shape

    def kernel(top_ref, down_ref, gate_ref, up_ref, d_gate_ref, d_up_ref):
        grad = lax.dot_general(
            top_ref[...], down_ref[...], (((1,), (1,)), ((), ())), preferred_element_type=jnp.float32
        )
        gate = gate_ref[...]
        act, bend = gelu_parts(gate)
        d_gate_ref[...] = (grad * up_ref[...] * gelu_slope(gate, bend)).astype(jnp.bfloat16)
        d_up_ref[...] = (grad * act).astype(jnp.bfloat16)

    block = pl.BlockSpec((chunk, ffw), lambda i: (i, 0))
    return pl.pallas_call(
        kernel,
        grid=(steps,),
        in_specs=[
            pl.BlockSpec((chunk, model), lambda i: (i, 0)),
            pl.BlockSpec((ffw, model), lambda i: (0, 0)),
            block,
            block,
        ],
        out_specs=[block, block],
        out_shape=[shaped((top.shape[0], ffw), jnp.bfloat16)] * 2,
        compiler_params=pltpu.CompilerParams(vmem_limit_bytes=VMEM_LIMIT),
        cost_estimate=LIGHT,
        name="ff_backward",
    )(top, down_w, gate_pre, up_pre)


def project(rows, weight, name, steps=8):
    chunk = rows.shape[0] // steps
    width = weight.shape[1]

    def kernel(rows_ref, weight_ref, out_ref):
        out_ref[...] = jnp.dot(rows_ref[...], weight_ref[...], preferred_element_type=jnp.float32)

    return pl.pallas_call(
        kernel,
        grid=(steps,),
        in_specs=[
            pl.BlockSpec((chunk, rows.shape[1]), lambda i: (i, 0)),
            pl.BlockSpec(weight.shape, lambda i: (0, 0)),
        ],
        out_specs=pl.BlockSpec((chunk, width), lambda i: (i, 0)),
        out_shape=shaped((rows.shape[0], width)),
        compiler_params=pltpu.CompilerParams(vmem_limit_bytes=VMEM_LIMIT),
        cost_estimate=pl.CostEstimate(
            flops=2 * rows.size * width,
            transcendentals=0,
            bytes_accessed=2 * rows.size + 4 * rows.shape[0] * width,
        ),
        name=name,
    )(rows, weight)


def dead_mask(rows, live_count):
    return (rows < live_count).astype(jnp.float32)


def lru_forward_kernel(
    live_ref,
    first_ref,
    pred_ref,
    u_ref,
    tail_ref,
    vec_ref,
    rec_ref,
    in_ref,
    xc_ref,
    keep_ref,
    drive_ref,
    rate_ref,
    entry_ref,
    sum_ref,
    ext_ref,
):
    blocks = u_ref.shape[0] // BLOCK
    tiles = lane_tiles(u_ref.shape[1])
    rows = lax.broadcasted_iota(jnp.int32, (BLOCK, LANES), 0)

    def block(index, carry):
        at = block_rows(index)
        first = first_ref[index]
        pred = pred_ref[index]
        live = dead_mask(rows, live_ref[index])
        before = jnp.maximum(pred, 0)
        joined = jnp.where((pred >= 0) & (first == 0), 1.0, 0.0)
        for low, size in tiles:
            lanes = slice(low, low + size)
            u_value = u_ref[at, lanes]
            ext_ref[0:8, :size] = tail_ref[before, :, lanes] * joined
            ext_ref[8 : 8 + BLOCK, :size] = u_value
            later = vec_ref[1:2, lanes] * ext_ref[7 : 7 + BLOCK, :size]
            for tap in range(2, TAPS):
                later = later + vec_ref[tap : tap + 1, lanes] * ext_ref[8 - tap : 8 - tap + BLOCK, :size]
            conv = vec_ref[4:5, lanes] + vec_ref[0:1, lanes] * u_value + later * live[:, :size]
            xc_ref[at, lanes] = conv.astype(jnp.bfloat16)
        low_rows = xc_ref[at, :]
        pre_rec = jnp.dot(low_rows, rec_ref[...], preferred_element_type=jnp.float32)
        pre_in = jnp.dot(low_rows, in_ref[...], preferred_element_type=jnp.float32)
        for tile, (low, size) in enumerate(tiles):
            lanes = slice(low, low + size)
            rate = jax.nn.sigmoid(pre_rec[:, lanes] + vec_ref[5:6, lanes])
            entry = jax.nn.sigmoid(pre_in[:, lanes] + vec_ref[6:7, lanes])
            minus = expm1_small(rate * vec_ref[7:8, lanes])
            rate_ref[tile, at, :size] = rate
            entry_ref[tile, at, :size] = entry
            keep_ref[tile, at, :size] = (1.0 + minus) * live[:, :size]
            drive_ref[tile, at, :size] = (
                jnp.sqrt(-minus * (2.0 + minus)) * entry * low_rows[:, lanes].astype(jnp.float32)
            )

        @pl.when(first > 0)
        def _():
            top = pl.ds(pl.multiple_of(index * BLOCK, BLOCK), 8)
            after = (rows[:8] > 0).astype(jnp.float32)
            for tile in range(len(tiles)):
                keep_ref[tile, top, :] = keep_ref[tile, top, :] * after

        return carry

    lax.fori_loop(0, blocks, block, 0)

    def step(place, carry):
        at = pl.ds(place, blocks, stride=BLOCK)
        after = []
        for tile, (total, state) in enumerate(carry):
            keep = keep_ref[tile, at, :]
            after.append((total * keep, keep * state + drive_ref[tile, at, :]))
        return tuple(after)

    ones = jnp.ones((blocks, LANES), jnp.float32)
    start = tuple((ones, jnp.zeros_like(ones)) for _ in tiles)
    ends = lax.fori_loop(0, BLOCK, step, start, unroll=UNROLL)
    for tile, (total, state) in enumerate(ends):
        sum_ref[0, tile] = total
        sum_ref[1, tile] = state


def lru_state_kernel(pos_ref, all_ref, keep_ref, drive_ref, ypre_ref, h_ref, hy_ref, enter_ref, line_ref):
    tiles = lane_tiles(ypre_ref.shape[1])
    turns, _, _, blocks, _ = all_ref.shape

    def chain(place, states):
        slot = pos_ref[place]
        turn, index = slot // blocks, slot % blocks
        after = []
        for tile, state in enumerate(states):
            line_ref[tile, pl.ds(slot, 1), :] = state
            keep = all_ref[turn, 0, tile, pl.ds(index, 1), :]
            after.append(keep * state + all_ref[turn, 1, tile, pl.ds(index, 1), :])
        return tuple(after)

    zero = jnp.zeros((1, LANES), jnp.float32)
    lax.fori_loop(0, turns * blocks, chain, tuple(zero for _ in tiles))
    for tile in range(len(tiles)):
        enter_ref[tile] = line_ref[tile, 0:blocks, :]

    def step(place, states):
        at = pl.ds(place, blocks, stride=BLOCK)
        after = []
        for tile, state in enumerate(states):
            state = keep_ref[tile, at, :] * state + drive_ref[tile, at, :]
            h_ref[tile, at, :] = state
            after.append(state)
        return tuple(after)

    start = tuple(line_ref[tile, 0:blocks, :] for tile in range(len(tiles)))
    lax.fori_loop(0, BLOCK, step, start, unroll=UNROLL)

    def block(index, carry):
        at = block_rows(index)
        for tile, (low, size) in enumerate(tiles):
            lanes = slice(low, low + size)
            act = gelu_parts(ypre_ref[at, lanes])[0]
            hy_ref[at, lanes] = (h_ref[tile, at, :size] * act).astype(jnp.bfloat16)
        return carry

    lax.fori_loop(0, blocks, block, 0)


def lru_back(pieces, out_w, state, branch_pre, keep, steps=8):
    count = len(pieces)
    halves, flat = piece_halves(pieces), jax.tree.leaves(pieces)
    rows, model = pieces[0].shape
    width = out_w.shape[0]
    tiles = lane_tiles(width)
    chunk = rows // steps
    blocks = count * rows // BLOCK

    def kernel(*refs):
        values = joined_rows(refs[: len(flat)], halves)
        w_ref, h_ref, ypre_ref, keep_ref, out_ref, dy_ref, dh_ref, send_ref = refs[len(flat) :]
        here = pl.program_id(0)
        out_ref[...] = values.reshape(count, chunk, model)
        grads = lax.dot_general(
            values, w_ref[...], (((1,), (1,)), ((), ())), preferred_element_type=jnp.float32
        )
        for slot in range(count):
            span = pl.ds(pl.multiple_of(slot * rows + here * chunk, chunk), chunk)
            for tile, (low, size) in enumerate(tiles):
                lanes = slice(low, low + size)
                value = ypre_ref[slot, :, lanes]
                act, bend = gelu_parts(value)
                grad = grads[slot * chunk : (slot + 1) * chunk, lanes]
                slope = gelu_slope(value, bend)
                dy_ref[slot, :, lanes] = (grad * h_ref[tile, slot, :, :size] * slope).astype(jnp.bfloat16)
                dh_ref[tile, span, :size] = grad * act

        @pl.when(here == steps - 1)
        def _():
            def step(turn, carry):
                at = pl.ds(BLOCK - 1 - turn, blocks, stride=BLOCK)
                return tuple(
                    keep_ref[tile, at, :] * (dh_ref[tile, at, :] + value)
                    for tile, value in enumerate(carry)
                )

            zero = jnp.zeros((blocks, LANES), jnp.float32)
            ends = lax.fori_loop(0, BLOCK, step, tuple(zero for _ in tiles), unroll=UNROLL)
            for tile, value in enumerate(ends):
                send_ref[tile] = value

    depth = len(tiles)
    total = count * rows
    out, dy, dh, send = pl.pallas_call(
        kernel,
        grid=(steps,),
        in_specs=piece_specs(pieces, steps)
        + [
            pl.BlockSpec((width, model), lambda i: (0, 0)),
            pl.BlockSpec((depth, count, chunk, LANES), lambda i: (0, 0, i, 0)),
            pl.BlockSpec((count, chunk, width), lambda i: (0, i, 0)),
            pl.BlockSpec((depth, total, LANES), lambda i: (0, 0, 0)),
        ],
        out_specs=[
            pl.BlockSpec((count, chunk, model), lambda i: (0, i, 0)),
            pl.BlockSpec((count, chunk, width), lambda i: (0, i, 0)),
            pl.BlockSpec((depth, total, LANES), lambda i: (0, 0, 0)),
            pl.BlockSpec((depth, blocks, LANES), lambda i: (0, 0, 0)),
        ],
        out_shape=[
            shaped((count, rows, model), jnp.bfloat16),
            shaped((count, rows, width), jnp.bfloat16),
            shaped((depth, total, LANES)),
            shaped((depth, blocks, LANES)),
        ],
        compiler_params=pltpu.CompilerParams(vmem_limit_bytes=VMEM_LIMIT),
        cost_estimate=LIGHT,
        name="lru_back",
    )(
        *flat,
        out_w,
        state.reshape(depth, count, rows, LANES),
        branch_pre.reshape(count, rows, width),
        keep,
    )
    return out.reshape(total, model), dy.reshape(total, width), dh, send


def fold_rows(values):
    return values.reshape(BLOCK // 8, 8, values.shape[1]).sum(axis=0)


def lru_grad_kernel(
    live_ref,
    first_ref,
    pred_ref,
    pos_ref,
    all_ref,
    back_ref,
    dh_ref,
    keep_ref,
    drive_ref,
    rate_ref,
    entry_ref,
    h_ref,
    enter_ref,
    xc_ref,
    u_ref,
    tail_ref,
    vec_ref,
    rec_ref,
    in_ref,
    drec_ref,
    din_ref,
    du_ref,
    last_ref,
    head_ref,
    total_ref,
    line_ref,
    g_ref,
    ext_ref,
    acc_ref,
    direct_ref,
):
    blocks = u_ref.shape[0] // BLOCK
    width = u_ref.shape[1]
    tiles = lane_tiles(width)
    every = back_ref.shape[0] * blocks
    rows = lax.broadcasted_iota(jnp.int32, (BLOCK, LANES), 0)

    def chain(count, carry):
        slot = pos_ref[every - 1 - count]
        turn, index = slot // blocks, slot % blocks
        after = []
        for tile, value in enumerate(carry):
            line_ref[tile, pl.ds(slot, 1), :] = value
            keep = all_ref[turn, 0, tile, pl.ds(index, 1), :]
            after.append(keep * value + back_ref[turn, tile, pl.ds(index, 1), :])
        return tuple(after)

    zero = jnp.zeros((1, LANES), jnp.float32)
    lax.fori_loop(0, every, chain, tuple(zero for _ in tiles))

    def step(turn, carry):
        at = pl.ds(BLOCK - 1 - turn, blocks, stride=BLOCK)
        after = []
        for tile, value in enumerate(carry):
            grad = dh_ref[tile, at, :] + value
            g_ref[tile, at, :] = grad
            after.append(keep_ref[tile, at, :] * grad)
        return tuple(after)

    start = tuple(line_ref[tile, 0:blocks, :] for tile in range(len(tiles)))
    lax.fori_loop(0, BLOCK, step, start, unroll=UNROLL)
    acc_ref[...] = jnp.zeros_like(acc_ref)
    contract = (((1,), (1,)), ((), ()))

    def block(index, carry):
        at = block_rows(index)
        first = first_ref[index]
        pred = pred_ref[index]
        live = dead_mask(rows, live_ref[index])
        before = jnp.maximum(pred, 0)
        joined = jnp.where((pred >= 0) & (first == 0), 1.0, 0.0)
        for tile, (low, size) in enumerate(tiles):
            lanes = slice(low, low + size)
            grad = g_ref[tile, at, :size]
            rate = rate_ref[tile, at, :size]
            entry = entry_ref[tile, at, :size]
            decay = vec_ref[7:8, lanes]
            minus = expm1_small(rate * decay)
            twice = minus * (2.0 + minus)
            ext_ref[7:8, :size] = enter_ref[tile, pl.ds(index, 1), :size]
            ext_ref[8 : 8 + BLOCK, :size] = h_ref[tile, at, :size]
            d_log = grad * (
                keep_ref[tile, at, :size] * ext_ref[7 : 7 + BLOCK, :size]
                + drive_ref[tile, at, :size] * ((1.0 + twice) / twice)
            )
            slow = rate * d_log
            acc_ref[7, :, lanes] += fold_rows(slow)
            d_rec = (decay * slow * (1.0 - rate)).astype(jnp.bfloat16)
            scaled = grad * jnp.sqrt(-twice) * entry
            d_in = scaled * xc_ref[at, lanes].astype(jnp.float32) * (1.0 - entry)
            d_in = d_in.astype(jnp.bfloat16)
            drec_ref[at, lanes] = d_rec
            din_ref[at, lanes] = d_in
            acc_ref[5, :, lanes] += fold_rows(d_rec.astype(jnp.float32))
            acc_ref[6, :, lanes] += fold_rows(d_in.astype(jnp.float32))
            direct_ref[:, lanes] = scaled
        direct_ref[...] += lax.dot_general(
            drec_ref[at, :], rec_ref[...], contract, preferred_element_type=jnp.float32
        ) + lax.dot_general(
            din_ref[at, :], in_ref[...], contract, preferred_element_type=jnp.float32
        )
        for low, size in tiles:
            lanes = slice(low, low + size)
            dxc = direct_ref[:, lanes]
            u_value = u_ref[at, lanes]
            ext_ref[0:8, :size] = tail_ref[before, :, lanes] * joined
            ext_ref[8 : 8 + BLOCK, :size] = u_value
            acc_ref[4, :, lanes] += fold_rows(dxc)
            acc_ref[0, :, lanes] += fold_rows(dxc * u_value)
            part = dxc * live[:, :size]
            for tap in range(1, TAPS):
                acc_ref[tap, :, lanes] += fold_rows(part * ext_ref[8 - tap : 8 - tap + BLOCK, :size])
            zero_tile = jnp.zeros((8, size), jnp.float32)
            ext_ref[0:8, :size] = zero_tile
            ext_ref[8 : 8 + BLOCK, :size] = part
            ext_ref[8 + BLOCK : 16 + BLOCK, :size] = zero_tile
            du_value = dxc * vec_ref[0:1, lanes]
            head = zero_tile
            for tap in range(1, TAPS):
                weight = vec_ref[tap : tap + 1, lanes]
                du_value = du_value + weight * ext_ref[8 + tap : 8 + tap + BLOCK, :size]
                head = head + weight * ext_ref[tap : tap + 8, :size]
            du_ref[at, lanes] = du_value.astype(jnp.bfloat16)
            last_ref[index, :, lanes] = du_value[BLOCK - 8 :]
            head_ref[index, :, lanes] = head * joined
        return carry

    lax.fori_loop(0, blocks, block, 0)
    for index in range(8):
        total_ref[index : index + 1, :] = jnp.sum(acc_ref[index], axis=0, keepdims=True)


def head_kernel(succ_ref, prev_ref, last_ref, head_ref, out_ref):
    blocks = last_ref.shape[0]

    def block(index, carry):
        succ = succ_ref[index]
        head = head_ref[jnp.maximum(succ, 0)]
        tail = last_ref[index] + jnp.where(succ >= 0, head, jnp.zeros_like(head))
        out_ref[index, :8, :] = prev_ref[index, :8, :]
        out_ref[index, 8:, :] = tail.astype(jnp.bfloat16)
        return carry

    lax.fori_loop(0, blocks, block, 0)


def shaped(shape, dtype=jnp.float32):
    return jax.ShapeDtypeStruct(shape, dtype)


def whole(kernel, scalars, arrays, outs, scratch, name):
    specs = [pl.BlockSpec(memory_space=pltpu.SMEM)] * len(scalars)
    specs += [pl.BlockSpec(memory_space=pltpu.VMEM)] * len(arrays)
    return pl.pallas_call(
        kernel,
        out_shape=outs,
        in_specs=specs,
        out_specs=[pl.BlockSpec(memory_space=pltpu.VMEM)] * len(outs),
        scratch_shapes=scratch,
        compiler_params=pltpu.CompilerParams(vmem_limit_bytes=VMEM_LIMIT),
        cost_estimate=LIGHT,
        name=name,
    )(*scalars, *arrays)


def shards(
    tokens,
    cotangent,
    lengths,
    offsets,
    deal,
    norm_gain1,
    w_branch,
    w_input,
    conv_kernel,
    conv_bias,
    gate_rec,
    bias_rec,
    gate_in,
    bias_in,
    decay_param,
    w_out,
    norm_gain2,
    w_gate,
    w_up,
    w_down,
):
    seq_size, z_size = lax.axis_size("seq"), lax.axis_size("fsdp")
    seq_at, z_at = lax.axis_index("seq"), lax.axis_index("fsdp")
    rows_here, model = tokens.shape
    blocks_here = rows_here // BLOCK
    blocks = seq_size * blocks_here
    every = blocks * z_size
    count = rows_here * seq_size
    width = w_branch.shape[1] // seq_size
    ffw = w_gate.shape[1] // seq_size
    chunk = w_branch.shape[0]
    gate_width = gate_rec.shape[1]
    groups = width // gate_width
    tiles = len(lane_tiles(width))
    tiled = shaped((tiles, count, LANES))

    order = jnp.array([k for k in range(seq_size) if k % 2 == 0] + [k for k in range(seq_size) if k % 2], jnp.int32)
    source = jnp.bitwise_xor(order, seq_at)
    flips = jnp.bitwise_xor(jnp.arange(z_size, dtype=jnp.int32), z_at)
    stored = (source[None, :, None] * z_size + flips[:, None, None]) * blocks_here
    stored = (stored + jnp.arange(blocks_here, dtype=jnp.int32)[None, None, :]).reshape(every)
    logical = deal[stored]
    places = jnp.arange(every, dtype=jnp.int32)
    at_place = logical[None, :] == places[:, None]
    position = jnp.sum(jnp.where(at_place, places[None, :], 0), axis=1)
    mine = logical[:blocks]

    def place_of(wanted):
        hit = logical[None, :] == wanted[:, None]
        return jnp.sum(jnp.where(hit, places[None, :] + 1, 0), axis=1) - 1

    pred = place_of(mine - 1)
    succ = place_of(mine + 1)
    left_over = lengths[None, :] - (mine[:, None] - offsets[None, :]) * BLOCK
    inside = (mine[:, None] >= offsets[None, :]) & (left_over > 0)
    live_count = jnp.max(jnp.where(inside, jnp.minimum(left_over, BLOCK), 0), axis=1)
    first = jnp.any(inside & (mine[:, None] == offsets[None, :]), axis=1).astype(jnp.int32)
    own_live = live_count[:blocks_here]
    live_col = (
        jnp.arange(BLOCK, dtype=jnp.int32)[None, :] < own_live[:, None]
    ).astype(jnp.float32).reshape(rows_here, 1)

    def columns(weight):
        return jnp.swapaxes(as_low(weight).reshape(chunk, seq_size, -1), 0, 1)

    def exchange(value):
        return lax.all_to_all(value, "seq", 0, 0, tiled=True)

    def gather_rows(value):
        return lax.all_gather(value, "fsdp", axis=0, tiled=True)

    def gather_columns(value):
        got = lax.all_gather(value, "fsdp", axis=0, tiled=False)
        return jnp.swapaxes(got, 0, 1).reshape(-1, value.shape[-1])

    gains = gather_small(as_low(jnp.stack([norm_gain1, norm_gain2])), "seq")
    x_first = plane_first(tokens)
    out_w = gather_rows(as_low(w_out))
    mix = exchange(jnp.stack([columns(w_input), columns(w_branch)], axis=1))
    x_even = plane_second(tokens, x_first)
    mix, out_w, x_even = barrier((mix, out_w, x_even))
    input_w = gather_columns(mix[:, 0])
    branch_w = gather_columns(mix[:, 1])
    x_pieces = plane_all(x_even)
    params = [conv_kernel, conv_bias[None], bias_rec[None], bias_in[None], decay_param[None]]
    gains = jnp.pad(gains.reshape(2 * seq_size, chunk), ((0, 0), (0, width // z_size - chunk)))
    params = jnp.concatenate([as_low(part) for part in params] + [gains], axis=0).T
    small = jnp.concatenate([as_low(gate_rec), as_low(gate_in), params], axis=1)
    small = gather_small(small, "fsdp")
    gains = small[:, :chunk, 2 * gate_width + 8 :].reshape(z_size, chunk, seq_size, 2)
    gains = as_wide(jnp.transpose(gains, (3, 2, 0, 1)).reshape(2, model))
    gain_one, gain_two = gains[:1], gains[1:]
    small = small.reshape(width, -1)

    same = jnp.arange(width)[:, None] // gate_width == jnp.arange(width)[None, :] // gate_width

    def diagonal(part):
        return jnp.where(same, jnp.tile(part, (1, groups)), jnp.zeros((), jnp.bfloat16))

    vectors = as_wide(small[:, 2 * gate_width : 2 * gate_width + 8]).T
    decay = vectors[7]
    vectors = jnp.concatenate([vectors[:7], -GATE_SCALE * jax.nn.softplus(-decay)[None]], axis=0)
    ff = jnp.stack([columns(w_gate), columns(w_up)], axis=1)
    top_own = as_low(live_col * as_wide(cotangent))
    x_pieces, ff, top_own = barrier((x_pieces, ff, top_own))
    ff = exchange(ff)
    top_even = plane_even(top_own)

    normed_one, u_value = stack(x_pieces, "norm_one", gain_one, (input_w,))
    u_value, gates_in = barrier((u_value, small))
    rec_w = diagonal(gates_in[:, :gate_width])
    in_w = diagonal(gates_in[:, gate_width : 2 * gate_width])
    down_w = gather_rows(as_low(w_down))

    def edges(rows):
        rows = spread_z(as_low(barrier(rows)).reshape(blocks * (TAPS - 1), width))
        rows = as_wide(rows).reshape(every, TAPS - 1, width)
        return jnp.pad(rows, ((0, 0), (9 - TAPS, 0), (0, 0)))

    tails = edges(u_value.reshape(blocks, BLOCK, width)[:, BLOCK - TAPS + 1 :])
    tails, rec_w, in_w, vectors, ff_gate, ff_up = barrier(
        (tails, rec_w, in_w, vectors, ff[:, 0], ff[:, 1])
    )
    gate_w = gather_columns(ff_gate)
    up_w = gather_columns(ff_up)
    conv_low, keep, drive, rate, entry, summary = whole(
        lru_forward_kernel,
        (live_count, first, pred),
        (u_value, tails, vectors, rec_w, in_w),
        (
            shaped((count, width), jnp.bfloat16),
            tiled,
            tiled,
            tiled,
            tiled,
            shaped((2, tiles, blocks, LANES)),
        ),
        [pltpu.VMEM((BLOCK + 8, LANES), jnp.float32)],
        "lru_forward",
    )
    branch_pre = project(normed_one, branch_w, "branch_pre")
    summaries = spread_z(summary)
    summaries, branch_pre, top_even = barrier((summaries, branch_pre, top_even))
    state, gated, enter = whole(
        lru_state_kernel,
        (position,),
        (summaries, keep, drive, branch_pre),
        (
            tiled,
            shaped((count, width), jnp.bfloat16),
            shaped((tiles, blocks, LANES)),
        ),
        [pltpu.VMEM((tiles, every, LANES), jnp.float32)],
        "lru_state",
    )
    resid_in = as_wide(tokens)
    mid_parts, mid_last = scatter_plane(slot_product((gated,), lambda rows: mm(rows, out_w)))
    top_even, mid_last = barrier((top_even, mid_last))
    (top_low,) = stack(plane_all(top_even), "stack_top")
    mid_parts, top_low, gate_w = barrier((mid_parts, top_low, gate_w))
    resid_mid = resid_in + summed(mid_parts)
    scale_two = lax.rsqrt(jnp.mean(resid_mid * resid_mid, axis=-1, keepdims=True) + NORM_EPSILON)
    own_two = as_low(resid_mid * scale_two * gain_two)
    two_first = plane_first(own_two)
    two_first, up_w = barrier((two_first, up_w))
    normed_two, gate_pre, up_pre, hidden = stack(
        plane_all(plane_second(own_two, two_first)), "ff_forward", None, (gate_w, up_w), True
    )
    d_gate, d_up = ff_backward(top_low, down_w, gate_pre, up_pre)
    two_parts, two_last = scatter_plane(
        slot_product((d_gate, d_up), lambda one, two: mm_nt(one, gate_w) + mm_nt(two, up_w))
    )
    late_gate, late_up, late_hidden, two_last = barrier((d_gate, d_up, hidden, two_last))
    grad_down = mm_tn(late_hidden, top_low, jnp.bfloat16)
    grad_down, late_gate, late_up = barrier((grad_down, late_gate, late_up))
    grad_gate = mm_tn(normed_two, late_gate, jnp.bfloat16)
    grad_up = mm_tn(normed_two, late_up, jnp.bfloat16)

    def home_rows(value):
        return lax.psum_scatter(value, "fsdp", scatter_dimension=0, tiled=True)

    def by_owner(values):
        parts = [value.reshape(seq_size, z_size, chunk, value.shape[-1]) for value in values]
        return jnp.transpose(jnp.stack(parts, axis=0), (2, 1, 0, 3, 4))

    def own_columns(got):
        return as_wide(jnp.swapaxes(got, 0, 1).reshape(chunk, -1))

    down_home = home_rows(grad_down)
    ff_pair = by_owner((grad_gate, grad_up)).reshape(z_size * seq_size * 2 * chunk, ffw)
    two_parts, ff_pair = barrier((two_parts, ff_pair))
    grad_normed_two = summed(two_parts)
    ff_home = home_rows(ff_pair)

    def gain_home(gain, pairs):
        total = sum(jnp.sum(grad * as_wide(as_low(weight)), axis=1) for grad, weight in pairs)
        return total / as_wide(as_low(gain))

    scaled_two = gain_two * grad_normed_two
    grad_mid = (
        live_col * as_wide(cotangent)
        + scale_two * scaled_two
        - resid_mid
        * scale_two
        * scale_two
        * scale_two
        * jnp.mean(scaled_two * resid_mid, axis=-1, keepdims=True)
    )
    grad_low = as_low(grad_mid)
    grad_low, late_hidden = barrier((grad_low, hidden))
    out_first = plane_first(grad_low)
    half = count // 2
    mlp_odd = swap(mm(late_hidden[half:], down_w, jnp.bfloat16), "seq", 1)
    mlp_pair = split_pairs(mm(late_hidden[:half], down_w) + as_wide(mlp_odd))
    out_first, mlp_pair, down_home = barrier((out_first, mlp_pair, down_home))
    out_pieces = plane_all(plane_second(grad_low, out_first))
    out_pieces, mlp_pair = barrier((out_pieces, mlp_pair))
    mlp_parts = scatter_pairs(mlp_pair)
    grad_out_low, d_branch, direct, send = lru_back(out_pieces, out_w, state, branch_pre, keep)
    backs = spread_z(send)
    grad_out = mm_tn(gated, grad_out_low, jnp.bfloat16)
    backs, grad_out = barrier((backs, grad_out))
    d_rec, d_in, du_part, du_last, heads, totals = whole(
        lru_grad_kernel,
        (live_count, first, pred, position),
        (
            summaries,
            backs,
            direct,
            keep,
            drive,
            rate,
            entry,
            state,
            enter,
            conv_low,
            u_value,
            tails,
            vectors,
            rec_w,
            in_w,
        ),
        (
            shaped((count, width), jnp.bfloat16),
            shaped((count, width), jnp.bfloat16),
            shaped((count, width), jnp.bfloat16),
            shaped((blocks, 8, width)),
            shaped((blocks, 8, width)),
            shaped((8, width)),
        ),
        [
            pltpu.VMEM((tiles, every, LANES), jnp.float32),
            pltpu.VMEM((tiles, count, LANES), jnp.float32),
            pltpu.VMEM((BLOCK + 16, LANES), jnp.float32),
            pltpu.VMEM((8, 8, width), jnp.float32),
            pltpu.VMEM((BLOCK, width), jnp.float32),
        ],
        "lru_grad",
    )
    du_part, heads, totals, d_rec, d_in, ff_home, mlp_parts, d_branch = barrier(
        (du_part, heads, totals, d_rec, d_in, ff_home, mlp_parts, d_branch)
    )
    grad_out, ff_home = barrier((grad_out, ff_home))
    out_home = home_rows(grad_out)
    grad_branch = mm_tn(normed_one, d_branch, jnp.bfloat16)
    ff_got = exchange(ff_home.reshape(seq_size, 2, chunk, ffw))
    heads = edges(heads[:, 9 - TAPS :])
    full_rec, full_in = mm_tn(conv_low, d_rec), mm_tn(conv_low, d_in)
    du_part = du_part.reshape(blocks, BLOCK, width)
    (patch,) = whole(
        head_kernel,
        (succ,),
        (du_part[:, BLOCK - 16 :], du_last, heads),
        (shaped((blocks, 16, width), jnp.bfloat16),),
        [],
        "lru_heads",
    )
    d_input = lax.dynamic_update_slice(du_part, patch, (0, BLOCK - 16, 0)).reshape(count, width)
    branch_pack = by_owner((grad_branch,)).reshape(z_size * seq_size * chunk, width)
    d_input, full_rec, full_in, ff_got, branch_pack, out_home = barrier(
        (d_input, full_rec, full_in, ff_got, branch_pack, out_home)
    )
    branch_home = home_rows(branch_pack)
    grad_input = mm_tn(normed_one, d_input, jnp.bfloat16)
    grad_gate_home, grad_up_home = own_columns(ff_got[:, 0]), own_columns(ff_got[:, 1])
    late_input, grad_input = barrier((d_input, grad_input))
    grad_gain_two = gain_home(norm_gain2, ((grad_gate_home, w_gate), (grad_up_home, w_up)))
    one_parts, one_last = scatter_plane(
        slot_product(
            (d_branch, late_input), lambda one, two: mm_nt(one, branch_w) + mm_nt(two, input_w)
        )
    )
    one_last, mlp_parts = barrier((one_last, mlp_parts))
    mixed = as_low(live_col * (resid_mid + summed(mlp_parts)))
    grad_normed_one = summed(one_parts)
    scaled_one = gain_one * grad_normed_one
    scale_one = lax.rsqrt(jnp.mean(resid_in * resid_in, axis=-1, keepdims=True) + NORM_EPSILON)
    tokens_grad = as_low(
        grad_mid
        + scale_one * scaled_one
        - resid_in
        * scale_one
        * scale_one
        * scale_one
        * jnp.mean(scaled_one * resid_in, axis=-1, keepdims=True)
    )

    def blocks_of(full, start):
        place = start + jnp.arange(width)[:, None] % gate_width
        fold = (place == jnp.arange(2 * gate_width)[None, :]).astype(jnp.float32)
        full = jnp.where(same, full, 0.0)
        return jnp.dot(full, fold, precision=lax.Precision.HIGHEST)

    totals = jnp.concatenate(
        [totals[:7], totals[7:] * (GATE_SCALE * jax.nn.sigmoid(-decay))[None]], axis=0
    )
    gates = blocks_of(full_rec, 0) + blocks_of(full_in, gate_width)
    owned = width // z_size
    gates = as_low(gates).reshape(z_size, owned, 2 * gate_width)
    totals = jnp.swapaxes(jnp.pad(totals, ((0, 8), (0, 0))).reshape(16, z_size, owned), 0, 1)
    totals = as_low(totals)
    lanes = max(width, 2 * gate_width)
    edge = seq_size * chunk
    pack = jnp.concatenate(
        [
            jnp.pad(part, ((0, 0), (0, 0), (0, lanes - part.shape[-1])))
            for part in (
                by_owner((grad_input,)).reshape(z_size, edge, width),
                gates,
                totals,
            )
        ],
        axis=1,
    )
    pack, branch_home = barrier((pack.reshape(z_size * pack.shape[1], lanes), branch_home))
    pack = home_rows(pack)
    grad_branch_home = own_columns(exchange(branch_home.reshape(seq_size, chunk, width)))
    grad_input_home = own_columns(exchange(pack[:edge, :width].reshape(seq_size, chunk, width)))
    grad_gain_one = gain_home(
        norm_gain1, ((grad_branch_home, w_branch), (grad_input_home, w_input))
    )
    gates = as_wide(pack[edge : edge + owned])
    totals = as_wide(pack[edge + owned :, :owned])
    return (
        mixed,
        tokens_grad,
        grad_gain_one,
        grad_branch_home,
        grad_input_home,
        totals[:TAPS],
        totals[4],
        gates[:, :gate_width],
        totals[5],
        gates[:, gate_width : 2 * gate_width],
        totals[6],
        totals[7],
        as_wide(out_home),
        grad_gain_two,
        grad_gate_home,
        grad_up_home,
        as_wide(down_home),
    )


def solution(mesh):
    row = P(("seq", "fsdp"))
    rows = P(("seq", "fsdp"), None)
    columns = P(None, ("seq", "fsdp"))
    return jax.shard_map(
        shards,
        mesh=mesh,
        in_specs=(
            rows,
            rows,
            P(),
            P(),
            P(),
            row,
            rows,
            rows,
            columns,
            row,
            rows,
            row,
            rows,
            row,
            row,
            rows,
            row,
            rows,
            rows,
            rows,
        ),
        out_specs=(
            rows,
            rows,
            row,
            rows,
            rows,
            columns,
            row,
            rows,
            row,
            rows,
            row,
            row,
            rows,
            row,
            rows,
            rows,
            rows,
        ),
        check_vma=False,
    )
```

```python
import jax
import jax.numpy as jnp
from jax import lax
from jax.experimental import pallas as pl
from jax.experimental.pallas import tpu as pltpu
from jax.sharding import PartitionSpec as P

BLOCK = 128
LANES = 128
TAPS = 4
UNROLL = 8
NORM_EPSILON = 1e-06
GATE_SCALE = 8.0
VMEM_LIMIT = 48 * 1024 * 1024
GELU_C = 0.7978845608028654
GELU_A = 0.044715
LIGHT = pl.CostEstimate(flops=1, transcendentals=0, bytes_accessed=1)


def as_low(values):
    return values.astype(jnp.bfloat16)


def as_wide(values):
    return values.astype(jnp.float32)


def mm(left, right, out=jnp.float32):
    return jnp.dot(left, right, preferred_element_type=jnp.float32).astype(out)


def mm_tn(left, right, out=jnp.float32):
    return lax.dot_general(
        left, right, (((0,), (0,)), ((), ())), preferred_element_type=jnp.float32
    ).astype(out)


def mm_nt(left, right, out=jnp.float32):
    return lax.dot_general(
        left, right, (((1,), (1,)), ((), ())), preferred_element_type=jnp.float32
    ).astype(out)


def swap(values, axis, flip):
    count = lax.axis_size(axis)
    return lax.ppermute(values, axis, [(i, i ^ flip) for i in range(count)])


barrier = lax.optimization_barrier


def plane_even(own):
    return [own] + [swap(own, "seq", k) for k in range(2, lax.axis_size("seq"), 2)]


def plane_first(own):
    count = lax.axis_size("seq")
    flips = (2, 4) if count == 8 else range(2, count, 2)
    return [swap(own, "seq", k) for k in flips]


def plane_second(own, first):
    even = [own, *first]
    if lax.axis_size("seq") == 8:
        half = own.shape[0] // 2
        near, side = first
        even.append((swap(side[:half], "seq", 2), swap(near[half:], "seq", 4)))
    return even


def plane_all(even):
    return list(even) + [jax.tree.map(lambda part: swap(part, "seq", 1), piece) for piece in even]


def slot_order():
    evens = lax.axis_size("seq") // 2
    return sorted(range(1, evens), key=lambda slot: -bin(slot).count("1")) + [0]


def scatter_plane(product):
    evens = lax.axis_size("seq") // 2
    order = slot_order()
    ready, pairs, after = {}, {}, None

    def odd(slot):
        value = as_low(product(evens + slot, after))
        ready[slot] = swap(value, "seq", 1)
        return value

    after = odd(order[0])
    for index, slot in enumerate(order[:-1]):
        after = odd(order[index + 1])
        after = product(slot, after) + as_wide(ready[slot])
        pairs[slot] = after
    if evens != 4:
        moved = [swap(as_low(pairs[slot]), "seq", 2 * slot) for slot in order[:-1]]
        return moved + [product(0, after) + as_wide(ready[0])], moved[0]
    near, side, far = (pairs[slot] for slot in (1, 2, 3))
    half = far.shape[0] // 2
    by_near = swap(as_low(jnp.concatenate([far[:half], near[:half]])), "seq", 2)
    by_side = swap(as_low(jnp.concatenate([far[half:], side[half:]])), "seq", 4)
    own = product(0, after) + as_wide(ready[0])
    by_near, by_side, last = barrier((by_near, by_side, own))
    near_low = swap(as_low(near[half:] + as_wide(by_side[:half])), "seq", 2)
    side_top = swap(as_low(side[:half] + as_wide(by_near[:half])), "seq", 4)
    return [last, (by_near[half:], near_low), (side_top, by_side[half:])], own


def split_pairs(pair):
    rows = pair.shape[0] // (lax.axis_size("seq") // 2)
    parts = [pair[slot * rows : (slot + 1) * rows] for slot in slot_order()]
    return [as_low(part) for part in parts[:-1]] + parts[-1:]


def scatter_pairs(parts):
    return [
        swap(part, "seq", 2 * slot) if slot else part for slot, part in zip(slot_order(), parts)
    ]


def slot_product(operands, multiply):
    rows = operands[0].shape[0] // lax.axis_size("seq")

    def product(slot, after):
        parts = tuple(operand[slot * rows : (slot + 1) * rows] for operand in operands)
        if after is not None:
            parts = barrier((*parts, after))[:-1]
        return multiply(*parts)

    return product


def summed(parts):
    total = None
    for part in parts:
        if isinstance(part, (tuple, list)):
            part = jnp.concatenate(part, axis=0)
        total = as_wide(part) if total is None else total + as_wide(part)
    return total


def gather_small(value, axis):
    value = value[None]
    bit = 1
    while bit < lax.axis_size(axis):
        other = swap(value, axis, bit)
        upper = (lax.axis_index(axis) // bit) % 2 == 1
        value = jnp.where(
            upper, jnp.concatenate([other, value]), jnp.concatenate([value, other])
        )
        bit *= 2
    return value


def spread_z(value):
    count = lax.axis_size("fsdp")
    return jnp.stack([value] + [swap(value, "fsdp", j) for j in range(1, count)], axis=0)


def gelu_parts(values):
    inner = GELU_C * (values + GELU_A * values * values * values)
    bend = jnp.tanh(inner)
    return (0.5 * values * (1.0 + bend), bend)


def gelu_slope(values, bend):
    return 0.5 * (1.0 + bend) + 0.5 * values * (1.0 - bend * bend) * GELU_C * (
        1.0 + 3.0 * GELU_A * values * values
    )


def expm1_small(values):
    series = values * (1.0 / 120.0) + 1.0 / 24.0
    for scale in (1.0 / 6.0, 0.5, 1.0):
        series = series * values + scale
    return series * values


def block_rows(index):
    return pl.ds(pl.multiple_of(index * BLOCK, BLOCK), BLOCK)


def lane_tiles(width):
    return [(low, min(LANES, width - low)) for low in range(0, width, LANES)]


def piece_specs(pieces, steps):
    specs = []
    chunk = pieces[0].shape[0] // steps
    block = (chunk, pieces[0].shape[1])
    last = steps // 2 - 1
    for piece in pieces:
        if isinstance(piece, (tuple, list)):
            specs.append(pl.BlockSpec(block, lambda i: (jnp.minimum(i, last), 0)))
            specs.append(pl.BlockSpec(block, lambda i: (jnp.maximum(i - last - 1, 0), 0)))
        else:
            specs.append(pl.BlockSpec(block, lambda i: (i, 0)))
    return specs


def piece_halves(pieces):
    return [len(piece) if isinstance(piece, (tuple, list)) else 1 for piece in pieces]


def joined_rows(refs, halves):
    upper = pl.program_id(0) < pl.num_programs(0) // 2
    rows, at = [], 0
    for parts in halves:
        value = refs[at][...]
        rows.append(value if parts == 1 else jnp.where(upper, value, refs[at + 1][...]))
        at += parts
    return jnp.concatenate(rows, axis=0)


def stack(pieces, name, gain=None, weights=(), gated=False, steps=8):
    count = len(pieces)
    halves, flat = piece_halves(pieces), jax.tree.leaves(pieces)
    rows, model = pieces[0].shape
    chunk = rows // steps
    extra = ([gain] if gain is not None else []) + list(weights)

    def kernel(*refs):
        values = joined_rows(refs[: len(flat)], halves)
        refs = refs[len(flat) :]
        if gain is not None:
            gain_ref, refs = refs[0], refs[1:]
            wide = values.astype(jnp.float32)
            scale = lax.rsqrt(jnp.mean(wide * wide, axis=-1, keepdims=True) + NORM_EPSILON)
            values = (wide * scale * gain_ref[...]).astype(jnp.bfloat16)
        weight_refs, refs = refs[: len(weights)], refs[len(weights) :]
        refs[0][...] = values.reshape(count, chunk, model)
        products = []
        for weight_ref, out_ref in zip(weight_refs, refs[1:]):
            out = jnp.dot(values, weight_ref[...], preferred_element_type=jnp.float32)
            products.append(out)
            if not gated:
                out_ref[...] = out.reshape(count, chunk, out.shape[1])
        if gated:
            act, bend = gelu_parts(products[0])
            for out_ref, out in zip(
                refs[1:], (act, products[1] * gelu_slope(products[0], bend), act * products[1])
            ):
                out_ref[...] = out.reshape(count, chunk, out.shape[1]).astype(out_ref.dtype)

    widths = [weight.shape[1] for weight in weights]
    outs = [shaped((count, rows, model), jnp.bfloat16)] + [shaped((count, rows, w)) for w in widths]
    if gated:
        outs.append(shaped((count, rows, widths[0]), jnp.bfloat16))
    done = pl.pallas_call(
        kernel,
        grid=(steps,),
        in_specs=piece_specs(pieces, steps) + [pl.BlockSpec(e.shape, lambda i: (0, 0)) for e in extra],
        out_specs=[pl.BlockSpec((count, chunk, o.shape[2]), lambda i: (0, i, 0)) for o in outs],
        out_shape=outs,
        compiler_params=pltpu.CompilerParams(vmem_limit_bytes=VMEM_LIMIT),
        cost_estimate=LIGHT,
        name=name,
    )(*flat, *extra)
    return [out.reshape(count * rows, out.shape[2]) for out in done]


def ff_backward(top, down_w, act, bend, steps=8):
    chunk = top.shape[0] // steps
    ffw, model = down_w.shape

    def kernel(top_ref, down_ref, act_ref, bend_ref, d_gate_ref, d_up_ref):
        grad = lax.dot_general(
            top_ref[...], down_ref[...], (((1,), (1,)), ((), ())), preferred_element_type=jnp.float32
        )
        d_gate_ref[...] = (grad * bend_ref[...]).astype(jnp.bfloat16)
        d_up_ref[...] = (grad * act_ref[...]).astype(jnp.bfloat16)

    block = pl.BlockSpec((chunk, ffw), lambda i: (i, 0))
    return pl.pallas_call(
        kernel,
        grid=(steps,),
        in_specs=[
            pl.BlockSpec((chunk, model), lambda i: (i, 0)),
            pl.BlockSpec((ffw, model), lambda i: (0, 0)),
            block,
            block,
        ],
        out_specs=[block, block],
        out_shape=[shaped((top.shape[0], ffw), jnp.bfloat16)] * 2,
        compiler_params=pltpu.CompilerParams(vmem_limit_bytes=VMEM_LIMIT),
        cost_estimate=LIGHT,
        name="ff_backward",
    )(top, down_w, act, bend)


def project(rows, weight, name, steps=8):
    chunk = rows.shape[0] // steps
    width = weight.shape[1]

    def kernel(rows_ref, weight_ref, out_ref):
        out_ref[...] = jnp.dot(rows_ref[...], weight_ref[...], preferred_element_type=jnp.float32)

    return pl.pallas_call(
        kernel,
        grid=(steps,),
        in_specs=[
            pl.BlockSpec((chunk, rows.shape[1]), lambda i: (i, 0)),
            pl.BlockSpec(weight.shape, lambda i: (0, 0)),
        ],
        out_specs=pl.BlockSpec((chunk, width), lambda i: (i, 0)),
        out_shape=shaped((rows.shape[0], width)),
        compiler_params=pltpu.CompilerParams(vmem_limit_bytes=VMEM_LIMIT),
        cost_estimate=pl.CostEstimate(
            flops=2 * rows.size * width,
            transcendentals=0,
            bytes_accessed=2 * rows.size + 4 * rows.shape[0] * width,
        ),
        name=name,
    )(rows, weight)


def dead_mask(rows, live_count):
    return (rows < live_count).astype(jnp.float32)


def lru_forward_kernel(
    live_ref,
    first_ref,
    pred_ref,
    u_ref,
    tail_ref,
    vec_ref,
    rec_ref,
    in_ref,
    xc_ref,
    keep_ref,
    drive_ref,
    rate_ref,
    slope_ref,
    into_ref,
    bent_ref,
    sum_ref,
    ext_ref,
):
    blocks = u_ref.shape[0] // BLOCK
    tiles = lane_tiles(u_ref.shape[1])
    rows = lax.broadcasted_iota(jnp.int32, (BLOCK, LANES), 0)

    def block(index, carry):
        at = block_rows(index)
        first = first_ref[index]
        pred = pred_ref[index]
        live = dead_mask(rows, live_ref[index])
        before = jnp.maximum(pred, 0)
        joined = jnp.where((pred >= 0) & (first == 0), 1.0, 0.0)
        for low, size in tiles:
            lanes = slice(low, low + size)
            u_value = u_ref[at, lanes]
            ext_ref[0:8, :size] = tail_ref[before, :, lanes] * joined
            ext_ref[8 : 8 + BLOCK, :size] = u_value
            later = vec_ref[1:2, lanes] * ext_ref[7 : 7 + BLOCK, :size]
            for tap in range(2, TAPS):
                later = later + vec_ref[tap : tap + 1, lanes] * ext_ref[8 - tap : 8 - tap + BLOCK, :size]
            conv = vec_ref[4:5, lanes] + vec_ref[0:1, lanes] * u_value + later * live[:, :size]
            xc_ref[at, lanes] = conv.astype(jnp.bfloat16)
        low_rows = xc_ref[at, :]
        pre_rec = jnp.dot(low_rows, rec_ref[...], preferred_element_type=jnp.float32)
        pre_in = jnp.dot(low_rows, in_ref[...], preferred_element_type=jnp.float32)
        for tile, (low, size) in enumerate(tiles):
            lanes = slice(low, low + size)
            rate = jax.nn.sigmoid(pre_rec[:, lanes] + vec_ref[5:6, lanes])
            entry = jax.nn.sigmoid(pre_in[:, lanes] + vec_ref[6:7, lanes])
            minus = expm1_small(rate * vec_ref[7:8, lanes])
            twice = minus * (2.0 + minus)
            into = jnp.sqrt(-twice) * entry
            drive = into * low_rows[:, lanes].astype(jnp.float32)
            rate_ref[tile, at, :size] = rate
            keep_ref[tile, at, :size] = (1.0 + minus) * live[:, :size]
            drive_ref[tile, at, :size] = drive
            slope_ref[tile, at, :size] = drive + drive / twice
            into_ref[tile, at, :size] = into
            bent_ref[tile, at, :size] = drive * (1.0 - entry)

        @pl.when(first > 0)
        def _():
            top = pl.ds(pl.multiple_of(index * BLOCK, BLOCK), 8)
            after = (rows[:8] > 0).astype(jnp.float32)
            for tile in range(len(tiles)):
                keep_ref[tile, top, :] = keep_ref[tile, top, :] * after

        return carry

    lax.fori_loop(0, blocks, block, 0)

    def step(place, carry):
        at = pl.ds(place, blocks, stride=BLOCK)
        after = []
        for tile, (total, state) in enumerate(carry):
            keep = keep_ref[tile, at, :]
            after.append((total * keep, keep * state + drive_ref[tile, at, :]))
        return tuple(after)

    ones = jnp.ones((blocks, LANES), jnp.float32)
    start = tuple((ones, jnp.zeros_like(ones)) for _ in tiles)
    ends = lax.fori_loop(0, BLOCK, step, start, unroll=UNROLL)
    for tile, (total, state) in enumerate(ends):
        sum_ref[0, tile] = total
        sum_ref[1, tile] = state


def lru_state_kernel(
    pos_ref,
    all_ref,
    keep_ref,
    drive_ref,
    rate_ref,
    slope_ref,
    ypre_ref,
    vec_ref,
    hy_ref,
    act_ref,
    bend_ref,
    slow_ref,
    rec_ref,
    line_ref,
    h_ref,
    ext_ref,
):
    tiles = lane_tiles(ypre_ref.shape[1])
    turns, _, _, blocks, _ = all_ref.shape

    def chain(place, states):
        slot = pos_ref[place]
        turn, index = slot // blocks, slot % blocks
        after = []
        for tile, state in enumerate(states):
            line_ref[tile, pl.ds(slot, 1), :] = state
            keep = all_ref[turn, 0, tile, pl.ds(index, 1), :]
            after.append(keep * state + all_ref[turn, 1, tile, pl.ds(index, 1), :])
        return tuple(after)

    zero = jnp.zeros((1, LANES), jnp.float32)
    lax.fori_loop(0, turns * blocks, chain, tuple(zero for _ in tiles))
    def step(place, states):
        at = pl.ds(place, blocks, stride=BLOCK)
        after = []
        for tile, state in enumerate(states):
            state = keep_ref[tile, at, :] * state + drive_ref[tile, at, :]
            h_ref[tile, at, :] = state
            after.append(state)
        return tuple(after)

    start = tuple(line_ref[tile, 0:blocks, :] for tile in range(len(tiles)))
    lax.fori_loop(0, BLOCK, step, start, unroll=UNROLL)

    def block(index, carry):
        at = block_rows(index)
        for tile, (low, size) in enumerate(tiles):
            lanes = slice(low, low + size)
            h_value = h_ref[tile, at, :size]
            value = ypre_ref[at, lanes]
            act, bend = gelu_parts(value)
            hy_ref[at, lanes] = (h_value * act).astype(jnp.bfloat16)
            act_ref[tile, at, :size] = act
            bend_ref[tile, at, :size] = h_value * gelu_slope(value, bend)
            ext_ref[7:8, :size] = line_ref[tile, pl.ds(index, 1), :size]
            ext_ref[8 : 8 + BLOCK, :size] = h_value
            rate = rate_ref[tile, at, :size]
            slow = rate * (
                keep_ref[tile, at, :size] * ext_ref[7 : 7 + BLOCK, :size]
                + slope_ref[tile, at, :size]
            )
            slow_ref[tile, at, :size] = slow
            rec_ref[tile, at, :size] = slow * (1.0 - rate) * vec_ref[7:8, lanes]
        return carry

    lax.fori_loop(0, blocks, block, 0)


def lru_back(pieces, out_w, act, bend, keep, steps=8):
    count = len(pieces)
    halves, flat = piece_halves(pieces), jax.tree.leaves(pieces)
    rows, model = pieces[0].shape
    width = out_w.shape[0]
    tiles = lane_tiles(width)
    chunk = rows // steps
    blocks = count * rows // BLOCK

    def kernel(*refs):
        values = joined_rows(refs[: len(flat)], halves)
        w_ref, act_ref, bend_ref, keep_ref, out_ref, dy_ref, dh_ref, send_ref = refs[len(flat) :]
        here = pl.program_id(0)
        out_ref[...] = values.reshape(count, chunk, model)
        grads = lax.dot_general(
            values, w_ref[...], (((1,), (1,)), ((), ())), preferred_element_type=jnp.float32
        )
        for slot in range(count):
            span = pl.ds(pl.multiple_of(slot * rows + here * chunk, chunk), chunk)
            for tile, (low, size) in enumerate(tiles):
                lanes = slice(low, low + size)
                grad = grads[slot * chunk : (slot + 1) * chunk, lanes]
                dy_ref[slot, :, lanes] = (grad * bend_ref[tile, slot, :, :size]).astype(jnp.bfloat16)
                dh_ref[tile, span, :size] = grad * act_ref[tile, slot, :, :size]

        @pl.when(here == steps - 1)
        def _():
            def step(turn, carry):
                at = pl.ds(BLOCK - 1 - turn, blocks, stride=BLOCK)
                return tuple(
                    keep_ref[tile, at, :] * (dh_ref[tile, at, :] + value)
                    for tile, value in enumerate(carry)
                )

            zero = jnp.zeros((blocks, LANES), jnp.float32)
            ends = lax.fori_loop(0, BLOCK, step, tuple(zero for _ in tiles), unroll=UNROLL)
            for tile, value in enumerate(ends):
                send_ref[tile] = value

    depth = len(tiles)
    total = count * rows
    out, dy, dh, send = pl.pallas_call(
        kernel,
        grid=(steps,),
        in_specs=piece_specs(pieces, steps)
        + [
            pl.BlockSpec((width, model), lambda i: (0, 0)),
            pl.BlockSpec((depth, count, chunk, LANES), lambda i: (0, 0, i, 0)),
            pl.BlockSpec((depth, count, chunk, LANES), lambda i: (0, 0, i, 0)),
            pl.BlockSpec((depth, total, LANES), lambda i: (0, 0, 0)),
        ],
        out_specs=[
            pl.BlockSpec((count, chunk, model), lambda i: (0, i, 0)),
            pl.BlockSpec((count, chunk, width), lambda i: (0, i, 0)),
            pl.BlockSpec((depth, total, LANES), lambda i: (0, 0, 0)),
            pl.BlockSpec((depth, blocks, LANES), lambda i: (0, 0, 0)),
        ],
        out_shape=[
            shaped((count, rows, model), jnp.bfloat16),
            shaped((count, rows, width), jnp.bfloat16),
            shaped((depth, total, LANES)),
            shaped((depth, blocks, LANES)),
        ],
        compiler_params=pltpu.CompilerParams(vmem_limit_bytes=VMEM_LIMIT),
        cost_estimate=LIGHT,
        name="lru_back",
    )(
        *flat,
        out_w,
        act.reshape(depth, count, rows, LANES),
        bend.reshape(depth, count, rows, LANES),
        keep,
    )
    return out.reshape(total, model), dy.reshape(total, width), dh, send


def fold_rows(values):
    return values.reshape(BLOCK // 8, 8, values.shape[1]).sum(axis=0)


def lru_grad_kernel(
    live_ref,
    first_ref,
    pred_ref,
    pos_ref,
    all_ref,
    back_ref,
    dh_ref,
    keep_ref,
    slow_ref,
    bent_rec_ref,
    into_ref,
    bent_in_ref,
    u_ref,
    tail_ref,
    vec_ref,
    rec_ref,
    in_ref,
    drec_ref,
    din_ref,
    du_ref,
    last_ref,
    head_ref,
    total_ref,
    line_ref,
    g_ref,
    ext_ref,
    acc_ref,
    direct_ref,
):
    blocks = u_ref.shape[0] // BLOCK
    width = u_ref.shape[1]
    tiles = lane_tiles(width)
    every = back_ref.shape[0] * blocks
    rows = lax.broadcasted_iota(jnp.int32, (BLOCK, LANES), 0)

    def chain(count, carry):
        slot = pos_ref[every - 1 - count]
        turn, index = slot // blocks, slot % blocks
        after = []
        for tile, value in enumerate(carry):
            line_ref[tile, pl.ds(slot, 1), :] = value
            keep = all_ref[turn, 0, tile, pl.ds(index, 1), :]
            after.append(keep * value + back_ref[turn, tile, pl.ds(index, 1), :])
        return tuple(after)

    zero = jnp.zeros((1, LANES), jnp.float32)
    lax.fori_loop(0, every, chain, tuple(zero for _ in tiles))

    def step(turn, carry):
        at = pl.ds(BLOCK - 1 - turn, blocks, stride=BLOCK)
        after = []
        for tile, value in enumerate(carry):
            grad = dh_ref[tile, at, :] + value
            g_ref[tile, at, :] = grad
            after.append(keep_ref[tile, at, :] * grad)
        return tuple(after)

    start = tuple(line_ref[tile, 0:blocks, :] for tile in range(len(tiles)))
    lax.fori_loop(0, BLOCK, step, start, unroll=UNROLL)
    acc_ref[...] = jnp.zeros_like(acc_ref)
    contract = (((1,), (1,)), ((), ()))

    def block(index, carry):
        at = block_rows(index)
        first = first_ref[index]
        pred = pred_ref[index]
        live = dead_mask(rows, live_ref[index])
        before = jnp.maximum(pred, 0)
        joined = jnp.where((pred >= 0) & (first == 0), 1.0, 0.0)
        for tile, (low, size) in enumerate(tiles):
            lanes = slice(low, low + size)
            grad = g_ref[tile, at, :size]
            acc_ref[7, :, lanes] += fold_rows(grad * slow_ref[tile, at, :size])
            d_rec = (grad * bent_rec_ref[tile, at, :size]).astype(jnp.bfloat16)
            d_in = (grad * bent_in_ref[tile, at, :size]).astype(jnp.bfloat16)
            drec_ref[at, lanes] = d_rec
            din_ref[at, lanes] = d_in
            acc_ref[5, :, lanes] += fold_rows(d_rec.astype(jnp.float32))
            acc_ref[6, :, lanes] += fold_rows(d_in.astype(jnp.float32))
            direct_ref[:, lanes] = grad * into_ref[tile, at, :size]
        direct_ref[...] += lax.dot_general(
            drec_ref[at, :], rec_ref[...], contract, preferred_element_type=jnp.float32
        ) + lax.dot_general(
            din_ref[at, :], in_ref[...], contract, preferred_element_type=jnp.float32
        )
        for low, size in tiles:
            lanes = slice(low, low + size)
            dxc = direct_ref[:, lanes]
            u_value = u_ref[at, lanes]
            ext_ref[0:8, :size] = tail_ref[before, :, lanes] * joined
            ext_ref[8 : 8 + BLOCK, :size] = u_value
            acc_ref[4, :, lanes] += fold_rows(dxc)
            acc_ref[0, :, lanes] += fold_rows(dxc * u_value)
            part = dxc * live[:, :size]
            for tap in range(1, TAPS):
                acc_ref[tap, :, lanes] += fold_rows(part * ext_ref[8 - tap : 8 - tap + BLOCK, :size])
            zero_tile = jnp.zeros((8, size), jnp.float32)
            ext_ref[0:8, :size] = zero_tile
            ext_ref[8 : 8 + BLOCK, :size] = part
            ext_ref[8 + BLOCK : 16 + BLOCK, :size] = zero_tile
            du_value = dxc * vec_ref[0:1, lanes]
            head = zero_tile
            for tap in range(1, TAPS):
                weight = vec_ref[tap : tap + 1, lanes]
                du_value = du_value + weight * ext_ref[8 + tap : 8 + tap + BLOCK, :size]
                head = head + weight * ext_ref[tap : tap + 8, :size]
            du_ref[at, lanes] = du_value.astype(jnp.bfloat16)
            last_ref[index, :, lanes] = du_value[BLOCK - 8 :]
            head_ref[index, :, lanes] = head * joined
        return carry

    lax.fori_loop(0, blocks, block, 0)
    for index in range(8):
        total_ref[index : index + 1, :] = jnp.sum(acc_ref[index], axis=0, keepdims=True)


def head_kernel(succ_ref, prev_ref, last_ref, head_ref, out_ref):
    blocks = last_ref.shape[0]

    def block(index, carry):
        succ = succ_ref[index]
        head = head_ref[jnp.maximum(succ, 0)]
        tail = last_ref[index] + jnp.where(succ >= 0, head, jnp.zeros_like(head))
        out_ref[index, :8, :] = prev_ref[index, :8, :]
        out_ref[index, 8:, :] = tail.astype(jnp.bfloat16)
        return carry

    lax.fori_loop(0, blocks, block, 0)


def shaped(shape, dtype=jnp.float32):
    return jax.ShapeDtypeStruct(shape, dtype)


def whole(kernel, scalars, arrays, outs, scratch, name):
    specs = [pl.BlockSpec(memory_space=pltpu.SMEM)] * len(scalars)
    specs += [pl.BlockSpec(memory_space=pltpu.VMEM)] * len(arrays)
    return pl.pallas_call(
        kernel,
        out_shape=outs,
        in_specs=specs,
        out_specs=[pl.BlockSpec(memory_space=pltpu.VMEM)] * len(outs),
        scratch_shapes=scratch,
        compiler_params=pltpu.CompilerParams(vmem_limit_bytes=VMEM_LIMIT),
        cost_estimate=LIGHT,
        name=name,
    )(*scalars, *arrays)


def shards(
    tokens,
    cotangent,
    lengths,
    offsets,
    deal,
    norm_gain1,
    w_branch,
    w_input,
    conv_kernel,
    conv_bias,
    gate_rec,
    bias_rec,
    gate_in,
    bias_in,
    decay_param,
    w_out,
    norm_gain2,
    w_gate,
    w_up,
    w_down,
):
    seq_size, z_size = lax.axis_size("seq"), lax.axis_size("fsdp")
    seq_at, z_at = lax.axis_index("seq"), lax.axis_index("fsdp")
    rows_here, model = tokens.shape
    blocks_here = rows_here // BLOCK
    blocks = seq_size * blocks_here
    every = blocks * z_size
    count = rows_here * seq_size
    width = w_branch.shape[1] // seq_size
    ffw = w_gate.shape[1] // seq_size
    chunk = w_branch.shape[0]
    gate_width = gate_rec.shape[1]
    groups = width // gate_width
    tiles = len(lane_tiles(width))
    tiled = shaped((tiles, count, LANES))

    order = jnp.array([k for k in range(seq_size) if k % 2 == 0] + [k for k in range(seq_size) if k % 2], jnp.int32)
    source = jnp.bitwise_xor(order, seq_at)
    flips = jnp.bitwise_xor(jnp.arange(z_size, dtype=jnp.int32), z_at)
    stored = (source[None, :, None] * z_size + flips[:, None, None]) * blocks_here
    stored = (stored + jnp.arange(blocks_here, dtype=jnp.int32)[None, None, :]).reshape(every)
    logical = deal[stored]
    places = jnp.arange(every, dtype=jnp.int32)
    at_place = logical[None, :] == places[:, None]
    position = jnp.sum(jnp.where(at_place, places[None, :], 0), axis=1)
    mine = logical[:blocks]

    def place_of(wanted):
        hit = logical[None, :] == wanted[:, None]
        return jnp.sum(jnp.where(hit, places[None, :] + 1, 0), axis=1) - 1

    pred = place_of(mine - 1)
    succ = place_of(mine + 1)
    left_over = lengths[None, :] - (mine[:, None] - offsets[None, :]) * BLOCK
    inside = (mine[:, None] >= offsets[None, :]) & (left_over > 0)
    live_count = jnp.max(jnp.where(inside, jnp.minimum(left_over, BLOCK), 0), axis=1)
    first = jnp.any(inside & (mine[:, None] == offsets[None, :]), axis=1).astype(jnp.int32)
    own_live = live_count[:blocks_here]
    live_col = (
        jnp.arange(BLOCK, dtype=jnp.int32)[None, :] < own_live[:, None]
    ).astype(jnp.float32).reshape(rows_here, 1)

    def columns(weight):
        return jnp.swapaxes(as_low(weight).reshape(chunk, seq_size, -1), 0, 1)

    def exchange(value):
        return lax.all_to_all(value, "seq", 0, 0, tiled=True)

    def gather_rows(value):
        return lax.all_gather(value, "fsdp", axis=0, tiled=True)

    def gather_columns(value):
        got = lax.all_gather(value, "fsdp", axis=0, tiled=False)
        return jnp.swapaxes(got, 0, 1).reshape(-1, value.shape[-1])

    gains = gather_small(as_low(jnp.stack([norm_gain1, norm_gain2])), "seq")
    mix = jnp.stack([columns(w_input), columns(w_branch)], axis=1)
    mix, own_tokens, gains = barrier((mix, tokens, gains))
    x_first = plane_first(own_tokens)
    out_w = gather_rows(as_low(w_out))
    mix = exchange(mix)
    params = [conv_kernel, conv_bias[None], bias_rec[None], bias_in[None], decay_param[None]]
    gains = jnp.pad(gains.reshape(2 * seq_size, chunk), ((0, 0), (0, width // z_size - chunk)))
    params = jnp.concatenate([as_low(part) for part in params] + [gains], axis=0).T
    small = jnp.concatenate([as_low(gate_rec), as_low(gate_in), params], axis=1)
    small = gather_small(small, "fsdp")
    mix, out_w, small, x_first = barrier((mix, out_w, small, x_first))
    x_even = plane_second(own_tokens, x_first)
    input_w = gather_columns(mix[:, 0])
    branch_w = gather_columns(mix[:, 1])
    x_pieces = plane_all(x_even)
    gains = small[:, :chunk, 2 * gate_width + 8 :].reshape(z_size, chunk, seq_size, 2)
    gains = as_wide(jnp.transpose(gains, (3, 2, 0, 1)).reshape(2, model))
    gain_one, gain_two = gains[:1], gains[1:]
    small = small.reshape(width, -1)

    same = jnp.arange(width)[:, None] // gate_width == jnp.arange(width)[None, :] // gate_width

    def diagonal(part):
        return jnp.where(same, jnp.tile(part, (1, groups)), jnp.zeros((), jnp.bfloat16))

    vectors = as_wide(small[:, 2 * gate_width : 2 * gate_width + 8]).T
    decay = vectors[7]
    vectors = jnp.concatenate([vectors[:7], -GATE_SCALE * jax.nn.softplus(-decay)[None]], axis=0)
    ff = jnp.stack([columns(w_gate), columns(w_up)], axis=1)
    top_own = as_low(live_col * as_wide(cotangent))
    x_pieces, ff, top_own = barrier((x_pieces, ff, top_own))
    ff = exchange(ff)
    x_pieces, top_own = barrier((x_pieces, top_own))
    top_even = plane_even(top_own)

    normed_one, u_value = stack(x_pieces, "norm_one", gain_one, (input_w,))
    u_value, gates_in = barrier((u_value, small))
    rec_w = diagonal(gates_in[:, :gate_width])
    in_w = diagonal(gates_in[:, gate_width : 2 * gate_width])
    down_w = gather_rows(as_low(w_down))

    def edges(rows):
        rows = spread_z(as_low(barrier(rows)).reshape(blocks * (TAPS - 1), width))
        rows = as_wide(rows).reshape(every, TAPS - 1, width)
        return jnp.pad(rows, ((0, 0), (9 - TAPS, 0), (0, 0)))

    tails = edges(u_value.reshape(blocks, BLOCK, width)[:, BLOCK - TAPS + 1 :])
    tails, rec_w, in_w, vectors, ff_gate, ff_up = barrier(
        (tails, rec_w, in_w, vectors, ff[:, 0], ff[:, 1])
    )
    gate_w = gather_columns(ff_gate)
    up_w = gather_columns(ff_up)
    conv_low, keep, drive, rate, slope, into, bent_in, summary = whole(
        lru_forward_kernel,
        (live_count, first, pred),
        (u_value, tails, vectors, rec_w, in_w),
        (
            shaped((count, width), jnp.bfloat16),
            *[tiled] * 6,
            shaped((2, tiles, blocks, LANES)),
        ),
        [pltpu.VMEM((BLOCK + 8, LANES), jnp.float32)],
        "lru_forward",
    )
    branch_pre = project(normed_one, branch_w, "branch_pre")
    summaries = spread_z(summary)
    summaries, branch_pre, top_even = barrier((summaries, branch_pre, top_even))
    gated, act, bend, slow, bent_rec = whole(
        lru_state_kernel,
        (position,),
        (summaries, keep, drive, rate, slope, branch_pre, vectors),
        (shaped((count, width), jnp.bfloat16), *[tiled] * 4),
        [
            pltpu.VMEM((tiles, every, LANES), jnp.float32),
            pltpu.VMEM((tiles, count, LANES), jnp.float32),
            pltpu.VMEM((BLOCK + 8, LANES), jnp.float32),
        ],
        "lru_state",
    )
    resid_in = as_wide(tokens)
    mid_parts, mid_last = scatter_plane(slot_product((gated,), lambda rows: mm(rows, out_w)))
    top_even, mid_last = barrier((top_even, mid_last))
    (top_low,) = stack(plane_all(top_even), "stack_top")
    mid_parts, top_low, gate_w = barrier((mid_parts, top_low, gate_w))
    resid_mid = resid_in + summed(mid_parts)
    scale_two = lax.rsqrt(jnp.mean(resid_mid * resid_mid, axis=-1, keepdims=True) + NORM_EPSILON)
    own_two = as_low(resid_mid * scale_two * gain_two)
    two_first = plane_first(own_two)
    two_first, up_w = barrier((two_first, up_w))
    normed_two, ff_act, ff_bend, hidden = stack(
        plane_all(plane_second(own_two, two_first)), "ff_forward", None, (gate_w, up_w), True
    )
    grad_down = mm_tn(hidden, top_low, jnp.bfloat16)
    ff_act, ff_bend, grad_down, down_w = barrier((ff_act, ff_bend, grad_down, down_w))
    d_gate, d_up = ff_backward(top_low, down_w, ff_act, ff_bend)
    two_parts, two_last = scatter_plane(
        slot_product((d_gate, d_up), lambda one, two: mm_nt(one, gate_w) + mm_nt(two, up_w))
    )
    down_home = lax.psum_scatter(grad_down, "fsdp", scatter_dimension=0, tiled=True)
    late_gate, late_up, late_hidden, two_last = barrier((d_gate, d_up, hidden, two_last))
    grad_gate = mm_tn(normed_two, late_gate, jnp.bfloat16)
    grad_up = mm_tn(normed_two, late_up, jnp.bfloat16)

    def home_rows(value):
        return lax.psum_scatter(value, "fsdp", scatter_dimension=0, tiled=True)

    def by_owner(values):
        parts = [value.reshape(seq_size, z_size, chunk, value.shape[-1]) for value in values]
        return jnp.transpose(jnp.stack(parts, axis=0), (2, 1, 0, 3, 4))

    def own_columns(got):
        return as_wide(jnp.swapaxes(got, 0, 1).reshape(chunk, -1))

    ff_pair = by_owner((grad_gate, grad_up)).reshape(z_size * seq_size * 2 * chunk, ffw)
    half = count // 2
    mlp_odd = swap(mm(late_hidden[half:], down_w, jnp.bfloat16), "seq", 1)
    mlp_pair = split_pairs(mm(late_hidden[:half], down_w) + as_wide(mlp_odd))
    two_parts, ff_pair, mlp_pair = barrier((two_parts, ff_pair, mlp_pair))
    grad_normed_two = summed(two_parts)
    ff_home = home_rows(ff_pair)

    def gain_home(gain, pairs):
        total = sum(jnp.sum(grad * as_wide(as_low(weight)), axis=1) for grad, weight in pairs)
        return total / as_wide(as_low(gain))

    scaled_two = gain_two * grad_normed_two
    grad_mid = (
        live_col * as_wide(cotangent)
        + scale_two * scaled_two
        - resid_mid
        * scale_two
        * scale_two
        * scale_two
        * jnp.mean(scaled_two * resid_mid, axis=-1, keepdims=True)
    )
    grad_low = as_low(grad_mid)
    out_first = plane_first(grad_low)
    out_first, down_home = barrier((out_first, down_home))
    out_pieces = plane_all(plane_second(grad_low, out_first))
    out_pieces, mlp_pair = barrier((out_pieces, mlp_pair))
    mlp_parts = scatter_pairs(mlp_pair)
    grad_out_low, d_branch, direct, send = lru_back(out_pieces, out_w, act, bend, keep)
    backs = spread_z(send)
    grad_out = mm_tn(gated, grad_out_low, jnp.bfloat16)
    backs, grad_out = barrier((backs, grad_out))
    d_rec, d_in, du_part, du_last, heads, totals = whole(
        lru_grad_kernel,
        (live_count, first, pred, position),
        (
            summaries,
            backs,
            direct,
            keep,
            slow,
            bent_rec,
            into,
            bent_in,
            u_value,
            tails,
            vectors,
            rec_w,
            in_w,
        ),
        (
            shaped((count, width), jnp.bfloat16),
            shaped((count, width), jnp.bfloat16),
            shaped((count, width), jnp.bfloat16),
            shaped((blocks, 8, width)),
            shaped((blocks, 8, width)),
            shaped((8, width)),
        ),
        [
            pltpu.VMEM((tiles, every, LANES), jnp.float32),
            pltpu.VMEM((tiles, count, LANES), jnp.float32),
            pltpu.VMEM((BLOCK + 16, LANES), jnp.float32),
            pltpu.VMEM((8, 8, width), jnp.float32),
            pltpu.VMEM((BLOCK, width), jnp.float32),
        ],
        "lru_grad",
    )
    du_part, heads, totals, d_rec, d_in, mlp_parts, d_branch, ff_home = barrier(
        (du_part, heads, totals, d_rec, d_in, mlp_parts, d_branch, ff_home)
    )
    grad_out, ff_home = barrier((grad_out, ff_home))
    out_home = home_rows(grad_out)
    grad_branch = mm_tn(normed_one, d_branch, jnp.bfloat16)
    heads = edges(heads[:, 9 - TAPS :])
    full_rec, full_in = mm_tn(conv_low, d_rec), mm_tn(conv_low, d_in)
    du_part = du_part.reshape(blocks, BLOCK, width)
    (patch,) = whole(
        head_kernel,
        (succ,),
        (du_part[:, BLOCK - 16 :], du_last, heads),
        (shaped((blocks, 16, width), jnp.bfloat16),),
        [],
        "lru_heads",
    )
    d_input = lax.dynamic_update_slice(du_part, patch, (0, BLOCK - 16, 0)).reshape(count, width)
    branch_pack = by_owner((grad_branch,)).reshape(z_size * seq_size * chunk, width)
    d_input, full_rec, full_in, branch_pack, ff_home, out_home = barrier(
        (d_input, full_rec, full_in, branch_pack, ff_home, out_home)
    )
    ff_got = exchange(ff_home.reshape(seq_size, 2, chunk, ffw))
    branch_home = home_rows(branch_pack)
    grad_input = mm_tn(normed_one, d_input, jnp.bfloat16)
    late_input, grad_input = barrier((d_input, grad_input))
    one_parts, one_last = scatter_plane(
        slot_product(
            (d_branch, late_input), lambda one, two: mm_nt(one, branch_w) + mm_nt(two, input_w)
        )
    )
    one_last, mlp_parts = barrier((one_last, mlp_parts))
    mixed = as_low(live_col * (resid_mid + summed(mlp_parts)))
    grad_normed_one = summed(one_parts)
    scaled_one = gain_one * grad_normed_one
    scale_one = lax.rsqrt(jnp.mean(resid_in * resid_in, axis=-1, keepdims=True) + NORM_EPSILON)
    tokens_grad = as_low(
        grad_mid
        + scale_one * scaled_one
        - resid_in
        * scale_one
        * scale_one
        * scale_one
        * jnp.mean(scaled_one * resid_in, axis=-1, keepdims=True)
    )

    def blocks_of(full, start):
        place = start + jnp.arange(width)[:, None] % gate_width
        fold = (place == jnp.arange(2 * gate_width)[None, :]).astype(jnp.float32)
        full = jnp.where(same, full, 0.0)
        return jnp.dot(full, fold, precision=lax.Precision.HIGHEST)

    totals = jnp.concatenate(
        [totals[:7], totals[7:] * (GATE_SCALE * jax.nn.sigmoid(-decay))[None]], axis=0
    )
    gates = blocks_of(full_rec, 0) + blocks_of(full_in, gate_width)
    owned = width // z_size
    gates = as_low(gates).reshape(z_size, owned, 2 * gate_width)
    totals = jnp.swapaxes(jnp.pad(totals, ((0, 8), (0, 0))).reshape(16, z_size, owned), 0, 1)
    totals = as_low(totals)
    lanes = max(width, 2 * gate_width)
    edge = seq_size * chunk
    pack = jnp.concatenate(
        [
            jnp.pad(part, ((0, 0), (0, 0), (0, lanes - part.shape[-1])))
            for part in (
                by_owner((grad_input,)).reshape(z_size, edge, width),
                gates,
                totals,
            )
        ],
        axis=1,
    )
    pack, branch_home = barrier((pack.reshape(z_size * pack.shape[1], lanes), branch_home))
    pack, ff_got = barrier((pack, ff_got))
    pack = home_rows(pack)
    grad_gate_home, grad_up_home = own_columns(ff_got[:, 0]), own_columns(ff_got[:, 1])
    grad_gain_two = gain_home(norm_gain2, ((grad_gate_home, w_gate), (grad_up_home, w_up)))
    grad_branch_home = own_columns(exchange(branch_home.reshape(seq_size, chunk, width)))
    grad_input_home = own_columns(exchange(pack[:edge, :width].reshape(seq_size, chunk, width)))
    grad_gain_one = gain_home(
        norm_gain1, ((grad_branch_home, w_branch), (grad_input_home, w_input))
    )
    gates = as_wide(pack[edge : edge + owned])
    totals = as_wide(pack[edge + owned :, :owned])
    return (
        mixed,
        tokens_grad,
        grad_gain_one,
        grad_branch_home,
        grad_input_home,
        totals[:TAPS],
        totals[4],
        gates[:, :gate_width],
        totals[5],
        gates[:, gate_width : 2 * gate_width],
        totals[6],
        totals[7],
        as_wide(out_home),
        grad_gain_two,
        grad_gate_home,
        grad_up_home,
        as_wide(down_home),
    )


def solution(mesh):
    row = P(("seq", "fsdp"))
    rows = P(("seq", "fsdp"), None)
    columns = P(None, ("seq", "fsdp"))
    return jax.shard_map(
        shards,
        mesh=mesh,
        in_specs=(
            rows,
            rows,
            P(),
            P(),
            P(),
            row,
            rows,
            rows,
            columns,
            row,
            rows,
            row,
            rows,
            row,
            row,
            rows,
            row,
            rows,
            rows,
            rows,
        ),
        out_specs=(
            rows,
            rows,
            row,
            rows,
            rows,
            columns,
            row,
            rows,
            row,
            rows,
            row,
            row,
            rows,
            row,
            rows,
            rows,
            rows,
        ),
        check_vma=False,
    )
```

```python
import jax
import jax.numpy as jnp
from jax import lax
from jax.experimental import pallas as pl
from jax.experimental.pallas import tpu as pltpu
from jax.sharding import PartitionSpec as P

BLOCK = 128
LANES = 128
TAPS = 4
UNROLL = 8
NORM_EPSILON = 1e-06
GATE_SCALE = 8.0
VMEM_LIMIT = 48 * 1024 * 1024
GELU_C = 0.7978845608028654
GELU_A = 0.044715
LIGHT = pl.CostEstimate(flops=1, transcendentals=0, bytes_accessed=1)


def as_low(values):
    return values.astype(jnp.bfloat16)


def as_wide(values):
    return values.astype(jnp.float32)


def mm(left, right, out=jnp.float32):
    return jnp.dot(left, right, preferred_element_type=jnp.float32).astype(out)


def mm_tn(left, right, out=jnp.float32):
    return lax.dot_general(
        left, right, (((0,), (0,)), ((), ())), preferred_element_type=jnp.float32
    ).astype(out)


def mm_nt(left, right, out=jnp.float32):
    return lax.dot_general(
        left, right, (((1,), (1,)), ((), ())), preferred_element_type=jnp.float32
    ).astype(out)


def swap(values, axis, flip):
    count = lax.axis_size(axis)
    return lax.ppermute(values, axis, [(i, i ^ flip) for i in range(count)])


barrier = lax.optimization_barrier


def plane_even(own):
    return [own] + [swap(own, "seq", k) for k in range(2, lax.axis_size("seq"), 2)]


def plane_first(own):
    count = lax.axis_size("seq")
    flips = (2, 4) if count == 8 else range(2, count, 2)
    return [swap(own, "seq", k) for k in flips]


def plane_second(own, first):
    even = [own, *first]
    if lax.axis_size("seq") == 8:
        half = own.shape[0] // 2
        near, side = first
        even.append((swap(side[:half], "seq", 2), swap(near[half:], "seq", 4)))
    return even


def plane_all(even):
    return list(even) + [jax.tree.map(lambda part: swap(part, "seq", 1), piece) for piece in even]


def slot_order():
    evens = lax.axis_size("seq") // 2
    return sorted(range(1, evens), key=lambda slot: -bin(slot).count("1")) + [0]


def scatter_plane(product):
    evens = lax.axis_size("seq") // 2
    order = slot_order()
    ready, pairs, after = {}, {}, None

    def odd(slot):
        value = as_low(product(evens + slot, after))
        ready[slot] = swap(value, "seq", 1)
        return value

    after = odd(order[0])
    for index, slot in enumerate(order[:-1]):
        after = odd(order[index + 1])
        after = product(slot, after) + as_wide(ready[slot])
        pairs[slot] = after
    if evens != 4:
        moved = [swap(as_low(pairs[slot]), "seq", 2 * slot) for slot in order[:-1]]
        return moved + [product(0, after) + as_wide(ready[0])], moved[0]
    near, side, far = (pairs[slot] for slot in (1, 2, 3))
    half = far.shape[0] // 2
    by_near = swap(as_low(jnp.concatenate([far[:half], near[:half]])), "seq", 2)
    by_side = swap(as_low(jnp.concatenate([far[half:], side[half:]])), "seq", 4)
    own = product(0, after) + as_wide(ready[0])
    by_near, by_side, last = barrier((by_near, by_side, own))
    near_low = swap(as_low(near[half:] + as_wide(by_side[:half])), "seq", 2)
    side_top = swap(as_low(side[:half] + as_wide(by_near[:half])), "seq", 4)
    return [last, (by_near[half:], near_low), (side_top, by_side[half:])], own


def split_pairs(pair):
    rows = pair.shape[0] // (lax.axis_size("seq") // 2)
    parts = [pair[slot * rows : (slot + 1) * rows] for slot in slot_order()]
    return [as_low(part) for part in parts[:-1]] + parts[-1:]


def scatter_pairs(parts):
    return [
        swap(part, "seq", 2 * slot) if slot else part for slot, part in zip(slot_order(), parts)
    ]


def slot_product(operands, multiply):
    rows = operands[0].shape[0] // lax.axis_size("seq")

    def product(slot, after):
        parts = tuple(operand[slot * rows : (slot + 1) * rows] for operand in operands)
        if after is not None:
            parts = barrier((*parts, after))[:-1]
        return multiply(*parts)

    return product


def summed(parts):
    total = None
    for part in parts:
        if isinstance(part, (tuple, list)):
            part = jnp.concatenate(part, axis=0)
        total = as_wide(part) if total is None else total + as_wide(part)
    return total


def gather_small(value, axis):
    value = value[None]
    bit = 1
    while bit < lax.axis_size(axis):
        other = swap(value, axis, bit)
        upper = (lax.axis_index(axis) // bit) % 2 == 1
        value = jnp.where(
            upper, jnp.concatenate([other, value]), jnp.concatenate([value, other])
        )
        bit *= 2
    return value


def spread_z(value):
    count = lax.axis_size("fsdp")
    return jnp.stack([value] + [swap(value, "fsdp", j) for j in range(1, count)], axis=0)


def gelu_parts(values):
    inner = GELU_C * (values + GELU_A * values * values * values)
    bend = jnp.tanh(inner)
    return (0.5 * values * (1.0 + bend), bend)


def gelu_slope(values, bend):
    return 0.5 * (1.0 + bend) + 0.5 * values * (1.0 - bend * bend) * GELU_C * (
        1.0 + 3.0 * GELU_A * values * values
    )


def expm1_small(values):
    series = values * (1.0 / 120.0) + 1.0 / 24.0
    for scale in (1.0 / 6.0, 0.5, 1.0):
        series = series * values + scale
    return series * values


def block_rows(index):
    return pl.ds(pl.multiple_of(index * BLOCK, BLOCK), BLOCK)


def lane_tiles(width):
    return [(low, min(LANES, width - low)) for low in range(0, width, LANES)]


def piece_specs(pieces, steps):
    specs = []
    chunk = pieces[0].shape[0] // steps
    block = (chunk, pieces[0].shape[1])
    last = steps // 2 - 1
    for piece in pieces:
        if isinstance(piece, (tuple, list)):
            specs.append(pl.BlockSpec(block, lambda i: (jnp.minimum(i, last), 0)))
            specs.append(pl.BlockSpec(block, lambda i: (jnp.maximum(i - last - 1, 0), 0)))
        else:
            specs.append(pl.BlockSpec(block, lambda i: (i, 0)))
    return specs


def piece_halves(pieces):
    return [len(piece) if isinstance(piece, (tuple, list)) else 1 for piece in pieces]


def joined_rows(refs, halves):
    upper = pl.program_id(0) < pl.num_programs(0) // 2
    rows, at = [], 0
    for parts in halves:
        value = refs[at][...]
        rows.append(value if parts == 1 else jnp.where(upper, value, refs[at + 1][...]))
        at += parts
    return jnp.concatenate(rows, axis=0)


def stack(pieces, name, gain=None, weights=(), gated=False, steps=8):
    count = len(pieces)
    halves, flat = piece_halves(pieces), jax.tree.leaves(pieces)
    rows, model = pieces[0].shape
    chunk = rows // steps
    extra = ([gain] if gain is not None else []) + list(weights)

    def kernel(*refs):
        values = joined_rows(refs[: len(flat)], halves)
        refs = refs[len(flat) :]
        if gain is not None:
            gain_ref, refs = refs[0], refs[1:]
            wide = values.astype(jnp.float32)
            scale = lax.rsqrt(jnp.mean(wide * wide, axis=-1, keepdims=True) + NORM_EPSILON)
            values = (wide * scale * gain_ref[...]).astype(jnp.bfloat16)
        weight_refs, refs = refs[: len(weights)], refs[len(weights) :]
        refs[0][...] = values.reshape(count, chunk, model)
        for weight_ref, out_ref in zip(weight_refs, refs[1:]):
            out = jnp.dot(values, weight_ref[...], preferred_element_type=jnp.float32)
            if not gated:
                out_ref[...] = out.reshape(count, chunk, out.shape[1])
        if gated:
            gate, up = out[:, : out.shape[1] // 2], out[:, out.shape[1] // 2 :]
            act, bend = gelu_parts(gate)
            for out_ref, out in zip(refs[1:], (act, up * gelu_slope(gate, bend), act * up)):
                out_ref[...] = out.reshape(count, chunk, out.shape[1]).astype(out_ref.dtype)

    widths = [weight.shape[1] for weight in weights]
    if gated:
        widths = [widths[0] // 2] * 2
    outs = [shaped((count, rows, model), jnp.bfloat16)] + [shaped((count, rows, w)) for w in widths]
    if gated:
        outs.append(shaped((count, rows, widths[0]), jnp.bfloat16))
    done = pl.pallas_call(
        kernel,
        grid=(steps,),
        in_specs=piece_specs(pieces, steps) + [pl.BlockSpec(e.shape, lambda i: (0, 0)) for e in extra],
        out_specs=[pl.BlockSpec((count, chunk, o.shape[2]), lambda i: (0, i, 0)) for o in outs],
        out_shape=outs,
        compiler_params=pltpu.CompilerParams(vmem_limit_bytes=VMEM_LIMIT),
        cost_estimate=LIGHT,
        name=name,
    )(*flat, *extra)
    return [out.reshape(count * rows, out.shape[2]) for out in done]


def ff_backward(top, down_w, act, bend, steps=8):
    chunk = top.shape[0] // steps
    ffw, model = down_w.shape

    def kernel(top_ref, down_ref, act_ref, bend_ref, out_ref):
        grad = lax.dot_general(
            top_ref[...], down_ref[...], (((1,), (1,)), ((), ())), preferred_element_type=jnp.float32
        )
        out_ref[:, :ffw] = (grad * bend_ref[...]).astype(jnp.bfloat16)
        out_ref[:, ffw:] = (grad * act_ref[...]).astype(jnp.bfloat16)

    block = pl.BlockSpec((chunk, ffw), lambda i: (i, 0))
    return pl.pallas_call(
        kernel,
        grid=(steps,),
        in_specs=[
            pl.BlockSpec((chunk, model), lambda i: (i, 0)),
            pl.BlockSpec((ffw, model), lambda i: (0, 0)),
            block,
            block,
        ],
        out_specs=pl.BlockSpec((chunk, 2 * ffw), lambda i: (i, 0)),
        out_shape=shaped((top.shape[0], 2 * ffw), jnp.bfloat16),
        compiler_params=pltpu.CompilerParams(vmem_limit_bytes=VMEM_LIMIT),
        cost_estimate=LIGHT,
        name="ff_backward",
    )(top, down_w, act, bend)


def project(rows, weight, name, steps=8):
    chunk = rows.shape[0] // steps
    width = weight.shape[1]

    def kernel(rows_ref, weight_ref, out_ref):
        out_ref[...] = jnp.dot(rows_ref[...], weight_ref[...], preferred_element_type=jnp.float32)

    return pl.pallas_call(
        kernel,
        grid=(steps,),
        in_specs=[
            pl.BlockSpec((chunk, rows.shape[1]), lambda i: (i, 0)),
            pl.BlockSpec(weight.shape, lambda i: (0, 0)),
        ],
        out_specs=pl.BlockSpec((chunk, width), lambda i: (i, 0)),
        out_shape=shaped((rows.shape[0], width)),
        compiler_params=pltpu.CompilerParams(vmem_limit_bytes=VMEM_LIMIT),
        cost_estimate=pl.CostEstimate(
            flops=2 * rows.size * width,
            transcendentals=0,
            bytes_accessed=2 * rows.size + 4 * rows.shape[0] * width,
        ),
        name=name,
    )(rows, weight)


def dead_mask(rows, live_count):
    return (rows < live_count).astype(jnp.float32)


def lru_forward_kernel(
    live_ref,
    first_ref,
    pred_ref,
    u_ref,
    tail_ref,
    vec_ref,
    rec_ref,
    in_ref,
    xc_ref,
    keep_ref,
    drive_ref,
    rate_ref,
    slope_ref,
    into_ref,
    bent_ref,
    sum_ref,
    ext_ref,
):
    blocks = u_ref.shape[0] // BLOCK
    tiles = lane_tiles(u_ref.shape[1])
    rows = lax.broadcasted_iota(jnp.int32, (BLOCK, LANES), 0)

    def block(index, carry):
        at = block_rows(index)
        first = first_ref[index]
        pred = pred_ref[index]
        live = dead_mask(rows, live_ref[index])
        before = jnp.maximum(pred, 0)
        joined = jnp.where((pred >= 0) & (first == 0), 1.0, 0.0)
        for low, size in tiles:
            lanes = slice(low, low + size)
            u_value = u_ref[at, lanes]
            ext_ref[0:8, :size] = tail_ref[before, :, lanes] * joined
            ext_ref[8 : 8 + BLOCK, :size] = u_value
            later = vec_ref[1:2, lanes] * ext_ref[7 : 7 + BLOCK, :size]
            for tap in range(2, TAPS):
                later = later + vec_ref[tap : tap + 1, lanes] * ext_ref[8 - tap : 8 - tap + BLOCK, :size]
            conv = vec_ref[4:5, lanes] + vec_ref[0:1, lanes] * u_value + later * live[:, :size]
            xc_ref[at, lanes] = conv.astype(jnp.bfloat16)
        low_rows = xc_ref[at, :]
        pre_rec = jnp.dot(low_rows, rec_ref[...], preferred_element_type=jnp.float32)
        pre_in = jnp.dot(low_rows, in_ref[...], preferred_element_type=jnp.float32)
        for tile, (low, size) in enumerate(tiles):
            lanes = slice(low, low + size)
            rate = jax.nn.sigmoid(pre_rec[:, lanes] + vec_ref[5:6, lanes])
            entry = jax.nn.sigmoid(pre_in[:, lanes] + vec_ref[6:7, lanes])
            minus = expm1_small(rate * vec_ref[7:8, lanes])
            twice = minus * (2.0 + minus)
            into = jnp.sqrt(-twice) * entry
            drive = into * low_rows[:, lanes].astype(jnp.float32)
            rate_ref[tile, at, :size] = rate
            keep_ref[tile, at, :size] = (1.0 + minus) * live[:, :size]
            drive_ref[tile, at, :size] = drive
            slope_ref[tile, at, :size] = drive + drive / twice
            into_ref[tile, at, :size] = into
            bent_ref[tile, at, :size] = drive * (1.0 - entry)

        @pl.when(first > 0)
        def _():
            top = pl.ds(pl.multiple_of(index * BLOCK, BLOCK), 8)
            after = (rows[:8] > 0).astype(jnp.float32)
            for tile in range(len(tiles)):
                keep_ref[tile, top, :] = keep_ref[tile, top, :] * after

        return carry

    lax.fori_loop(0, blocks, block, 0)

    def step(place, carry):
        at = pl.ds(place, blocks, stride=BLOCK)
        after = []
        for tile, (total, state) in enumerate(carry):
            keep = keep_ref[tile, at, :]
            after.append((total * keep, keep * state + drive_ref[tile, at, :]))
        return tuple(after)

    ones = jnp.ones((blocks, LANES), jnp.float32)
    start = tuple((ones, jnp.zeros_like(ones)) for _ in tiles)
    ends = lax.fori_loop(0, BLOCK, step, start, unroll=UNROLL)
    for tile, (total, state) in enumerate(ends):
        sum_ref[0, tile] = total
        sum_ref[1, tile] = state


def lru_state_kernel(
    pos_ref,
    all_ref,
    keep_ref,
    drive_ref,
    rate_ref,
    slope_ref,
    ypre_ref,
    vec_ref,
    hy_ref,
    act_ref,
    bend_ref,
    slow_ref,
    rec_ref,
    line_ref,
    h_ref,
    ext_ref,
):
    tiles = lane_tiles(ypre_ref.shape[1])
    turns, _, _, blocks, _ = all_ref.shape

    def chain(place, states):
        slot = pos_ref[place]
        turn, index = slot // blocks, slot % blocks
        after = []
        for tile, state in enumerate(states):
            line_ref[tile, pl.ds(slot, 1), :] = state
            keep = all_ref[turn, 0, tile, pl.ds(index, 1), :]
            after.append(keep * state + all_ref[turn, 1, tile, pl.ds(index, 1), :])
        return tuple(after)

    zero = jnp.zeros((1, LANES), jnp.float32)
    lax.fori_loop(0, turns * blocks, chain, tuple(zero for _ in tiles))
    def step(place, states):
        at = pl.ds(place, blocks, stride=BLOCK)
        after = []
        for tile, state in enumerate(states):
            state = keep_ref[tile, at, :] * state + drive_ref[tile, at, :]
            h_ref[tile, at, :] = state
            after.append(state)
        return tuple(after)

    start = tuple(line_ref[tile, 0:blocks, :] for tile in range(len(tiles)))
    lax.fori_loop(0, BLOCK, step, start, unroll=UNROLL)

    def block(index, carry):
        at = block_rows(index)
        for tile, (low, size) in enumerate(tiles):
            lanes = slice(low, low + size)
            h_value = h_ref[tile, at, :size]
            value = ypre_ref[at, lanes]
            act, bend = gelu_parts(value)
            hy_ref[at, lanes] = (h_value * act).astype(jnp.bfloat16)
            act_ref[tile, at, :size] = act
            bend_ref[tile, at, :size] = h_value * gelu_slope(value, bend)
            ext_ref[7:8, :size] = line_ref[tile, pl.ds(index, 1), :size]
            ext_ref[8 : 8 + BLOCK, :size] = h_value
            rate = rate_ref[tile, at, :size]
            slow = rate * (
                keep_ref[tile, at, :size] * ext_ref[7 : 7 + BLOCK, :size]
                + slope_ref[tile, at, :size]
            )
            slow_ref[tile, at, :size] = slow
            rec_ref[tile, at, :size] = slow * (1.0 - rate) * vec_ref[7:8, lanes]
        return carry

    lax.fori_loop(0, blocks, block, 0)


def lru_back(pieces, out_w, act, bend, keep, steps=8):
    count = len(pieces)
    halves, flat = piece_halves(pieces), jax.tree.leaves(pieces)
    rows, model = pieces[0].shape
    width = out_w.shape[0]
    tiles = lane_tiles(width)
    chunk = rows // steps
    blocks = count * rows // BLOCK

    def kernel(*refs):
        values = joined_rows(refs[: len(flat)], halves)
        w_ref, act_ref, bend_ref, keep_ref, out_ref, dy_ref, dh_ref, send_ref = refs[len(flat) :]
        here = pl.program_id(0)
        out_ref[...] = values.reshape(count, chunk, model)
        grads = lax.dot_general(
            values, w_ref[...], (((1,), (1,)), ((), ())), preferred_element_type=jnp.float32
        )
        for slot in range(count):
            span = pl.ds(pl.multiple_of(slot * rows + here * chunk, chunk), chunk)
            for tile, (low, size) in enumerate(tiles):
                lanes = slice(low, low + size)
                grad = grads[slot * chunk : (slot + 1) * chunk, lanes]
                dy_ref[slot, :, lanes] = (grad * bend_ref[tile, slot, :, :size]).astype(jnp.bfloat16)
                dh_ref[tile, span, :size] = grad * act_ref[tile, slot, :, :size]

        @pl.when(here == steps - 1)
        def _():
            def step(turn, carry):
                at = pl.ds(BLOCK - 1 - turn, blocks, stride=BLOCK)
                return tuple(
                    keep_ref[tile, at, :] * (dh_ref[tile, at, :] + value)
                    for tile, value in enumerate(carry)
                )

            zero = jnp.zeros((blocks, LANES), jnp.float32)
            ends = lax.fori_loop(0, BLOCK, step, tuple(zero for _ in tiles), unroll=UNROLL)
            for tile, value in enumerate(ends):
                send_ref[tile] = value

    depth = len(tiles)
    total = count * rows
    out, dy, dh, send = pl.pallas_call(
        kernel,
        grid=(steps,),
        in_specs=piece_specs(pieces, steps)
        + [
            pl.BlockSpec((width, model), lambda i: (0, 0)),
            pl.BlockSpec((depth, count, chunk, LANES), lambda i: (0, 0, i, 0)),
            pl.BlockSpec((depth, count, chunk, LANES), lambda i: (0, 0, i, 0)),
            pl.BlockSpec((depth, total, LANES), lambda i: (0, 0, 0)),
        ],
        out_specs=[
            pl.BlockSpec((count, chunk, model), lambda i: (0, i, 0)),
            pl.BlockSpec((count, chunk, width), lambda i: (0, i, 0)),
            pl.BlockSpec((depth, total, LANES), lambda i: (0, 0, 0)),
            pl.BlockSpec((depth, blocks, LANES), lambda i: (0, 0, 0)),
        ],
        out_shape=[
            shaped((count, rows, model), jnp.bfloat16),
            shaped((count, rows, width), jnp.bfloat16),
            shaped((depth, total, LANES)),
            shaped((depth, blocks, LANES)),
        ],
        compiler_params=pltpu.CompilerParams(vmem_limit_bytes=VMEM_LIMIT),
        cost_estimate=LIGHT,
        name="lru_back",
    )(
        *flat,
        out_w,
        act.reshape(depth, count, rows, LANES),
        bend.reshape(depth, count, rows, LANES),
        keep,
    )
    return out.reshape(total, model), dy.reshape(total, width), dh, send


def fold_rows(values):
    return values.reshape(BLOCK // 8, 8, values.shape[1]).sum(axis=0)


def lru_grad_kernel(
    live_ref,
    first_ref,
    pred_ref,
    pos_ref,
    all_ref,
    back_ref,
    dh_ref,
    keep_ref,
    slow_ref,
    bent_rec_ref,
    into_ref,
    bent_in_ref,
    u_ref,
    tail_ref,
    vec_ref,
    rec_ref,
    in_ref,
    drec_ref,
    din_ref,
    du_ref,
    last_ref,
    head_ref,
    total_ref,
    line_ref,
    g_ref,
    ext_ref,
    acc_ref,
    direct_ref,
):
    blocks = u_ref.shape[0] // BLOCK
    width = u_ref.shape[1]
    tiles = lane_tiles(width)
    every = back_ref.shape[0] * blocks
    rows = lax.broadcasted_iota(jnp.int32, (BLOCK, LANES), 0)

    def chain(count, carry):
        slot = pos_ref[every - 1 - count]
        turn, index = slot // blocks, slot % blocks
        after = []
        for tile, value in enumerate(carry):
            line_ref[tile, pl.ds(slot, 1), :] = value
            keep = all_ref[turn, 0, tile, pl.ds(index, 1), :]
            after.append(keep * value + back_ref[turn, tile, pl.ds(index, 1), :])
        return tuple(after)

    zero = jnp.zeros((1, LANES), jnp.float32)
    lax.fori_loop(0, every, chain, tuple(zero for _ in tiles))

    def step(turn, carry):
        at = pl.ds(BLOCK - 1 - turn, blocks, stride=BLOCK)
        after = []
        for tile, value in enumerate(carry):
            grad = dh_ref[tile, at, :] + value
            g_ref[tile, at, :] = grad
            after.append(keep_ref[tile, at, :] * grad)
        return tuple(after)

    start = tuple(line_ref[tile, 0:blocks, :] for tile in range(len(tiles)))
    lax.fori_loop(0, BLOCK, step, start, unroll=UNROLL)
    acc_ref[...] = jnp.zeros_like(acc_ref)
    contract = (((1,), (1,)), ((), ()))

    def block(index, carry):
        at = block_rows(index)
        first = first_ref[index]
        pred = pred_ref[index]
        live = dead_mask(rows, live_ref[index])
        before = jnp.maximum(pred, 0)
        joined = jnp.where((pred >= 0) & (first == 0), 1.0, 0.0)
        for tile, (low, size) in enumerate(tiles):
            lanes = slice(low, low + size)
            grad = g_ref[tile, at, :size]
            acc_ref[7, :, lanes] += fold_rows(grad * slow_ref[tile, at, :size])
            d_rec = (grad * bent_rec_ref[tile, at, :size]).astype(jnp.bfloat16)
            d_in = (grad * bent_in_ref[tile, at, :size]).astype(jnp.bfloat16)
            drec_ref[at, lanes] = d_rec
            din_ref[at, lanes] = d_in
            acc_ref[5, :, lanes] += fold_rows(d_rec.astype(jnp.float32))
            acc_ref[6, :, lanes] += fold_rows(d_in.astype(jnp.float32))
            direct_ref[:, lanes] = grad * into_ref[tile, at, :size]
        direct_ref[...] += lax.dot_general(
            drec_ref[at, :], rec_ref[...], contract, preferred_element_type=jnp.float32
        ) + lax.dot_general(
            din_ref[at, :], in_ref[...], contract, preferred_element_type=jnp.float32
        )
        for low, size in tiles:
            lanes = slice(low, low + size)
            dxc = direct_ref[:, lanes]
            u_value = u_ref[at, lanes]
            ext_ref[0:8, :size] = tail_ref[before, :, lanes] * joined
            ext_ref[8 : 8 + BLOCK, :size] = u_value
            acc_ref[4, :, lanes] += fold_rows(dxc)
            acc_ref[0, :, lanes] += fold_rows(dxc * u_value)
            part = dxc * live[:, :size]
            for tap in range(1, TAPS):
                acc_ref[tap, :, lanes] += fold_rows(part * ext_ref[8 - tap : 8 - tap + BLOCK, :size])
            zero_tile = jnp.zeros((8, size), jnp.float32)
            ext_ref[0:8, :size] = zero_tile
            ext_ref[8 : 8 + BLOCK, :size] = part
            ext_ref[8 + BLOCK : 16 + BLOCK, :size] = zero_tile
            du_value = dxc * vec_ref[0:1, lanes]
            head = zero_tile
            for tap in range(1, TAPS):
                weight = vec_ref[tap : tap + 1, lanes]
                du_value = du_value + weight * ext_ref[8 + tap : 8 + tap + BLOCK, :size]
                head = head + weight * ext_ref[tap : tap + 8, :size]
            du_ref[at, lanes] = du_value.astype(jnp.bfloat16)
            last_ref[index, :, lanes] = du_value[BLOCK - 8 :]
            head_ref[index, :, lanes] = head * joined
        return carry

    lax.fori_loop(0, blocks, block, 0)
    for index in range(8):
        total_ref[index : index + 1, :] = jnp.sum(acc_ref[index], axis=0, keepdims=True)


def head_kernel(succ_ref, prev_ref, last_ref, head_ref, out_ref):
    blocks = last_ref.shape[0]

    def block(index, carry):
        succ = succ_ref[index]
        head = head_ref[jnp.maximum(succ, 0)]
        tail = last_ref[index] + jnp.where(succ >= 0, head, jnp.zeros_like(head))
        out_ref[index, :8, :] = prev_ref[index, :8, :]
        out_ref[index, 8:, :] = tail.astype(jnp.bfloat16)
        return carry

    lax.fori_loop(0, blocks, block, 0)


def shaped(shape, dtype=jnp.float32):
    return jax.ShapeDtypeStruct(shape, dtype)


def whole(kernel, scalars, arrays, outs, scratch, name):
    specs = [pl.BlockSpec(memory_space=pltpu.SMEM)] * len(scalars)
    specs += [pl.BlockSpec(memory_space=pltpu.VMEM)] * len(arrays)
    return pl.pallas_call(
        kernel,
        out_shape=outs,
        in_specs=specs,
        out_specs=[pl.BlockSpec(memory_space=pltpu.VMEM)] * len(outs),
        scratch_shapes=scratch,
        compiler_params=pltpu.CompilerParams(vmem_limit_bytes=VMEM_LIMIT),
        cost_estimate=LIGHT,
        name=name,
    )(*scalars, *arrays)


def shards(
    tokens,
    cotangent,
    lengths,
    offsets,
    deal,
    norm_gain1,
    w_branch,
    w_input,
    conv_kernel,
    conv_bias,
    gate_rec,
    bias_rec,
    gate_in,
    bias_in,
    decay_param,
    w_out,
    norm_gain2,
    w_gate,
    w_up,
    w_down,
):
    seq_size, z_size = lax.axis_size("seq"), lax.axis_size("fsdp")
    seq_at, z_at = lax.axis_index("seq"), lax.axis_index("fsdp")
    rows_here, model = tokens.shape
    blocks_here = rows_here // BLOCK
    blocks = seq_size * blocks_here
    every = blocks * z_size
    count = rows_here * seq_size
    width = w_branch.shape[1] // seq_size
    ffw = w_gate.shape[1] // seq_size
    chunk = w_branch.shape[0]
    gate_width = gate_rec.shape[1]
    groups = width // gate_width
    tiles = len(lane_tiles(width))
    tiled = shaped((tiles, count, LANES))

    order = jnp.array([k for k in range(seq_size) if k % 2 == 0] + [k for k in range(seq_size) if k % 2], jnp.int32)
    source = jnp.bitwise_xor(order, seq_at)
    flips = jnp.bitwise_xor(jnp.arange(z_size, dtype=jnp.int32), z_at)
    stored = (source[None, :, None] * z_size + flips[:, None, None]) * blocks_here
    stored = (stored + jnp.arange(blocks_here, dtype=jnp.int32)[None, None, :]).reshape(every)
    logical = deal[stored]
    places = jnp.arange(every, dtype=jnp.int32)
    at_place = logical[None, :] == places[:, None]
    position = jnp.sum(jnp.where(at_place, places[None, :], 0), axis=1)
    mine = logical[:blocks]

    def place_of(wanted):
        hit = logical[None, :] == wanted[:, None]
        return jnp.sum(jnp.where(hit, places[None, :] + 1, 0), axis=1) - 1

    pred = place_of(mine - 1)
    succ = place_of(mine + 1)
    left_over = lengths[None, :] - (mine[:, None] - offsets[None, :]) * BLOCK
    inside = (mine[:, None] >= offsets[None, :]) & (left_over > 0)
    live_count = jnp.max(jnp.where(inside, jnp.minimum(left_over, BLOCK), 0), axis=1)
    first = jnp.any(inside & (mine[:, None] == offsets[None, :]), axis=1).astype(jnp.int32)
    own_live = live_count[:blocks_here]
    live_col = (
        jnp.arange(BLOCK, dtype=jnp.int32)[None, :] < own_live[:, None]
    ).astype(jnp.float32).reshape(rows_here, 1)

    def columns(weight):
        return jnp.swapaxes(as_low(weight).reshape(chunk, seq_size, -1), 0, 1)

    def exchange(value):
        return lax.all_to_all(value, "seq", 0, 0, tiled=True)

    def gather_rows(value):
        return lax.all_gather(value, "fsdp", axis=0, tiled=True)

    def gather_columns(value):
        got = lax.all_gather(value, "fsdp", axis=0, tiled=False)
        return jnp.swapaxes(got, 0, 1).reshape(-1, value.shape[-1])

    gains = gather_small(as_low(jnp.stack([norm_gain1, norm_gain2])), "seq")
    mix = jnp.stack([columns(w_input), columns(w_branch)], axis=1)
    mix, own_tokens, gains = barrier((mix, tokens, gains))
    x_first = plane_first(own_tokens)
    out_w = gather_rows(as_low(w_out))
    mix = exchange(mix)
    params = [conv_kernel, conv_bias[None], bias_rec[None], bias_in[None], decay_param[None]]
    gains = jnp.pad(gains.reshape(2 * seq_size, chunk), ((0, 0), (0, width // z_size - chunk)))
    params = jnp.concatenate([as_low(part) for part in params] + [gains], axis=0).T
    small = jnp.concatenate([as_low(gate_rec), as_low(gate_in), params], axis=1)
    small = gather_small(small, "fsdp")
    mix, out_w, small, x_first = barrier((mix, out_w, small, x_first))
    x_even = plane_second(own_tokens, x_first)
    input_w = gather_columns(mix[:, 0])
    branch_w = gather_columns(mix[:, 1])
    x_pieces = plane_all(x_even)
    gains = small[:, :chunk, 2 * gate_width + 8 :].reshape(z_size, chunk, seq_size, 2)
    gains = as_wide(jnp.transpose(gains, (3, 2, 0, 1)).reshape(2, model))
    gain_one, gain_two = gains[:1], gains[1:]
    small = small.reshape(width, -1)

    same = jnp.arange(width)[:, None] // gate_width == jnp.arange(width)[None, :] // gate_width

    def diagonal(part):
        return jnp.where(same, jnp.tile(part, (1, groups)), jnp.zeros((), jnp.bfloat16))

    vectors = as_wide(small[:, 2 * gate_width : 2 * gate_width + 8]).T
    decay = vectors[7]
    vectors = jnp.concatenate([vectors[:7], -GATE_SCALE * jax.nn.softplus(-decay)[None]], axis=0)
    ff = jnp.concatenate([columns(w_gate), columns(w_up)], axis=2)
    top_own = as_low(live_col * as_wide(cotangent))
    x_pieces, ff, top_own = barrier((x_pieces, ff, top_own))
    ff = exchange(ff)
    x_pieces, top_own = barrier((x_pieces, top_own))
    top_even = plane_even(top_own)

    normed_one, u_value = stack(x_pieces, "norm_one", gain_one, (input_w,))
    u_value, gates_in = barrier((u_value, small))
    rec_w = diagonal(gates_in[:, :gate_width])
    in_w = diagonal(gates_in[:, gate_width : 2 * gate_width])
    down_w = gather_rows(as_low(w_down))

    def edges(rows):
        rows = spread_z(as_low(barrier(rows)).reshape(blocks * (TAPS - 1), width))
        rows = as_wide(rows).reshape(every, TAPS - 1, width)
        return jnp.pad(rows, ((0, 0), (9 - TAPS, 0), (0, 0)))

    tails = edges(u_value.reshape(blocks, BLOCK, width)[:, BLOCK - TAPS + 1 :])
    tails, rec_w, in_w, vectors, ff = barrier((tails, rec_w, in_w, vectors, ff))
    ff_w = gather_columns(ff)
    conv_low, keep, drive, rate, slope, into, bent_in, summary = whole(
        lru_forward_kernel,
        (live_count, first, pred),
        (u_value, tails, vectors, rec_w, in_w),
        (
            shaped((count, width), jnp.bfloat16),
            *[tiled] * 6,
            shaped((2, tiles, blocks, LANES)),
        ),
        [pltpu.VMEM((BLOCK + 8, LANES), jnp.float32)],
        "lru_forward",
    )
    branch_pre = project(normed_one, branch_w, "branch_pre")
    summaries = spread_z(summary)
    summaries, branch_pre, top_even = barrier((summaries, branch_pre, top_even))
    gated, act, bend, slow, bent_rec = whole(
        lru_state_kernel,
        (position,),
        (summaries, keep, drive, rate, slope, branch_pre, vectors),
        (shaped((count, width), jnp.bfloat16), *[tiled] * 4),
        [
            pltpu.VMEM((tiles, every, LANES), jnp.float32),
            pltpu.VMEM((tiles, count, LANES), jnp.float32),
            pltpu.VMEM((BLOCK + 8, LANES), jnp.float32),
        ],
        "lru_state",
    )
    resid_in = as_wide(tokens)
    mid_parts, mid_last = scatter_plane(slot_product((gated,), lambda rows: mm(rows, out_w)))
    top_even, mid_last = barrier((top_even, mid_last))
    (top_low,) = stack(plane_all(top_even), "stack_top")
    mid_parts, top_low = barrier((mid_parts, top_low))
    resid_mid = resid_in + summed(mid_parts)
    scale_two = lax.rsqrt(jnp.mean(resid_mid * resid_mid, axis=-1, keepdims=True) + NORM_EPSILON)
    own_two = as_low(resid_mid * scale_two * gain_two)
    two_first = plane_first(own_two)
    two_first, ff_w = barrier((two_first, ff_w))
    normed_two, ff_act, ff_bend, hidden = stack(
        plane_all(plane_second(own_two, two_first)), "ff_forward", None, (ff_w,), True
    )
    grad_down = mm_tn(hidden, top_low, jnp.bfloat16)
    ff_act, ff_bend, grad_down, down_w = barrier((ff_act, ff_bend, grad_down, down_w))
    d_ff = ff_backward(top_low, down_w, ff_act, ff_bend)
    two_parts, two_last = scatter_plane(
        slot_product((d_ff,), lambda rows: mm_nt(rows, ff_w))
    )
    down_home = lax.psum_scatter(grad_down, "fsdp", scatter_dimension=0, tiled=True)
    late_ff, late_hidden, two_last = barrier((d_ff, hidden, two_last))
    grad_ff = mm_tn(normed_two, late_ff, jnp.bfloat16)

    def home_rows(value):
        return lax.psum_scatter(value, "fsdp", scatter_dimension=0, tiled=True)

    def by_owner(values):
        parts = [value.reshape(seq_size, z_size, chunk, value.shape[-1]) for value in values]
        return jnp.transpose(jnp.stack(parts, axis=0), (2, 1, 0, 3, 4))

    def own_columns(got):
        return as_wide(jnp.swapaxes(got, 0, 1).reshape(chunk, -1))

    ff_pair = by_owner((grad_ff,)).reshape(z_size * seq_size * chunk, 2 * ffw)
    half = count // 2
    mlp_odd = swap(mm(late_hidden[half:], down_w, jnp.bfloat16), "seq", 1)
    mlp_pair = split_pairs(mm(late_hidden[:half], down_w) + as_wide(mlp_odd))
    two_parts, ff_pair, mlp_pair = barrier((two_parts, ff_pair, mlp_pair))
    grad_normed_two = summed(two_parts)
    ff_home = home_rows(ff_pair)

    def gain_home(gain, pairs):
        total = sum(jnp.sum(grad * as_wide(as_low(weight)), axis=1) for grad, weight in pairs)
        return total / as_wide(as_low(gain))

    scaled_two = gain_two * grad_normed_two
    grad_mid = (
        live_col * as_wide(cotangent)
        + scale_two * scaled_two
        - resid_mid
        * scale_two
        * scale_two
        * scale_two
        * jnp.mean(scaled_two * resid_mid, axis=-1, keepdims=True)
    )
    grad_low = as_low(grad_mid)
    out_first = plane_first(grad_low)
    out_first, down_home = barrier((out_first, down_home))
    out_pieces = plane_all(plane_second(grad_low, out_first))
    out_pieces, mlp_pair = barrier((out_pieces, mlp_pair))
    mlp_parts = scatter_pairs(mlp_pair)
    grad_out_low, d_branch, direct, send = lru_back(out_pieces, out_w, act, bend, keep)
    backs = spread_z(send)
    grad_out = mm_tn(gated, grad_out_low, jnp.bfloat16)
    backs, grad_out = barrier((backs, grad_out))
    d_rec, d_in, du_part, du_last, heads, totals = whole(
        lru_grad_kernel,
        (live_count, first, pred, position),
        (
            summaries,
            backs,
            direct,
            keep,
            slow,
            bent_rec,
            into,
            bent_in,
            u_value,
            tails,
            vectors,
            rec_w,
            in_w,
        ),
        (
            shaped((count, width), jnp.bfloat16),
            shaped((count, width), jnp.bfloat16),
            shaped((count, width), jnp.bfloat16),
            shaped((blocks, 8, width)),
            shaped((blocks, 8, width)),
            shaped((8, width)),
        ),
        [
            pltpu.VMEM((tiles, every, LANES), jnp.float32),
            pltpu.VMEM((tiles, count, LANES), jnp.float32),
            pltpu.VMEM((BLOCK + 16, LANES), jnp.float32),
            pltpu.VMEM((8, 8, width), jnp.float32),
            pltpu.VMEM((BLOCK, width), jnp.float32),
        ],
        "lru_grad",
    )
    du_part, heads, totals, d_rec, d_in, mlp_parts, d_branch, ff_home = barrier(
        (du_part, heads, totals, d_rec, d_in, mlp_parts, d_branch, ff_home)
    )
    grad_out, ff_home = barrier((grad_out, ff_home))
    out_home = home_rows(grad_out)
    grad_branch = mm_tn(normed_one, d_branch, jnp.bfloat16)
    heads = edges(heads[:, 9 - TAPS :])
    full_rec, full_in = mm_tn(conv_low, d_rec), mm_tn(conv_low, d_in)
    du_part = du_part.reshape(blocks, BLOCK, width)
    (patch,) = whole(
        head_kernel,
        (succ,),
        (du_part[:, BLOCK - 16 :], du_last, heads),
        (shaped((blocks, 16, width), jnp.bfloat16),),
        [],
        "lru_heads",
    )
    d_input = lax.dynamic_update_slice(du_part, patch, (0, BLOCK - 16, 0)).reshape(count, width)
    branch_pack = by_owner((grad_branch,)).reshape(z_size * seq_size * chunk, width)
    d_input, full_rec, full_in, branch_pack, ff_home, out_home = barrier(
        (d_input, full_rec, full_in, branch_pack, ff_home, out_home)
    )
    ff_got = exchange(ff_home.reshape(seq_size, chunk, 2 * ffw))
    branch_home = home_rows(branch_pack)
    grad_input = mm_tn(normed_one, d_input, jnp.bfloat16)
    late_input, grad_input = barrier((d_input, grad_input))
    one_parts, one_last = scatter_plane(
        slot_product(
            (d_branch, late_input), lambda one, two: mm_nt(one, branch_w) + mm_nt(two, input_w)
        )
    )
    one_last, mlp_parts = barrier((one_last, mlp_parts))
    mixed = as_low(live_col * (resid_mid + summed(mlp_parts)))
    grad_normed_one = summed(one_parts)
    scaled_one = gain_one * grad_normed_one
    scale_one = lax.rsqrt(jnp.mean(resid_in * resid_in, axis=-1, keepdims=True) + NORM_EPSILON)
    tokens_grad = as_low(
        grad_mid
        + scale_one * scaled_one
        - resid_in
        * scale_one
        * scale_one
        * scale_one
        * jnp.mean(scaled_one * resid_in, axis=-1, keepdims=True)
    )

    def blocks_of(full, start):
        place = start + jnp.arange(width)[:, None] % gate_width
        fold = (place == jnp.arange(2 * gate_width)[None, :]).astype(jnp.float32)
        full = jnp.where(same, full, 0.0)
        return jnp.dot(full, fold, precision=lax.Precision.HIGHEST)

    totals = jnp.concatenate(
        [totals[:7], totals[7:] * (GATE_SCALE * jax.nn.sigmoid(-decay))[None]], axis=0
    )
    gates = blocks_of(full_rec, 0) + blocks_of(full_in, gate_width)
    owned = width // z_size
    gates = as_low(gates).reshape(z_size, owned, 2 * gate_width)
    totals = jnp.swapaxes(jnp.pad(totals, ((0, 8), (0, 0))).reshape(16, z_size, owned), 0, 1)
    totals = as_low(totals)
    lanes = max(width, 2 * gate_width)
    edge = seq_size * chunk
    pack = jnp.concatenate(
        [
            jnp.pad(part, ((0, 0), (0, 0), (0, lanes - part.shape[-1])))
            for part in (
                by_owner((grad_input,)).reshape(z_size, edge, width),
                gates,
                totals,
            )
        ],
        axis=1,
    )
    pack, branch_home = barrier((pack.reshape(z_size * pack.shape[1], lanes), branch_home))
    pack, ff_got = barrier((pack, ff_got))
    pack = home_rows(pack)
    grad_gate_home, grad_up_home = own_columns(ff_got[..., :ffw]), own_columns(ff_got[..., ffw:])
    grad_gain_two = gain_home(norm_gain2, ((grad_gate_home, w_gate), (grad_up_home, w_up)))
    grad_branch_home = own_columns(exchange(branch_home.reshape(seq_size, chunk, width)))
    grad_input_home = own_columns(exchange(pack[:edge, :width].reshape(seq_size, chunk, width)))
    grad_gain_one = gain_home(
        norm_gain1, ((grad_branch_home, w_branch), (grad_input_home, w_input))
    )
    gates = as_wide(pack[edge : edge + owned])
    totals = as_wide(pack[edge + owned :, :owned])
    return (
        mixed,
        tokens_grad,
        grad_gain_one,
        grad_branch_home,
        grad_input_home,
        totals[:TAPS],
        totals[4],
        gates[:, :gate_width],
        totals[5],
        gates[:, gate_width : 2 * gate_width],
        totals[6],
        totals[7],
        as_wide(out_home),
        grad_gain_two,
        grad_gate_home,
        grad_up_home,
        as_wide(down_home),
    )


def solution(mesh):
    row = P(("seq", "fsdp"))
    rows = P(("seq", "fsdp"), None)
    columns = P(None, ("seq", "fsdp"))
    return jax.shard_map(
        shards,
        mesh=mesh,
        in_specs=(
            rows,
            rows,
            P(),
            P(),
            P(),
            row,
            rows,
            rows,
            columns,
            row,
            rows,
            row,
            rows,
            row,
            row,
            rows,
            row,
            rows,
            rows,
            rows,
        ),
        out_specs=(
            rows,
            rows,
            row,
            rows,
            rows,
            columns,
            row,
            rows,
            row,
            rows,
            row,
            row,
            rows,
            row,
            rows,
            rows,
            rows,
        ),
        check_vma=False,
    )
```

```python
import jax
import jax.numpy as jnp
from jax import lax
from jax.experimental import pallas as pl
from jax.experimental.pallas import tpu as pltpu
from jax.sharding import PartitionSpec as P

BLOCK = 128
LANES = 128
TAPS = 4
UNROLL = 8
NORM_EPSILON = 1e-06
GATE_SCALE = 8.0
VMEM_LIMIT = 48 * 1024 * 1024
GELU_C = 0.7978845608028654
GELU_A = 0.044715
LIGHT = pl.CostEstimate(flops=1, transcendentals=0, bytes_accessed=1)


def as_low(values):
    return values.astype(jnp.bfloat16)


def as_wide(values):
    return values.astype(jnp.float32)


def mm(left, right, out=jnp.float32):
    return jnp.dot(left, right, preferred_element_type=jnp.float32).astype(out)


def mm_tn(left, right, out=jnp.float32):
    return lax.dot_general(
        left, right, (((0,), (0,)), ((), ())), preferred_element_type=jnp.float32
    ).astype(out)


def mm_nt(left, right, out=jnp.float32):
    return lax.dot_general(
        left, right, (((1,), (1,)), ((), ())), preferred_element_type=jnp.float32
    ).astype(out)


def swap(values, axis, flip):
    count = lax.axis_size(axis)
    return lax.ppermute(values, axis, [(i, i ^ flip) for i in range(count)])


barrier = lax.optimization_barrier


def plane_even(own):
    return [own] + [swap(own, "seq", k) for k in range(2, lax.axis_size("seq"), 2)]


def plane_first(own):
    count = lax.axis_size("seq")
    flips = (2, 4) if count == 8 else range(2, count, 2)
    return [swap(own, "seq", k) for k in flips]


def plane_second(own, first):
    even = [own, *first]
    if lax.axis_size("seq") == 8:
        half = own.shape[0] // 2
        near, side = first
        even.append((swap(side[:half], "seq", 2), swap(near[half:], "seq", 4)))
    return even


def plane_all(even):
    return list(even) + [jax.tree.map(lambda part: swap(part, "seq", 1), piece) for piece in even]


def slot_order():
    evens = lax.axis_size("seq") // 2
    return sorted(range(1, evens), key=lambda slot: -bin(slot).count("1")) + [0]


def scatter_plane(product):
    evens = lax.axis_size("seq") // 2
    order = slot_order()
    ready, pairs, after = {}, {}, None

    def odd(slot):
        value = as_low(product(evens + slot, after))
        ready[slot] = swap(value, "seq", 1)
        return value

    after = odd(order[0])
    for index, slot in enumerate(order[:-1]):
        after = odd(order[index + 1])
        after = product(slot, after) + as_wide(ready[slot])
        pairs[slot] = after
    if evens != 4:
        moved = [swap(as_low(pairs[slot]), "seq", 2 * slot) for slot in order[:-1]]
        return moved + [product(0, after) + as_wide(ready[0])], moved[0]
    near, side, far = (pairs[slot] for slot in (1, 2, 3))
    half = far.shape[0] // 2
    by_near = swap(as_low(jnp.concatenate([far[:half], near[:half]])), "seq", 2)
    by_side = swap(as_low(jnp.concatenate([far[half:], side[half:]])), "seq", 4)
    own = product(0, after) + as_wide(ready[0])
    by_near, by_side, last = barrier((by_near, by_side, own))
    near_low = swap(as_low(near[half:] + as_wide(by_side[:half])), "seq", 2)
    side_top = swap(as_low(side[:half] + as_wide(by_near[:half])), "seq", 4)
    return [last, (by_near[half:], near_low), (side_top, by_side[half:])], own


def split_pairs(pair):
    rows = pair.shape[0] // (lax.axis_size("seq") // 2)
    parts = [pair[slot * rows : (slot + 1) * rows] for slot in slot_order()]
    return [as_low(part) for part in parts[:-1]] + parts[-1:]


def scatter_pairs(parts):
    return [
        swap(part, "seq", 2 * slot) if slot else part for slot, part in zip(slot_order(), parts)
    ]


def slot_product(operands, multiply):
    rows = operands[0].shape[0] // lax.axis_size("seq")

    def product(slot, after):
        parts = tuple(operand[slot * rows : (slot + 1) * rows] for operand in operands)
        if after is not None:
            parts = barrier((*parts, after))[:-1]
        return multiply(*parts)

    return product


def summed(parts):
    total = None
    for part in parts:
        if isinstance(part, (tuple, list)):
            part = jnp.concatenate(part, axis=0)
        total = as_wide(part) if total is None else total + as_wide(part)
    return total


def gather_small(value, axis):
    value = value[None]
    bit = 1
    while bit < lax.axis_size(axis):
        other = swap(value, axis, bit)
        upper = (lax.axis_index(axis) // bit) % 2 == 1
        value = jnp.where(
            upper, jnp.concatenate([other, value]), jnp.concatenate([value, other])
        )
        bit *= 2
    return value


def spread_z(value):
    count = lax.axis_size("fsdp")
    return jnp.stack([value] + [swap(value, "fsdp", j) for j in range(1, count)], axis=0)


def gelu_parts(values):
    inner = GELU_C * (values + GELU_A * values * values * values)
    bend = jnp.tanh(inner)
    return (0.5 * values * (1.0 + bend), bend)


def gelu_slope(values, bend):
    return 0.5 * (1.0 + bend) + 0.5 * values * (1.0 - bend * bend) * GELU_C * (
        1.0 + 3.0 * GELU_A * values * values
    )


def expm1_small(values):
    series = values * (1.0 / 120.0) + 1.0 / 24.0
    for scale in (1.0 / 6.0, 0.5, 1.0):
        series = series * values + scale
    return series * values


def block_rows(index):
    return pl.ds(pl.multiple_of(index * BLOCK, BLOCK), BLOCK)


def lane_tiles(width):
    return [(low, min(LANES, width - low)) for low in range(0, width, LANES)]


def piece_specs(pieces, steps):
    specs = []
    chunk = pieces[0].shape[0] // steps
    block = (chunk, pieces[0].shape[1])
    last = steps // 2 - 1
    for piece in pieces:
        if isinstance(piece, (tuple, list)):
            specs.append(pl.BlockSpec(block, lambda i: (jnp.minimum(i, last), 0)))
            specs.append(pl.BlockSpec(block, lambda i: (jnp.maximum(i - last - 1, 0), 0)))
        else:
            specs.append(pl.BlockSpec(block, lambda i: (i, 0)))
    return specs


def piece_halves(pieces):
    return [len(piece) if isinstance(piece, (tuple, list)) else 1 for piece in pieces]


def joined_rows(refs, halves):
    upper = pl.program_id(0) < pl.num_programs(0) // 2
    rows, at = [], 0
    for parts in halves:
        value = refs[at][...]
        rows.append(value if parts == 1 else jnp.where(upper, value, refs[at + 1][...]))
        at += parts
    return jnp.concatenate(rows, axis=0)


def stack(pieces, name, gain=None, weights=(), gated=False, steps=4):
    count = len(pieces)
    halves, flat = piece_halves(pieces), jax.tree.leaves(pieces)
    rows, model = pieces[0].shape
    chunk = rows // steps
    extra = ([gain] if gain is not None else []) + list(weights)

    def kernel(*refs):
        values = joined_rows(refs[: len(flat)], halves)
        refs = refs[len(flat) :]
        if gain is not None:
            gain_ref, refs = refs[0], refs[1:]
            wide = values.astype(jnp.float32)
            scale = lax.rsqrt(jnp.mean(wide * wide, axis=-1, keepdims=True) + NORM_EPSILON)
            values = (wide * scale * gain_ref[...]).astype(jnp.bfloat16)
        weight_refs, refs = refs[: len(weights)], refs[len(weights) :]
        refs[0][...] = values.reshape(count, chunk, model)
        for weight_ref, out_ref in zip(weight_refs, refs[1:]):
            out = jnp.dot(values, weight_ref[...], preferred_element_type=jnp.float32)
            if not gated:
                out_ref[...] = out.reshape(count, chunk, out.shape[1])
        if gated:
            gate, up = out[:, : out.shape[1] // 2], out[:, out.shape[1] // 2 :]
            act, bend = gelu_parts(gate)
            for out_ref, out in zip(refs[1:], (act, up * gelu_slope(gate, bend), act * up)):
                out_ref[...] = out.reshape(count, chunk, out.shape[1]).astype(out_ref.dtype)

    widths = [weight.shape[1] for weight in weights]
    if gated:
        widths = [widths[0] // 2] * 2
    outs = [shaped((count, rows, model), jnp.bfloat16)] + [shaped((count, rows, w)) for w in widths]
    if gated:
        outs.append(shaped((count, rows, widths[0]), jnp.bfloat16))
    done = pl.pallas_call(
        kernel,
        grid=(steps,),
        in_specs=piece_specs(pieces, steps) + [pl.BlockSpec(e.shape, lambda i: (0, 0)) for e in extra],
        out_specs=[pl.BlockSpec((count, chunk, o.shape[2]), lambda i: (0, i, 0)) for o in outs],
        out_shape=outs,
        compiler_params=pltpu.CompilerParams(vmem_limit_bytes=VMEM_LIMIT),
        cost_estimate=LIGHT,
        name=name,
    )(*flat, *extra)
    return [out.reshape(count * rows, out.shape[2]) for out in done]


def ff_backward(top, down_w, act, bend, steps=8):
    chunk = top.shape[0] // steps
    ffw, model = down_w.shape

    def kernel(top_ref, down_ref, act_ref, bend_ref, out_ref):
        grad = lax.dot_general(
            top_ref[...], down_ref[...], (((1,), (1,)), ((), ())), preferred_element_type=jnp.float32
        )
        out_ref[:, :ffw] = (grad * bend_ref[...]).astype(jnp.bfloat16)
        out_ref[:, ffw:] = (grad * act_ref[...]).astype(jnp.bfloat16)

    block = pl.BlockSpec((chunk, ffw), lambda i: (i, 0))
    return pl.pallas_call(
        kernel,
        grid=(steps,),
        in_specs=[
            pl.BlockSpec((chunk, model), lambda i: (i, 0)),
            pl.BlockSpec((ffw, model), lambda i: (0, 0)),
            block,
            block,
        ],
        out_specs=pl.BlockSpec((chunk, 2 * ffw), lambda i: (i, 0)),
        out_shape=shaped((top.shape[0], 2 * ffw), jnp.bfloat16),
        compiler_params=pltpu.CompilerParams(vmem_limit_bytes=VMEM_LIMIT),
        cost_estimate=LIGHT,
        name="ff_backward",
    )(top, down_w, act, bend)


def project(rows, weight, name, steps=8):
    chunk = rows.shape[0] // steps
    width = weight.shape[1]

    def kernel(rows_ref, weight_ref, out_ref):
        out_ref[...] = jnp.dot(rows_ref[...], weight_ref[...], preferred_element_type=jnp.float32)

    return pl.pallas_call(
        kernel,
        grid=(steps,),
        in_specs=[
            pl.BlockSpec((chunk, rows.shape[1]), lambda i: (i, 0)),
            pl.BlockSpec(weight.shape, lambda i: (0, 0)),
        ],
        out_specs=pl.BlockSpec((chunk, width), lambda i: (i, 0)),
        out_shape=shaped((rows.shape[0], width)),
        compiler_params=pltpu.CompilerParams(vmem_limit_bytes=VMEM_LIMIT),
        cost_estimate=pl.CostEstimate(
            flops=2 * rows.size * width,
            transcendentals=0,
            bytes_accessed=2 * rows.size + 4 * rows.shape[0] * width,
        ),
        name=name,
    )(rows, weight)


def dead_mask(rows, live_count):
    return (rows < live_count).astype(jnp.float32)


def lru_forward_kernel(
    live_ref,
    first_ref,
    pred_ref,
    u_ref,
    tail_ref,
    vec_ref,
    rec_ref,
    in_ref,
    xc_ref,
    keep_ref,
    drive_ref,
    rate_ref,
    slope_ref,
    into_ref,
    bent_ref,
    sum_ref,
    ext_ref,
):
    blocks = u_ref.shape[0] // BLOCK
    tiles = lane_tiles(u_ref.shape[1])
    rows = lax.broadcasted_iota(jnp.int32, (BLOCK, LANES), 0)

    def block(index, carry):
        at = block_rows(index)
        first = first_ref[index]
        pred = pred_ref[index]
        live = dead_mask(rows, live_ref[index])
        before = jnp.maximum(pred, 0)
        joined = jnp.where((pred >= 0) & (first == 0), 1.0, 0.0)
        for low, size in tiles:
            lanes = slice(low, low + size)
            u_value = u_ref[at, lanes]
            ext_ref[0:8, :size] = tail_ref[before, :, lanes] * joined
            ext_ref[8 : 8 + BLOCK, :size] = u_value
            later = vec_ref[1:2, lanes] * ext_ref[7 : 7 + BLOCK, :size]
            for tap in range(2, TAPS):
                later = later + vec_ref[tap : tap + 1, lanes] * ext_ref[8 - tap : 8 - tap + BLOCK, :size]
            conv = vec_ref[4:5, lanes] + vec_ref[0:1, lanes] * u_value + later * live[:, :size]
            xc_ref[at, lanes] = conv.astype(jnp.bfloat16)
        low_rows = xc_ref[at, :]
        pre_rec = jnp.dot(low_rows, rec_ref[...], preferred_element_type=jnp.float32)
        pre_in = jnp.dot(low_rows, in_ref[...], preferred_element_type=jnp.float32)
        for tile, (low, size) in enumerate(tiles):
            lanes = slice(low, low + size)
            rate = jax.nn.sigmoid(pre_rec[:, lanes] + vec_ref[5:6, lanes])
            entry = jax.nn.sigmoid(pre_in[:, lanes] + vec_ref[6:7, lanes])
            minus = expm1_small(rate * vec_ref[7:8, lanes])
            twice = minus * (2.0 + minus)
            into = jnp.sqrt(-twice) * entry
            drive = into * low_rows[:, lanes].astype(jnp.float32)
            rate_ref[tile, at, :size] = rate
            keep_ref[tile, at, :size] = (1.0 + minus) * live[:, :size]
            drive_ref[tile, at, :size] = drive
            slope_ref[tile, at, :size] = drive + drive / twice
            into_ref[tile, at, :size] = into
            bent_ref[tile, at, :size] = drive * (1.0 - entry)

        @pl.when(first > 0)
        def _():
            top = pl.ds(pl.multiple_of(index * BLOCK, BLOCK), 8)
            after = (rows[:8] > 0).astype(jnp.float32)
            for tile in range(len(tiles)):
                keep_ref[tile, top, :] = keep_ref[tile, top, :] * after

        return carry

    lax.fori_loop(0, blocks, block, 0)

    def step(place, carry):
        at = pl.ds(place, blocks, stride=BLOCK)
        after = []
        for tile, (total, state) in enumerate(carry):
            keep = keep_ref[tile, at, :]
            after.append((total * keep, keep * state + drive_ref[tile, at, :]))
        return tuple(after)

    ones = jnp.ones((blocks, LANES), jnp.float32)
    start = tuple((ones, jnp.zeros_like(ones)) for _ in tiles)
    ends = lax.fori_loop(0, BLOCK, step, start, unroll=UNROLL)
    for tile, (total, state) in enumerate(ends):
        sum_ref[0, tile] = total
        sum_ref[1, tile] = state


def lru_state_kernel(
    pos_ref,
    all_ref,
    keep_ref,
    drive_ref,
    rate_ref,
    slope_ref,
    ypre_ref,
    vec_ref,
    hy_ref,
    act_ref,
    bend_ref,
    slow_ref,
    rec_ref,
    line_ref,
    h_ref,
    ext_ref,
):
    tiles = lane_tiles(ypre_ref.shape[1])
    turns, _, _, blocks, _ = all_ref.shape

    def chain(place, states):
        slot = pos_ref[place]
        turn, index = slot // blocks, slot % blocks
        after = []
        for tile, state in enumerate(states):
            line_ref[tile, pl.ds(slot, 1), :] = state
            keep = all_ref[turn, 0, tile, pl.ds(index, 1), :]
            after.append(keep * state + all_ref[turn, 1, tile, pl.ds(index, 1), :])
        return tuple(after)

    zero = jnp.zeros((1, LANES), jnp.float32)
    lax.fori_loop(0, turns * blocks, chain, tuple(zero for _ in tiles))
    def step(place, states):
        at = pl.ds(place, blocks, stride=BLOCK)
        after = []
        for tile, state in enumerate(states):
            state = keep_ref[tile, at, :] * state + drive_ref[tile, at, :]
            h_ref[tile, at, :] = state
            after.append(state)
        return tuple(after)

    start = tuple(line_ref[tile, 0:blocks, :] for tile in range(len(tiles)))
    lax.fori_loop(0, BLOCK, step, start, unroll=UNROLL)

    def block(index, carry):
        at = block_rows(index)
        for tile, (low, size) in enumerate(tiles):
            lanes = slice(low, low + size)
            h_value = h_ref[tile, at, :size]
            value = ypre_ref[at, lanes]
            act, bend = gelu_parts(value)
            hy_ref[at, lanes] = (h_value * act).astype(jnp.bfloat16)
            act_ref[tile, at, :size] = act
            bend_ref[tile, at, :size] = h_value * gelu_slope(value, bend)
            ext_ref[7:8, :size] = line_ref[tile, pl.ds(index, 1), :size]
            ext_ref[8 : 8 + BLOCK, :size] = h_value
            rate = rate_ref[tile, at, :size]
            slow = rate * (
                keep_ref[tile, at, :size] * ext_ref[7 : 7 + BLOCK, :size]
                + slope_ref[tile, at, :size]
            )
            slow_ref[tile, at, :size] = slow
            rec_ref[tile, at, :size] = slow * (1.0 - rate) * vec_ref[7:8, lanes]
        return carry

    lax.fori_loop(0, blocks, block, 0)


def lru_back(pieces, out_w, act, bend, keep, steps=4):
    count = len(pieces)
    halves, flat = piece_halves(pieces), jax.tree.leaves(pieces)
    rows, model = pieces[0].shape
    width = out_w.shape[0]
    tiles = lane_tiles(width)
    chunk = rows // steps
    blocks = count * rows // BLOCK

    def kernel(*refs):
        values = joined_rows(refs[: len(flat)], halves)
        w_ref, act_ref, bend_ref, keep_ref, out_ref, dy_ref, dh_ref, send_ref = refs[len(flat) :]
        here = pl.program_id(0)
        out_ref[...] = values.reshape(count, chunk, model)
        grads = lax.dot_general(
            values, w_ref[...], (((1,), (1,)), ((), ())), preferred_element_type=jnp.float32
        )
        for slot in range(count):
            span = pl.ds(pl.multiple_of(slot * rows + here * chunk, chunk), chunk)
            for tile, (low, size) in enumerate(tiles):
                lanes = slice(low, low + size)
                grad = grads[slot * chunk : (slot + 1) * chunk, lanes]
                dy_ref[slot, :, lanes] = (grad * bend_ref[tile, slot, :, :size]).astype(jnp.bfloat16)
                dh_ref[tile, span, :size] = grad * act_ref[tile, slot, :, :size]

        @pl.when(here == steps - 1)
        def _():
            def step(turn, carry):
                at = pl.ds(BLOCK - 1 - turn, blocks, stride=BLOCK)
                return tuple(
                    keep_ref[tile, at, :] * (dh_ref[tile, at, :] + value)
                    for tile, value in enumerate(carry)
                )

            zero = jnp.zeros((blocks, LANES), jnp.float32)
            ends = lax.fori_loop(0, BLOCK, step, tuple(zero for _ in tiles), unroll=UNROLL)
            for tile, value in enumerate(ends):
                send_ref[tile] = value

    depth = len(tiles)
    total = count * rows
    out, dy, dh, send = pl.pallas_call(
        kernel,
        grid=(steps,),
        in_specs=piece_specs(pieces, steps)
        + [
            pl.BlockSpec((width, model), lambda i: (0, 0)),
            pl.BlockSpec((depth, count, chunk, LANES), lambda i: (0, 0, i, 0)),
            pl.BlockSpec((depth, count, chunk, LANES), lambda i: (0, 0, i, 0)),
            pl.BlockSpec((depth, total, LANES), lambda i: (0, 0, 0)),
        ],
        out_specs=[
            pl.BlockSpec((count, chunk, model), lambda i: (0, i, 0)),
            pl.BlockSpec((count, chunk, width), lambda i: (0, i, 0)),
            pl.BlockSpec((depth, total, LANES), lambda i: (0, 0, 0)),
            pl.BlockSpec((depth, blocks, LANES), lambda i: (0, 0, 0)),
        ],
        out_shape=[
            shaped((count, rows, model), jnp.bfloat16),
            shaped((count, rows, width), jnp.bfloat16),
            shaped((depth, total, LANES)),
            shaped((depth, blocks, LANES)),
        ],
        compiler_params=pltpu.CompilerParams(vmem_limit_bytes=VMEM_LIMIT),
        cost_estimate=LIGHT,
        name="lru_back",
    )(
        *flat,
        out_w,
        act.reshape(depth, count, rows, LANES),
        bend.reshape(depth, count, rows, LANES),
        keep,
    )
    return out.reshape(total, model), dy.reshape(total, width), dh, send


def fold_rows(values):
    return values.reshape(BLOCK // 8, 8, values.shape[1]).sum(axis=0)


def lru_grad_kernel(
    live_ref,
    first_ref,
    pred_ref,
    pos_ref,
    all_ref,
    back_ref,
    dh_ref,
    keep_ref,
    slow_ref,
    bent_rec_ref,
    into_ref,
    bent_in_ref,
    u_ref,
    tail_ref,
    vec_ref,
    rec_ref,
    in_ref,
    drec_ref,
    din_ref,
    du_ref,
    last_ref,
    head_ref,
    total_ref,
    line_ref,
    g_ref,
    ext_ref,
    acc_ref,
    direct_ref,
):
    blocks = u_ref.shape[0] // BLOCK
    width = u_ref.shape[1]
    tiles = lane_tiles(width)
    every = back_ref.shape[0] * blocks
    rows = lax.broadcasted_iota(jnp.int32, (BLOCK, LANES), 0)

    def chain(count, carry):
        slot = pos_ref[every - 1 - count]
        turn, index = slot // blocks, slot % blocks
        after = []
        for tile, value in enumerate(carry):
            line_ref[tile, pl.ds(slot, 1), :] = value
            keep = all_ref[turn, 0, tile, pl.ds(index, 1), :]
            after.append(keep * value + back_ref[turn, tile, pl.ds(index, 1), :])
        return tuple(after)

    zero = jnp.zeros((1, LANES), jnp.float32)
    lax.fori_loop(0, every, chain, tuple(zero for _ in tiles))

    def step(turn, carry):
        at = pl.ds(BLOCK - 1 - turn, blocks, stride=BLOCK)
        after = []
        for tile, value in enumerate(carry):
            grad = dh_ref[tile, at, :] + value
            g_ref[tile, at, :] = grad
            after.append(keep_ref[tile, at, :] * grad)
        return tuple(after)

    start = tuple(line_ref[tile, 0:blocks, :] for tile in range(len(tiles)))
    lax.fori_loop(0, BLOCK, step, start, unroll=UNROLL)
    acc_ref[...] = jnp.zeros_like(acc_ref)
    contract = (((1,), (1,)), ((), ()))

    def block(index, carry):
        at = block_rows(index)
        first = first_ref[index]
        pred = pred_ref[index]
        live = dead_mask(rows, live_ref[index])
        before = jnp.maximum(pred, 0)
        joined = jnp.where((pred >= 0) & (first == 0), 1.0, 0.0)
        for tile, (low, size) in enumerate(tiles):
            lanes = slice(low, low + size)
            grad = g_ref[tile, at, :size]
            acc_ref[7, :, lanes] += fold_rows(grad * slow_ref[tile, at, :size])
            d_rec = (grad * bent_rec_ref[tile, at, :size]).astype(jnp.bfloat16)
            d_in = (grad * bent_in_ref[tile, at, :size]).astype(jnp.bfloat16)
            drec_ref[at, lanes] = d_rec
            din_ref[at, lanes] = d_in
            acc_ref[5, :, lanes] += fold_rows(d_rec.astype(jnp.float32))
            acc_ref[6, :, lanes] += fold_rows(d_in.astype(jnp.float32))
            direct_ref[:, lanes] = grad * into_ref[tile, at, :size]
        direct_ref[...] += lax.dot_general(
            drec_ref[at, :], rec_ref[...], contract, preferred_element_type=jnp.float32
        ) + lax.dot_general(
            din_ref[at, :], in_ref[...], contract, preferred_element_type=jnp.float32
        )
        for low, size in tiles:
            lanes = slice(low, low + size)
            dxc = direct_ref[:, lanes]
            u_value = u_ref[at, lanes]
            ext_ref[0:8, :size] = tail_ref[before, :, lanes] * joined
            ext_ref[8 : 8 + BLOCK, :size] = u_value
            acc_ref[4, :, lanes] += fold_rows(dxc)
            acc_ref[0, :, lanes] += fold_rows(dxc * u_value)
            part = dxc * live[:, :size]
            for tap in range(1, TAPS):
                acc_ref[tap, :, lanes] += fold_rows(part * ext_ref[8 - tap : 8 - tap + BLOCK, :size])
            zero_tile = jnp.zeros((8, size), jnp.float32)
            ext_ref[0:8, :size] = zero_tile
            ext_ref[8 : 8 + BLOCK, :size] = part
            ext_ref[8 + BLOCK : 16 + BLOCK, :size] = zero_tile
            du_value = dxc * vec_ref[0:1, lanes]
            head = zero_tile
            for tap in range(1, TAPS):
                weight = vec_ref[tap : tap + 1, lanes]
                du_value = du_value + weight * ext_ref[8 + tap : 8 + tap + BLOCK, :size]
                head = head + weight * ext_ref[tap : tap + 8, :size]
            du_ref[at, lanes] = du_value.astype(jnp.bfloat16)
            last_ref[index, :, lanes] = du_value[BLOCK - 8 :]
            head_ref[index, :, lanes] = head * joined
        return carry

    lax.fori_loop(0, blocks, block, 0)
    for index in range(8):
        total_ref[index : index + 1, :] = jnp.sum(acc_ref[index], axis=0, keepdims=True)


def head_kernel(succ_ref, prev_ref, last_ref, head_ref, out_ref):
    blocks = last_ref.shape[0]

    def block(index, carry):
        succ = succ_ref[index]
        head = head_ref[jnp.maximum(succ, 0)]
        tail = last_ref[index] + jnp.where(succ >= 0, head, jnp.zeros_like(head))
        out_ref[index, :8, :] = prev_ref[index, :8, :]
        out_ref[index, 8:, :] = tail.astype(jnp.bfloat16)
        return carry

    lax.fori_loop(0, blocks, block, 0)


def shaped(shape, dtype=jnp.float32):
    return jax.ShapeDtypeStruct(shape, dtype)


def whole(kernel, scalars, arrays, outs, scratch, name):
    specs = [pl.BlockSpec(memory_space=pltpu.SMEM)] * len(scalars)
    specs += [pl.BlockSpec(memory_space=pltpu.VMEM)] * len(arrays)
    return pl.pallas_call(
        kernel,
        out_shape=outs,
        in_specs=specs,
        out_specs=[pl.BlockSpec(memory_space=pltpu.VMEM)] * len(outs),
        scratch_shapes=scratch,
        compiler_params=pltpu.CompilerParams(vmem_limit_bytes=VMEM_LIMIT),
        cost_estimate=LIGHT,
        name=name,
    )(*scalars, *arrays)


def shards(
    tokens,
    cotangent,
    lengths,
    offsets,
    deal,
    norm_gain1,
    w_branch,
    w_input,
    conv_kernel,
    conv_bias,
    gate_rec,
    bias_rec,
    gate_in,
    bias_in,
    decay_param,
    w_out,
    norm_gain2,
    w_gate,
    w_up,
    w_down,
):
    seq_size, z_size = lax.axis_size("seq"), lax.axis_size("fsdp")
    seq_at, z_at = lax.axis_index("seq"), lax.axis_index("fsdp")
    rows_here, model = tokens.shape
    blocks_here = rows_here // BLOCK
    blocks = seq_size * blocks_here
    every = blocks * z_size
    count = rows_here * seq_size
    width = w_branch.shape[1] // seq_size
    ffw = w_gate.shape[1] // seq_size
    chunk = w_branch.shape[0]
    gate_width = gate_rec.shape[1]
    groups = width // gate_width
    tiles = len(lane_tiles(width))
    tiled = shaped((tiles, count, LANES))

    order = jnp.array([k for k in range(seq_size) if k % 2 == 0] + [k for k in range(seq_size) if k % 2], jnp.int32)
    source = jnp.bitwise_xor(order, seq_at)
    flips = jnp.bitwise_xor(jnp.arange(z_size, dtype=jnp.int32), z_at)
    stored = (source[None, :, None] * z_size + flips[:, None, None]) * blocks_here
    stored = (stored + jnp.arange(blocks_here, dtype=jnp.int32)[None, None, :]).reshape(every)
    logical = deal[stored]
    places = jnp.arange(every, dtype=jnp.int32)
    at_place = logical[None, :] == places[:, None]
    position = jnp.sum(jnp.where(at_place, places[None, :], 0), axis=1)
    mine = logical[:blocks]

    def place_of(wanted):
        hit = logical[None, :] == wanted[:, None]
        return jnp.sum(jnp.where(hit, places[None, :] + 1, 0), axis=1) - 1

    pred = place_of(mine - 1)
    succ = place_of(mine + 1)
    left_over = lengths[None, :] - (mine[:, None] - offsets[None, :]) * BLOCK
    inside = (mine[:, None] >= offsets[None, :]) & (left_over > 0)
    live_count = jnp.max(jnp.where(inside, jnp.minimum(left_over, BLOCK), 0), axis=1)
    first = jnp.any(inside & (mine[:, None] == offsets[None, :]), axis=1).astype(jnp.int32)
    own_live = live_count[:blocks_here]
    live_col = (
        jnp.arange(BLOCK, dtype=jnp.int32)[None, :] < own_live[:, None]
    ).astype(jnp.float32).reshape(rows_here, 1)

    def columns(weight):
        return jnp.swapaxes(as_low(weight).reshape(chunk, seq_size, -1), 0, 1)

    def exchange(value):
        return lax.all_to_all(value, "seq", 0, 0, tiled=True)

    def gather_rows(value):
        return lax.all_gather(value, "fsdp", axis=0, tiled=True)

    def gather_columns(value):
        got = lax.all_gather(value, "fsdp", axis=0, tiled=False)
        return jnp.swapaxes(got, 0, 1).reshape(-1, value.shape[-1])

    gains = gather_small(as_low(jnp.stack([norm_gain1, norm_gain2])), "seq")
    mix = jnp.stack([columns(w_input), columns(w_branch)], axis=1)
    mix, own_tokens, gains = barrier((mix, tokens, gains))
    x_first = plane_first(own_tokens)
    out_w = gather_rows(as_low(w_out))
    mix = exchange(mix)
    params = [conv_kernel, conv_bias[None], bias_rec[None], bias_in[None], decay_param[None]]
    gains = jnp.pad(gains.reshape(2 * seq_size, chunk), ((0, 0), (0, width // z_size - chunk)))
    params = jnp.concatenate([as_low(part) for part in params] + [gains], axis=0).T
    small = jnp.concatenate([as_low(gate_rec), as_low(gate_in), params], axis=1)
    small = gather_small(small, "fsdp")
    mix, out_w, small, x_first = barrier((mix, out_w, small, x_first))
    x_even = plane_second(own_tokens, x_first)
    input_w = gather_columns(mix[:, 0])
    branch_w = gather_columns(mix[:, 1])
    x_pieces = plane_all(x_even)
    gains = small[:, :chunk, 2 * gate_width + 8 :].reshape(z_size, chunk, seq_size, 2)
    gains = as_wide(jnp.transpose(gains, (3, 2, 0, 1)).reshape(2, model))
    gain_one, gain_two = gains[:1], gains[1:]
    small = small.reshape(width, -1)

    same = jnp.arange(width)[:, None] // gate_width == jnp.arange(width)[None, :] // gate_width

    def diagonal(part):
        return jnp.where(same, jnp.tile(part, (1, groups)), jnp.zeros((), jnp.bfloat16))

    vectors = as_wide(small[:, 2 * gate_width : 2 * gate_width + 8]).T
    decay = vectors[7]
    vectors = jnp.concatenate([vectors[:7], -GATE_SCALE * jax.nn.softplus(-decay)[None]], axis=0)
    ff = jnp.concatenate([columns(w_gate), columns(w_up)], axis=2)
    top_own = as_low(live_col * as_wide(cotangent))
    x_pieces, ff, top_own = barrier((x_pieces, ff, top_own))
    ff = exchange(ff)
    x_pieces, top_own = barrier((x_pieces, top_own))
    top_even = plane_even(top_own)

    normed_one, u_value = stack(x_pieces, "norm_one", gain_one, (input_w,))
    u_value, gates_in = barrier((u_value, small))
    rec_w = diagonal(gates_in[:, :gate_width])
    in_w = diagonal(gates_in[:, gate_width : 2 * gate_width])
    down_w = gather_rows(as_low(w_down))

    def edges(rows):
        rows = spread_z(as_low(barrier(rows)).reshape(blocks * (TAPS - 1), width))
        rows = as_wide(rows).reshape(every, TAPS - 1, width)
        return jnp.pad(rows, ((0, 0), (9 - TAPS, 0), (0, 0)))

    tails = edges(u_value.reshape(blocks, BLOCK, width)[:, BLOCK - TAPS + 1 :])
    tails, rec_w, in_w, vectors, ff = barrier((tails, rec_w, in_w, vectors, ff))
    ff_w = gather_columns(ff)
    conv_low, keep, drive, rate, slope, into, bent_in, summary = whole(
        lru_forward_kernel,
        (live_count, first, pred),
        (u_value, tails, vectors, rec_w, in_w),
        (
            shaped((count, width), jnp.bfloat16),
            *[tiled] * 6,
            shaped((2, tiles, blocks, LANES)),
        ),
        [pltpu.VMEM((BLOCK + 8, LANES), jnp.float32)],
        "lru_forward",
    )
    branch_pre = project(normed_one, branch_w, "branch_pre")
    summaries = spread_z(summary)
    summaries, branch_pre, top_even = barrier((summaries, branch_pre, top_even))
    gated, act, bend, slow, bent_rec = whole(
        lru_state_kernel,
        (position,),
        (summaries, keep, drive, rate, slope, branch_pre, vectors),
        (shaped((count, width), jnp.bfloat16), *[tiled] * 4),
        [
            pltpu.VMEM((tiles, every, LANES), jnp.float32),
            pltpu.VMEM((tiles, count, LANES), jnp.float32),
            pltpu.VMEM((BLOCK + 8, LANES), jnp.float32),
        ],
        "lru_state",
    )
    resid_in = as_wide(tokens)
    mid_parts, mid_last = scatter_plane(slot_product((gated,), lambda rows: mm(rows, out_w)))
    top_even, mid_last = barrier((top_even, mid_last))
    (top_low,) = stack(plane_all(top_even), "stack_top")
    mid_parts, top_low = barrier((mid_parts, top_low))
    resid_mid = resid_in + summed(mid_parts)
    scale_two = lax.rsqrt(jnp.mean(resid_mid * resid_mid, axis=-1, keepdims=True) + NORM_EPSILON)
    own_two = as_low(resid_mid * scale_two * gain_two)
    two_first = plane_first(own_two)
    two_first, ff_w = barrier((two_first, ff_w))
    normed_two, ff_act, ff_bend, hidden = stack(
        plane_all(plane_second(own_two, two_first)), "ff_forward", None, (ff_w,), True
    )
    grad_down = mm_tn(hidden, top_low, jnp.bfloat16)
    ff_act, ff_bend, grad_down, down_w = barrier((ff_act, ff_bend, grad_down, down_w))
    d_ff = ff_backward(top_low, down_w, ff_act, ff_bend)
    two_parts, two_last = scatter_plane(
        slot_product((d_ff,), lambda rows: mm_nt(rows, ff_w))
    )
    down_home = lax.psum_scatter(grad_down, "fsdp", scatter_dimension=0, tiled=True)
    late_ff, late_hidden, two_last = barrier((d_ff, hidden, two_last))
    grad_ff = mm_tn(normed_two, late_ff, jnp.bfloat16)

    def home_rows(value):
        return lax.psum_scatter(value, "fsdp", scatter_dimension=0, tiled=True)

    def by_owner(values):
        parts = [value.reshape(seq_size, z_size, chunk, value.shape[-1]) for value in values]
        return jnp.transpose(jnp.stack(parts, axis=0), (2, 1, 0, 3, 4))

    def own_columns(got):
        return as_wide(jnp.swapaxes(got, 0, 1).reshape(chunk, -1))

    ff_pair = by_owner((grad_ff,)).reshape(z_size * seq_size * chunk, 2 * ffw)
    half = count // 2
    mlp_odd = swap(mm(late_hidden[half:], down_w, jnp.bfloat16), "seq", 1)
    mlp_pair = split_pairs(mm(late_hidden[:half], down_w) + as_wide(mlp_odd))
    two_parts, ff_pair, mlp_pair = barrier((two_parts, ff_pair, mlp_pair))
    grad_normed_two = summed(two_parts)
    ff_home = home_rows(ff_pair)

    def gain_home(gain, pairs):
        total = sum(jnp.sum(grad * as_wide(as_low(weight)), axis=1) for grad, weight in pairs)
        return total / as_wide(as_low(gain))

    scaled_two = gain_two * grad_normed_two
    grad_mid = (
        live_col * as_wide(cotangent)
        + scale_two * scaled_two
        - resid_mid
        * scale_two
        * scale_two
        * scale_two
        * jnp.mean(scaled_two * resid_mid, axis=-1, keepdims=True)
    )
    grad_low = as_low(grad_mid)
    out_first = plane_first(grad_low)
    out_first, down_home = barrier((out_first, down_home))
    out_pieces = plane_all(plane_second(grad_low, out_first))
    out_pieces, mlp_pair = barrier((out_pieces, mlp_pair))
    mlp_parts = scatter_pairs(mlp_pair)
    grad_out_low, d_branch, direct, send = lru_back(out_pieces, out_w, act, bend, keep)
    backs = spread_z(send)
    grad_out = mm_tn(gated, grad_out_low, jnp.bfloat16)
    backs, grad_out = barrier((backs, grad_out))
    d_rec, d_in, du_part, du_last, heads, totals = whole(
        lru_grad_kernel,
        (live_count, first, pred, position),
        (
            summaries,
            backs,
            direct,
            keep,
            slow,
            bent_rec,
            into,
            bent_in,
            u_value,
            tails,
            vectors,
            rec_w,
            in_w,
        ),
        (
            shaped((count, width), jnp.bfloat16),
            shaped((count, width), jnp.bfloat16),
            shaped((count, width), jnp.bfloat16),
            shaped((blocks, 8, width)),
            shaped((blocks, 8, width)),
            shaped((8, width)),
        ),
        [
            pltpu.VMEM((tiles, every, LANES), jnp.float32),
            pltpu.VMEM((tiles, count, LANES), jnp.float32),
            pltpu.VMEM((BLOCK + 16, LANES), jnp.float32),
            pltpu.VMEM((8, 8, width), jnp.float32),
            pltpu.VMEM((BLOCK, width), jnp.float32),
        ],
        "lru_grad",
    )
    du_part, heads, totals, d_rec, d_in, mlp_parts, d_branch, ff_home = barrier(
        (du_part, heads, totals, d_rec, d_in, mlp_parts, d_branch, ff_home)
    )
    grad_out, ff_home = barrier((grad_out, ff_home))
    out_home = home_rows(grad_out)
    grad_branch = mm_tn(normed_one, d_branch, jnp.bfloat16)
    heads = edges(heads[:, 9 - TAPS :])
    full_rec, full_in = mm_tn(conv_low, d_rec), mm_tn(conv_low, d_in)
    du_part = du_part.reshape(blocks, BLOCK, width)
    (patch,) = whole(
        head_kernel,
        (succ,),
        (du_part[:, BLOCK - 16 :], du_last, heads),
        (shaped((blocks, 16, width), jnp.bfloat16),),
        [],
        "lru_heads",
    )
    d_input = lax.dynamic_update_slice(du_part, patch, (0, BLOCK - 16, 0)).reshape(count, width)
    branch_pack = by_owner((grad_branch,)).reshape(z_size * seq_size * chunk, width)
    d_input, full_rec, full_in, branch_pack, ff_home, out_home = barrier(
        (d_input, full_rec, full_in, branch_pack, ff_home, out_home)
    )
    ff_got = exchange(ff_home.reshape(seq_size, chunk, 2 * ffw))
    branch_home = home_rows(branch_pack)
    grad_input = mm_tn(normed_one, d_input, jnp.bfloat16)
    late_input, grad_input = barrier((d_input, grad_input))
    one_parts, one_last = scatter_plane(
        slot_product(
            (d_branch, late_input), lambda one, two: mm_nt(one, branch_w) + mm_nt(two, input_w)
        )
    )
    one_last, mlp_parts = barrier((one_last, mlp_parts))
    mixed = as_low(live_col * (resid_mid + summed(mlp_parts)))
    grad_normed_one = summed(one_parts)
    scaled_one = gain_one * grad_normed_one
    scale_one = lax.rsqrt(jnp.mean(resid_in * resid_in, axis=-1, keepdims=True) + NORM_EPSILON)
    tokens_grad = as_low(
        grad_mid
        + scale_one * scaled_one
        - resid_in
        * scale_one
        * scale_one
        * scale_one
        * jnp.mean(scaled_one * resid_in, axis=-1, keepdims=True)
    )

    def blocks_of(full, start):
        place = start + jnp.arange(width)[:, None] % gate_width
        fold = (place == jnp.arange(2 * gate_width)[None, :]).astype(jnp.float32)
        full = jnp.where(same, full, 0.0)
        return jnp.dot(full, fold, precision=lax.Precision.HIGHEST)

    totals = jnp.concatenate(
        [totals[:7], totals[7:] * (GATE_SCALE * jax.nn.sigmoid(-decay))[None]], axis=0
    )
    gates = blocks_of(full_rec, 0) + blocks_of(full_in, gate_width)
    owned = width // z_size
    gates = as_low(gates).reshape(z_size, owned, 2 * gate_width)
    totals = jnp.swapaxes(jnp.pad(totals, ((0, 8), (0, 0))).reshape(16, z_size, owned), 0, 1)
    totals = as_low(totals)
    lanes = max(width, 2 * gate_width)
    edge = seq_size * chunk
    pack = jnp.concatenate(
        [
            jnp.pad(part, ((0, 0), (0, 0), (0, lanes - part.shape[-1])))
            for part in (
                by_owner((grad_input,)).reshape(z_size, edge, width),
                gates,
                totals,
            )
        ],
        axis=1,
    )
    pack, branch_home = barrier((pack.reshape(z_size * pack.shape[1], lanes), branch_home))
    pack, ff_got, down_home = barrier((pack, ff_got, down_home))
    pack = home_rows(pack)
    grad_gate_home, grad_up_home = own_columns(ff_got[..., :ffw]), own_columns(ff_got[..., ffw:])
    grad_gain_two = gain_home(norm_gain2, ((grad_gate_home, w_gate), (grad_up_home, w_up)))
    grad_branch_home = own_columns(exchange(branch_home.reshape(seq_size, chunk, width)))
    grad_input_home = own_columns(exchange(pack[:edge, :width].reshape(seq_size, chunk, width)))
    grad_gain_one = gain_home(
        norm_gain1, ((grad_branch_home, w_branch), (grad_input_home, w_input))
    )
    gates = as_wide(pack[edge : edge + owned])
    totals = as_wide(pack[edge + owned :, :owned])
    return (
        mixed,
        tokens_grad,
        grad_gain_one,
        grad_branch_home,
        grad_input_home,
        totals[:TAPS],
        totals[4],
        gates[:, :gate_width],
        totals[5],
        gates[:, gate_width : 2 * gate_width],
        totals[6],
        totals[7],
        as_wide(out_home),
        grad_gain_two,
        grad_gate_home,
        grad_up_home,
        as_wide(down_home),
    )


def solution(mesh):
    row = P(("seq", "fsdp"))
    rows = P(("seq", "fsdp"), None)
    columns = P(None, ("seq", "fsdp"))
    return jax.shard_map(
        shards,
        mesh=mesh,
        in_specs=(
            rows,
            rows,
            P(),
            P(),
            P(),
            row,
            rows,
            rows,
            columns,
            row,
            rows,
            row,
            rows,
            row,
            row,
            rows,
            row,
            rows,
            rows,
            rows,
        ),
        out_specs=(
            rows,
            rows,
            row,
            rows,
            rows,
            columns,
            row,
            rows,
            row,
            rows,
            row,
            row,
            rows,
            row,
            rows,
            rows,
            rows,
        ),
        check_vma=False,
    )
```
